256 devices in a mesh: col: 32 (over z, y), sec: 8 (over x, core).
Axes of the slice: x: 4, y: 4, z: 8, core: 2. Of those that a mesh axis runs over, the one named last changes fastest.
Arguments:
- transfer: float32 [64, 8, 256, 256], P('col', 'sec'), as said below
- hamiltonian: float32 [64, 3, 8, 256, 256], P('col', None, 'sec'), may hold values from -0.375 to 0.375
- kept: int32 [64, 8], P('col', 'sec'), may hold values from 128 to 256, as said below
Outputs:
- left_env: float32 [64, 8, 256, 256], P('col', 'sec')
- energy: float32 [64, 3], P('col')
The draws below stay inside these ranges and needn't reach their ends.
Inputs may be any that keep to these rules, and one draw needn't show every extreme that they name: Every kept dimension lies between half a sector and a whole sector, and some sector keeps all 256 states. `transfer`: each block is the identity plus an independent normal matrix of entries with deviation 0.2 / sqrt(256).
All inputs are finite; a program needn't handle non-finite values.
Results may differ from the reference program's by a relative error of at most 0.0003.
Values sent between devices are 32-bit elements; how exact they have to be, the bound alone decides.
A program may use at most 64 MiB of HBM per device.

```python
import jax
import jax.numpy as jnp
from jax import lax

B = 256
TERMS = 3
NCOL = 64
NSEC = 8


def draw_transfer(key, part):
    noise = jax.random.normal(jax.random.fold_in(key, 11), (NCOL, NSEC, B, B), jnp.float32)
    eye = jnp.eye(B, dtype=jnp.float32)
    return eye[None, None, :, :] + noise * (0.2 / B ** 0.5)


def draw_kept(key, part):
    values = jax.random.randint(jax.random.fold_in(key, 21), (NCOL * NSEC,), B // 2, B + 1)
    spot = jax.random.randint(jax.random.fold_in(key, 22), (), 0, NCOL * NSEC)
    values = values.at[spot].set(B)
    return values.reshape(NCOL, NSEC).astype(jnp.int32)


def shard_levels(rng, dims, shards, least, top_value):
    gain = 1.0
    for dim, blocks in shards:
        heights = jax.random.uniform(jax.random.fold_in(jax.random.fold_in(rng, 6), dim), (blocks,), jnp.float32, least / len(shards), top_value / len(shards))
        gain = gain * jnp.repeat(jnp.exp(heights), dims[dim] // blocks).reshape((-1,) + (1,) * (len(dims) - 1 - dim))
    return gain


def normal_values(own_key, extent, deviation, most, cuts=(), kind=jnp.bfloat16):
    drawn = deviation * jax.random.normal(own_key, extent, jnp.float32)
    if cuts:
        drawn = drawn * shard_levels(own_key, extent, cuts, -0.22, 0.18)
    return jnp.clip(drawn, -most, most).astype(kind)


def setup_inputs(seed: int = 0) -> dict:
    key_list = jax.random.split(jax.random.key(seed), 4)
    return {
        "transfer": draw_transfer(jax.random.fold_in(key_list[3], 71), 0),
        "hamiltonian": normal_values(key_list[1], (NCOL, TERMS, NSEC, B, B), (1.0 / B ** 0.5), 0.375, ((0, 32), (2, 8)), jnp.float32),
        "kept": draw_kept(jax.random.fold_in(key_list[3], 71), 0),
    }


def one_sector(input_tensors):
    mats, kept_s, ham = input_tensors
    eye = jnp.eye(B, dtype=jnp.float32)

    def forward(acc, mat):
        return jnp.dot(acc, mat, precision=lax.Precision.HIGHEST), acc

    def backward(acc, mat):
        return jnp.dot(mat, acc, precision=lax.Precision.HIGHEST), acc

    whole, lefts = lax.scan(forward, eye, mats)
    unused, right_environments = lax.scan(backward, eye, mats, reverse=True)
    column_tensors = jnp.arange(B, dtype=jnp.int32)
    mask = (column_tensors[None, :] < kept_s[:, None]).astype(jnp.float32)
    masked = lefts * mask[:, None, :]
    inner_contraction = jnp.einsum("cji,jk->cik", masked, whole, precision=lax.Precision.HIGHEST)
    inner_contraction = jnp.einsum("fas,fms->fam", inner_contraction, right_environments, precision=lax.Precision.HIGHEST)
    partial_value = jnp.einsum("cil,ctil->ct", inner_contraction, ham, precision=lax.Precision.HIGHEST)
    norm = jnp.sum(whole * whole)
    return masked, partial_value, norm


def reference(transfer, hamiltonian, kept):
    mats = jnp.moveaxis(transfer, 1, 0)
    kept_t = jnp.moveaxis(kept, 1, 0)
    ham = jnp.moveaxis(hamiltonian, 2, 0)
    masked, partial_value, norm = lax.map(one_sector, (mats, kept_t, ham))
    left_env = jnp.moveaxis(masked, 0, 1)
    energy = (NSEC * B) * jnp.sum(partial_value, axis=0) / jnp.sum(norm)
    return left_env, energy
```

```python
import jax
import jax.numpy as jnp
from jax import lax
from jax.experimental import pallas as pl
from jax.experimental.pallas import tpu as pltpu
from jax.sharding import PartitionSpec as P

MESH = pl.DeviceIdType.MESH
F32 = jnp.float32
BF16 = jnp.bfloat16
Y = 4
Z = 8
S = 8
N = 256
HALF = N // 2
QUARTER = N // 4
TERMS = 3
NN = (((1,), (0,)), ((), ()))
NT = (((1,), (1,)), ((), ()))
TN = (((0,), (0,)), ((), ()))


def split(x):
    high = x.astype(BF16)
    return high, (x - high.astype(F32)).astype(BF16)


def mm(a, b, dims=NN):
    ah, al = split(a)
    bh, bl = split(b)

    def dot(p, q):
        return lax.dot_general(p, q, dims, preferred_element_type=F32)

    return dot(ah, bh) + (dot(ah, bl) + dot(al, bh))


def kernel(
    t_hbm, h_hbm, kept_ref,
    left_hbm, energy_ref,
    t, h, g, r, acc_p, acc_m, post, lout, red,
    load_sem, store_sem, g_send, g_recv, z_send, z_recv, y_send, y_recv, s_send, s_recv,
):
    col = lax.axis_index("col")
    sec = lax.axis_index("sec")
    y = lax.rem(col, Y)
    z = col // Y

    def at_y(d):
        return z * Y + lax.rem(y + d + Y, Y)

    def at_z(d):
        return lax.rem(z + d + Z, Z) * Y + y

    loads = []
    for c in range(2):
        loads.append(pltpu.make_async_copy(t_hbm.at[c, 0], t.at[c], load_sem.at[c]))
    loads.append(pltpu.make_async_copy(h_hbm.at[:, :, 0], h, load_sem.at[2]))
    for copy in loads:
        copy.start()

    barrier = pltpu.get_barrier_semaphore()
    partners = [(at_y(1), sec), (at_y(-1), sec), (at_z(1), sec), (at_z(-1), sec)]
    partners += [(col, lax.rem(sec + d, S)) for d in range(1, S)]
    for partner in partners:
        pl.semaphore_signal(barrier, inc=1, device_id=partner, device_id_type=MESH)

    sends = []

    def send(ref, target, send_sem, recv_sem):
        copy = pltpu.make_async_remote_copy(
            src_ref=ref, dst_ref=ref, send_sem=send_sem, recv_sem=recv_sem,
            device_id=target, device_id_type=MESH,
        )
        copy.start()
        sends.append(copy)

    def arrived(ref, send_sem, recv_sem):
        pltpu.make_async_remote_copy(
            src_ref=ref, dst_ref=ref, send_sem=send_sem, recv_sem=recv_sem,
            device_id=(col, sec), device_id_type=MESH,
        ).wait_recv()

    top = pl.ds(0, HALF)
    bottom = pl.ds(HALF, HALF)
    loads[0].wait()
    loads[1].wait()
    g[y] = mm(t[0], t[1])
    pl.semaphore_wait(barrier, len(partners))

    y_plus, y_minus = (at_y(1), sec), (at_y(-1), sec)
    z_plus, z_minus = (at_z(1), sec), (at_z(-1), sec)
    before, after, opposite = lax.rem(y + 3, Y), lax.rem(y + 1, Y), lax.rem(y + 2, Y)

    def g_copy(direction, index, block, rows):
        target = y_plus if direction == 0 else y_minus
        send(g.at[block, rows], target, g_send.at[direction, index], g_recv.at[direction, index])

    def g_wait(direction, index, block, rows):
        arrived(g.at[block, rows], g_send.at[direction, index], g_recv.at[direction, index])

    g_copy(0, 0, y, top)
    g_copy(1, 0, y, bottom)
    g_copy(0, 1, y, bottom)
    g_copy(1, 1, y, top)
    g_wait(0, 0, before, top)
    g_copy(0, 2, before, top)
    g_wait(1, 0, after, bottom)
    g_copy(1, 2, after, bottom)
    g_wait(0, 1, before, bottom)
    g_wait(1, 1, after, top)
    g_wait(0, 2, opposite, top)
    g_wait(1, 2, opposite, bottom)

    low = mm(g[0], g[1])
    high = mm(g[2], g[3])
    r[z] = mm(low, high)

    def quarter(q):
        return pl.ds(pl.multiple_of(lax.rem(y + q, Y) * QUARTER, QUARTER), QUARTER)

    def z_block(direction, step):
        return lax.rem(z - step + Z, Z) if direction == 0 else lax.rem(z + step, Z)

    def z_copy(direction, step, part):
        ref = r.at[z_block(direction, step - 1), quarter(2 * direction + part)]
        target = z_plus if direction == 0 else z_minus
        send(ref, target, z_send.at[direction, step - 1, part], z_recv.at[direction, step - 1, part])

    def z_wait(direction, step, part):
        ref = r.at[z_block(direction, step), quarter(2 * direction + part)]
        arrived(ref, z_send.at[direction, step - 1, part], z_recv.at[direction, step - 1, part])

    def y_copy(direction, step, part):
        ref = r.at[z_block(direction, step), quarter(2 * direction + part)]
        target = y_plus if part == 0 else y_minus
        send(ref, target, y_send.at[direction, step - 1, part], y_recv.at[direction, step - 1, part])

    def y_wait(direction, step, part):
        ref = r.at[z_block(direction, step), quarter(2 * direction + (3 if part == 0 else 2))]
        arrived(ref, y_send.at[direction, step - 1, part], y_recv.at[direction, step - 1, part])

    for part in range(2):
        for direction in range(2):
            z_copy(direction, 1, part)

    acc_p[...] = low
    acc_m[...] = high

    @pl.when(y == 0)
    def _():
        acc_m[...] = mm(g[1], acc_m[...])

    @pl.when(y == 1)
    def _():
        acc_p[...] = g[0]

    @pl.when(y == 2)
    def _():
        acc_m[...] = g[3]

    @pl.when(y == 3)
    def _():
        acc_p[...] = mm(acc_p[...], g[2])

    row = lax.broadcasted_iota(jnp.int32, (N, N), 0)
    column = lax.broadcasted_iota(jnp.int32, (N, N), 1)

    @pl.when(y == 0)
    def _():
        acc_p[...] = (row == column).astype(F32)

    @pl.when(y == 3)
    def _():
        acc_m[...] = (row == column).astype(F32)

    def take_blocks(step):
        for direction in range(2):
            for part in range(2):
                y_wait(direction, step, part)
        plus = z_block(0, step)
        minus = z_block(1, step)

        @pl.when(step <= z)
        def _():
            acc_p[...] = mm(r[plus], acc_p[...])

        @pl.when(step == z + 1)
        def _():
            post[...] = r[plus]

        @pl.when(step > z + 1)
        def _():
            post[...] = mm(r[plus], post[...])

        @pl.when(step <= Z - 1 - z)
        def _():
            acc_m[...] = mm(acc_m[...], r[minus])

        @pl.when(step == Z - z)
        def _():
            post[...] = r[minus]

        @pl.when(step > Z - z)
        def _():
            post[...] = mm(post[...], r[minus])

    for step in range(1, 5):
        for part in range(2):
            for direction in range(2):
                z_wait(direction, step, part)
                if step < 4:
                    z_copy(direction, step + 1, part)
                    y_copy(direction, step, part)
        if step > 1:
            take_blocks(step - 1)

    middle = lax.rem(z + 4, Z)

    @pl.when(z < 4)
    def _():
        acc_m[...] = mm(acc_m[...], r[middle])

    @pl.when(z < 3)
    def _():
        acc_m[...] = mm(acc_m[...], post[...])

    @pl.when(z >= 4)
    def _():
        acc_p[...] = mm(r[middle], acc_p[...])

    @pl.when(z > 4)
    def _():
        acc_p[...] = mm(post[...], acc_p[...])

    left0 = acc_p[...]
    right1 = acc_m[...]
    left1 = mm(left0, t[0])
    right0 = mm(t[1], right1)
    lout[0] = jnp.where(column < kept_ref[0, 0], left0, 0.0)
    lout[1] = jnp.where(column < kept_ref[0, 1], left1, 0.0)
    stores = []
    for c in range(2):
        copy = pltpu.make_async_copy(lout.at[c], left_hbm.at[c, 0], store_sem.at[c])
        copy.start()
        stores.append(copy)
    whole = mm(left1, right0)
    loads[2].wait()

    def fold(x):
        return jnp.sum(x, axis=0, keepdims=True)

    def lanes(x):
        x = fold(x)
        return x[:, :128] + x[:, 128:]

    rows = []
    for c, (left, right) in enumerate(((left0, right0), (left1, right1))):
        inner = mm(mm(left, whole, TN), right, NT)
        inner = jnp.where(row < kept_ref[0, c], inner, 0.0)
        for k in range(TERMS):
            rows.append(lanes(inner * h[c, k]))
    rows.append(lanes(whole * whole))
    rows.append(jnp.zeros((1, 128), F32))
    red[sec] = jnp.concatenate(rows, axis=0)

    for d in range(1, S):
        send(red.at[sec], (col, lax.rem(sec + d, S)), s_send.at[d], s_recv.at[d])
    for d in range(1, S):
        arrived(red.at[lax.rem(sec - d + S, S)], s_send.at[d], s_recv.at[d])
    total = red[0]
    for k in range(1, S):
        total = total + red[k]
    total = jnp.sum(total, axis=1, keepdims=True)
    values = (float(N * S) * total[0:6]) / total[6:7]
    place = 3 * lax.broadcasted_iota(jnp.int32, (2, 3), 0) + lax.broadcasted_iota(jnp.int32, (2, 3), 1)
    energy = jnp.zeros((2, 3), F32)
    for k in range(6):
        energy = jnp.where(place == k, values[k:k + 1], energy)
    energy_ref[...] = energy

    for copy in sends:
        copy.wait_send()
    for copy in stores:
        copy.wait()


def per_device(transfer, hamiltonian, kept):
    dma = pltpu.SemaphoreType.DMA
    return pl.pallas_call(
        kernel,
        name="chain",
        out_shape=(
            jax.ShapeDtypeStruct((2, 1, N, N), F32),
            jax.ShapeDtypeStruct((2, TERMS), F32),
        ),
        in_specs=[
            pl.BlockSpec(memory_space=pl.ANY),
            pl.BlockSpec(memory_space=pl.ANY),
            pl.BlockSpec(memory_space=pltpu.SMEM),
        ],
        out_specs=(
            pl.BlockSpec(memory_space=pl.ANY),
            pl.BlockSpec(memory_space=pltpu.VMEM),
        ),
        scratch_shapes=[
            pltpu.VMEM((2, N, N), F32),
            pltpu.VMEM((2, TERMS, N, N), F32),
            pltpu.VMEM((Y, N, N), F32),
            pltpu.VMEM((Z, N, N), F32),
            pltpu.VMEM((N, N), F32),
            pltpu.VMEM((N, N), F32),
            pltpu.VMEM((N, N), F32),
            pltpu.VMEM((2, N, N), F32),
            pltpu.VMEM((S, 8, 128), F32),
            dma((3,)),
            dma((2,)),
            dma((2, 3)),
            dma((2, 3)),
            dma((2, 4, 2)),
            dma((2, 4, 2)),
            dma((2, 3, 2)),
            dma((2, 3, 2)),
            dma((S,)),
            dma((S,)),
        ],
        compiler_params=pltpu.CompilerParams(collective_id=0, has_side_effects=True),
    )(transfer, hamiltonian, kept.T)


def solution(mesh):
    in_specs = (P("col", "sec", None, None), P("col", None, "sec", None, None), P("col", "sec"))
    out_specs = (P("col", "sec", None, None), P("col", None))
    return jax.shard_map(
        per_device, mesh=mesh, in_specs=in_specs, out_specs=out_specs, check_vma=False
    )
```

```python
import jax
import jax.numpy as jnp
from jax import lax
from jax.experimental import pallas as pl
from jax.experimental.pallas import tpu as pltpu
from jax.sharding import PartitionSpec as P

MESH = pl.DeviceIdType.MESH
F32 = jnp.float32
BF16 = jnp.bfloat16
Y = 4
Z = 8
S = 8
N = 256
HALF = N // 2
QUARTER = N // 4
PARTS = 4
ROWS = HALF // PARTS
TERMS = 3
NN = (((1,), (0,)), ((), ()))
NT = (((1,), (1,)), ((), ()))
TN = (((0,), (0,)), ((), ()))


def split(x):
    high = x.astype(BF16)
    return high, (x - high.astype(F32)).astype(BF16)


def mm(a, b, dims=NN):
    ah, al = split(a)
    bh, bl = split(b)

    def dot(p, q):
        return lax.dot_general(p, q, dims, preferred_element_type=F32)

    return dot(ah, bh) + (dot(ah, bl) + dot(al, bh))


def kernel(
    t_hbm, h_hbm, kept_ref,
    lout, sums_ref,
    t, h, g, r, acc_p, acc_m, post, left1_ref, right0_ref, ahead, whole_ref, red,
    load_sem, g_send, g_recv, z_send, z_recv, y_send, y_recv, s_send, s_recv,
):
    col = lax.axis_index("col")
    sec = lax.axis_index("sec")
    y = lax.rem(col, Y)
    z = col // Y

    def at_y(d):
        return z * Y + lax.rem(y + d + Y, Y)

    def at_z(d):
        return lax.rem(z + d + Z, Z) * Y + y

    loads = []
    for c in range(2):
        loads.append(pltpu.make_async_copy(t_hbm.at[c, 0], t.at[c], load_sem.at[c]))
    loads.append(pltpu.make_async_copy(h_hbm.at[:, :, 0], h, load_sem.at[2]))
    for copy in loads:
        copy.start()

    barrier = pltpu.get_barrier_semaphore()
    partners = [(at_y(1), sec), (at_y(-1), sec), (at_z(1), sec), (at_z(-1), sec)]
    partners += [(col, lax.rem(sec + d, S)) for d in range(1, S)]
    for partner in partners:
        pl.semaphore_signal(barrier, inc=1, device_id=partner, device_id_type=MESH)

    sends = []

    def send(ref, target, send_sem, recv_sem):
        copy = pltpu.make_async_remote_copy(
            src_ref=ref, dst_ref=ref, send_sem=send_sem, recv_sem=recv_sem,
            device_id=target, device_id_type=MESH,
        )
        copy.start()
        sends.append(copy)

    def arrived(ref, send_sem, recv_sem):
        pltpu.make_async_remote_copy(
            src_ref=ref, dst_ref=ref, send_sem=send_sem, recv_sem=recv_sem,
            device_id=(col, sec), device_id_type=MESH,
        ).wait_recv()

    top = pl.ds(0, HALF)
    bottom = pl.ds(HALF, HALF)
    loads[0].wait()
    loads[1].wait()
    g[y, top] = mm(t[0, top], t[1])
    pl.semaphore_wait(barrier, len(partners))

    y_plus, y_minus = (at_y(1), sec), (at_y(-1), sec)
    z_plus, z_minus = (at_z(1), sec), (at_z(-1), sec)
    before, after, opposite = lax.rem(y + 3, Y), lax.rem(y + 1, Y), lax.rem(y + 2, Y)

    def g_copy(direction, index, block, rows):
        target = y_plus if direction == 0 else y_minus
        send(g.at[block, rows], target, g_send.at[direction, index], g_recv.at[direction, index])

    def g_wait(direction, index, block, rows):
        arrived(g.at[block, rows], g_send.at[direction, index], g_recv.at[direction, index])

    g_copy(0, 0, y, top)
    g[y, bottom] = mm(t[0, bottom], t[1])
    g_copy(1, 0, y, bottom)
    g_copy(0, 1, y, bottom)
    g_copy(1, 1, y, top)
    g_wait(0, 0, before, top)
    g_copy(0, 2, before, top)
    g_wait(1, 0, after, bottom)
    g_copy(1, 2, after, bottom)
    g_wait(0, 1, before, bottom)
    g_wait(1, 1, after, top)
    g_wait(0, 2, opposite, top)
    g_wait(1, 2, opposite, bottom)

    low = mm(g[0], g[1])
    high = mm(g[2], g[3])
    r[z] = mm(low, high)

    def chunk(direction, part, shift=0):
        start = lax.rem(y * QUARTER + direction * HALF + part * ROWS + shift, N)
        return pl.ds(pl.multiple_of(start, ROWS), ROWS)

    def z_block(direction, step):
        return lax.rem(z - step + Z, Z) if direction == 0 else lax.rem(z + step, Z)

    def z_copy(direction, step, part):
        ref = r.at[z_block(direction, step - 1), chunk(direction, part)]
        target = z_plus if direction == 0 else z_minus
        send(ref, target, z_send.at[direction, step - 1, part], z_recv.at[direction, step - 1, part])

    def z_wait(direction, step, part):
        ref = r.at[z_block(direction, step), chunk(direction, part)]
        arrived(ref, z_send.at[direction, step - 1, part], z_recv.at[direction, step - 1, part])

    def y_copy(direction, step, part):
        ref = r.at[z_block(direction, step), chunk(direction, part)]
        target = y_plus if part < PARTS // 2 else y_minus
        send(ref, target, y_send.at[direction, step - 1, part], y_recv.at[direction, step - 1, part])

    def y_wait(direction, step, part):
        shift = 3 * QUARTER if part < PARTS // 2 else QUARTER
        ref = r.at[z_block(direction, step), chunk(direction, part, shift)]
        arrived(ref, y_send.at[direction, step - 1, part], y_recv.at[direction, step - 1, part])

    for part in range(PARTS):
        for direction in range(2):
            z_copy(direction, 1, part)

    acc_p[...] = low
    acc_m[...] = high

    @pl.when(y == 0)
    def _():
        acc_m[...] = mm(g[1], acc_m[...])

    @pl.when(y == 1)
    def _():
        acc_p[...] = g[0]

    @pl.when(y == 2)
    def _():
        acc_m[...] = g[3]

    @pl.when(y == 3)
    def _():
        acc_p[...] = mm(acc_p[...], g[2])

    row = lax.broadcasted_iota(jnp.int32, (N, N), 0)
    column = lax.broadcasted_iota(jnp.int32, (N, N), 1)

    @pl.when(y == 0)
    def _():
        acc_p[...] = (row == column).astype(F32)

    @pl.when(y == 3)
    def _():
        acc_m[...] = (row == column).astype(F32)

    def lefts_from(left0):
        left1 = mm(left0, t[0])
        left1_ref[...] = left1
        lout[0] = jnp.where(column < kept_ref[0, 0], left0, 0.0)
        lout[1] = jnp.where(column < kept_ref[0, 1], left1, 0.0)

    def take_blocks(step):
        for direction in range(2):
            for part in range(PARTS):
                y_wait(direction, step, part)
        plus = z_block(0, step)
        minus = z_block(1, step)

        @pl.when(step <= z)
        def _():
            acc_p[...] = mm(r[plus], acc_p[...])

        @pl.when(step == z + 1)
        def _():
            post[...] = r[plus]

        @pl.when(step > z + 1)
        def _():
            post[...] = mm(r[plus], post[...])

        @pl.when(step <= Z - 1 - z)
        def _():
            acc_m[...] = mm(acc_m[...], r[minus])

        @pl.when(step == Z - z)
        def _():
            post[...] = r[minus]

        @pl.when(step > Z - z)
        def _():
            post[...] = mm(post[...], r[minus])

    for step in range(1, 4):
        for part in range(PARTS):
            for direction in range(2):
                z_wait(direction, step, part)
                z_copy(direction, step + 1, part)
                y_copy(direction, step, part)
        if step > 1:
            take_blocks(step - 1)
    take_blocks(3)

    @pl.when(z < 4)
    def _():
        lefts_from(acc_p[...])
        ahead[...] = mm(left1_ref[...], t[1])

    @pl.when(z >= 4)
    def _():
        right0_ref[...] = mm(t[1], acc_m[...])
        ahead[...] = mm(t[0], right0_ref[...])

    for part in range(PARTS):
        for direction in range(2):
            z_wait(direction, 4, part)
    middle = lax.rem(z + 4, Z)

    @pl.when(z < 4)
    def _():
        acc_m[...] = mm(acc_m[...], r[middle])

    @pl.when(z < 3)
    def _():
        acc_m[...] = mm(acc_m[...], post[...])

    @pl.when(z >= 4)
    def _():
        acc_p[...] = mm(r[middle], acc_p[...])

    @pl.when(z > 4)
    def _():
        acc_p[...] = mm(post[...], acc_p[...])

    @pl.when(z < 4)
    def _():
        whole_ref[...] = mm(ahead[...], acc_m[...])
        right0_ref[...] = mm(t[1], acc_m[...])

    @pl.when(z >= 4)
    def _():
        whole_ref[...] = mm(acc_p[...], ahead[...])
        lefts_from(acc_p[...])

    left0, left1, right0, right1 = acc_p[...], left1_ref[...], right0_ref[...], acc_m[...]
    whole = whole_ref[...]
    loads[2].wait()

    def fold(x):
        return jnp.sum(x, axis=0, keepdims=True)

    def lanes(x):
        x = fold(x)
        return x[:, :128] + x[:, 128:]

    rows = []
    for c, (left, right) in enumerate(((left0, right0), (left1, right1))):
        inner = mm(mm(left, whole, TN), right, NT)
        inner = jnp.where(row < kept_ref[0, c], inner, 0.0)
        for k in range(TERMS):
            rows.append(lanes(inner * h[c, k]))
    rows.append(lanes(whole * whole))
    rows.append(jnp.zeros((1, 128), F32))
    red[sec] = jnp.concatenate(rows, axis=0)

    for d in (4, 3, 5, 2, 6, 1, 7):
        send(red.at[sec], (col, lax.rem(sec + d, S)), s_send.at[d], s_recv.at[d])
    for d in range(1, S):
        arrived(red.at[lax.rem(sec - d + S, S)], s_send.at[d], s_recv.at[d])
    total = red[0]
    for k in range(1, S):
        total = total + red[k]
    sums_ref[...] = total

    for copy in sends:
        copy.wait_send()


def finish(lefts, sums_ref, left_hbm, energy_ref, sems):
    stores = []
    for c in range(2):
        copy = pltpu.make_async_copy(lefts.at[c], left_hbm.at[c, 0], sems.at[c])
        copy.start()
        stores.append(copy)
    total = sums_ref[...]
    total = jnp.sum(total, axis=1, keepdims=True)
    values = (float(N * S) * total[0:6]) / total[6:7]
    place = 3 * lax.broadcasted_iota(jnp.int32, (2, 3), 0) + lax.broadcasted_iota(jnp.int32, (2, 3), 1)
    energy = jnp.zeros((2, 3), F32)
    for k in range(6):
        energy = jnp.where(place == k, values[k:k + 1], energy)
    energy_ref[...] = energy
    for copy in stores:
        copy.wait()


def per_device(transfer, hamiltonian, kept):
    dma = pltpu.SemaphoreType.DMA
    vmem = pl.BlockSpec(memory_space=pltpu.VMEM)
    lefts, sums = pl.pallas_call(
        kernel,
        name="chain",
        out_shape=(pltpu.VMEM((2, N, N), F32), pltpu.VMEM((8, 128), F32)),
        in_specs=[
            pl.BlockSpec(memory_space=pl.ANY),
            pl.BlockSpec(memory_space=pl.ANY),
            pl.BlockSpec(memory_space=pltpu.SMEM),
        ],
        out_specs=(vmem, vmem),
        scratch_shapes=[
            pltpu.VMEM((2, N, N), F32),
            pltpu.VMEM((2, TERMS, N, N), F32),
            pltpu.VMEM((Y, N, N), F32),
            pltpu.VMEM((Z, N, N), F32),
            *[pltpu.VMEM((N, N), F32)] * 7,
            pltpu.VMEM((S, 8, 128), F32),
            dma((3,)),
            dma((2, 3)),
            dma((2, 3)),
            dma((2, 4, PARTS)),
            dma((2, 4, PARTS)),
            dma((2, 3, PARTS)),
            dma((2, 3, PARTS)),
            dma((S,)),
            dma((S,)),
        ],
        compiler_params=pltpu.CompilerParams(collective_id=0, has_side_effects=True),
    )(transfer, hamiltonian, kept.T)
    return pl.pallas_call(
        finish,
        name="finish",
        out_shape=(
            jax.ShapeDtypeStruct((2, 1, N, N), F32),
            jax.ShapeDtypeStruct((2, TERMS), F32),
        ),
        in_specs=[vmem, vmem],
        out_specs=(pl.BlockSpec(memory_space=pl.ANY), vmem),
        scratch_shapes=[dma((2,))],
    )(*(pltpu.with_memory_space_constraint(x, pltpu.VMEM) for x in (lefts, sums)))


def solution(mesh):
    in_specs = (P("col", "sec", None, None), P("col", None, "sec", None, None), P("col", "sec"))
    out_specs = (P("col", "sec", None, None), P("col", None))
    return jax.shard_map(
        per_device, mesh=mesh, in_specs=in_specs, out_specs=out_specs, check_vma=False
    )
```

```python
import jax
import jax.numpy as jnp
from jax import lax
from jax.experimental import pallas as pl
from jax.experimental.pallas import tpu as pltpu
from jax.sharding import PartitionSpec as P

MESH = pl.DeviceIdType.MESH
F32 = jnp.float32
BF16 = jnp.bfloat16
Y = 4
Z = 8
S = 8
N = 256
HALF = N // 2
QUARTER = N // 4
PARTS = 4
ROWS = HALF // PARTS
TERMS = 3
NN = (((1,), (0,)), ((), ()))
NT = (((1,), (1,)), ((), ()))
TN = (((0,), (0,)), ((), ()))


def split(x):
    high = x.astype(BF16)
    return high, (x - high.astype(F32)).astype(BF16)


def mm(a, b, dims=NN):
    ah, al = split(a)
    bh, bl = split(b)

    def dot(p, q):
        return lax.dot_general(p, q, dims, preferred_element_type=F32)

    return dot(ah, bh) + (dot(ah, bl) + dot(al, bh))


def kernel(
    t_hbm, h_hbm, kept_ref,
    lout, sums_ref,
    t, h, g, r, acc_p, acc_m, post, left1_ref, inner, red,
    load_sem, g_send, g_recv, z_send, z_recv, y_send, y_recv, s_send, s_recv,
):
    col = lax.axis_index("col")
    sec = lax.axis_index("sec")
    y = lax.rem(col, Y)
    z = col // Y

    def at_y(d):
        return z * Y + lax.rem(y + d + Y, Y)

    def at_z(d):
        return lax.rem(z + d + Z, Z) * Y + y

    loads = []
    for c in range(2):
        loads.append(pltpu.make_async_copy(t_hbm.at[c, 0], t.at[c], load_sem.at[c]))
    loads.append(pltpu.make_async_copy(h_hbm.at[:, :, 0], h, load_sem.at[2]))
    loads[0].start()
    loads[1].start()

    barrier = pltpu.get_barrier_semaphore()
    partners = [(at_y(1), sec), (at_y(-1), sec), (at_z(1), sec), (at_z(-1), sec)]
    partners += [(col, lax.rem(sec + d, S)) for d in range(1, S)]
    for partner in partners:
        pl.semaphore_signal(barrier, inc=1, device_id=partner, device_id_type=MESH)

    sends = []

    def send(ref, target, send_sem, recv_sem):
        copy = pltpu.make_async_remote_copy(
            src_ref=ref, dst_ref=ref, send_sem=send_sem, recv_sem=recv_sem,
            device_id=target, device_id_type=MESH,
        )
        copy.start()
        sends.append(copy)

    def arrived(ref, send_sem, recv_sem):
        pltpu.make_async_remote_copy(
            src_ref=ref, dst_ref=ref, send_sem=send_sem, recv_sem=recv_sem,
            device_id=(col, sec), device_id_type=MESH,
        ).wait_recv()

    top = pl.ds(0, HALF)
    bottom = pl.ds(HALF, HALF)
    loads[0].wait()
    loads[1].wait()
    loads[2].start()
    g[y, top] = mm(t[0, top], t[1])
    pl.semaphore_wait(barrier, len(partners))

    y_plus, y_minus = (at_y(1), sec), (at_y(-1), sec)
    z_plus, z_minus = (at_z(1), sec), (at_z(-1), sec)
    before, after, opposite = lax.rem(y + 3, Y), lax.rem(y + 1, Y), lax.rem(y + 2, Y)

    def g_rows(direction, index):
        part = (index + 2 * direction) % 4
        return pl.ds(part * QUARTER, QUARTER)

    def g_copy(direction, index, block):
        target = y_plus if direction == 0 else y_minus
        rows = g_rows(direction, index % 4)
        send(g.at[block, rows], target, g_send.at[direction, index], g_recv.at[direction, index])

    def g_wait(direction, index, block):
        rows = g_rows(direction, index % 4)
        arrived(g.at[block, rows], g_send.at[direction, index], g_recv.at[direction, index])

    g_copy(0, 0, y)
    g_copy(0, 1, y)
    g[y, bottom] = mm(t[0, bottom], t[1])
    for direction, index in ((1, 0), (1, 1), (0, 2), (1, 2), (0, 3), (1, 3)):
        g_copy(direction, index, y)

    loads[2].wait()
    row = lax.broadcasted_iota(jnp.int32, (N, N), 0)
    column = lax.broadcasted_iota(jnp.int32, (N, N), 1)
    for c in range(2):
        kept = row < kept_ref[0, c]
        for k in range(TERMS):
            h[c, k] = jnp.where(kept, h[c, k], 0.0)
    for k in range(TERMS):

        @pl.when(z < 4)
        def _():
            h[0, k] = mm(h[0, k], t[1])

        @pl.when(z >= 4)
        def _():
            h[1, k] = mm(t[0], h[1, k])

    neighbours = (before, after)
    for index in range(2):
        for direction in range(2):
            g_wait(direction, index, neighbours[direction])
            g_copy(direction, index + 4, neighbours[direction])
    for index in range(2, 4):
        for direction in range(2):
            g_wait(direction, index, neighbours[direction])
    for index in range(4, 6):
        for direction in range(2):
            g_wait(direction, index, opposite)

    low = mm(g[0], g[1])
    high = mm(g[2], g[3])
    r[z] = mm(low, high)

    def chunk(direction, part, shift=0):
        start = lax.rem(y * QUARTER + direction * HALF + part * ROWS + shift, N)
        return pl.ds(pl.multiple_of(start, ROWS), ROWS)

    def z_block(direction, step):
        return lax.rem(z - step + Z, Z) if direction == 0 else lax.rem(z + step, Z)

    def z_copy(direction, step, part):
        ref = r.at[z_block(direction, step - 1), chunk(direction, part)]
        target = z_plus if direction == 0 else z_minus
        send(ref, target, z_send.at[direction, step - 1, part], z_recv.at[direction, step - 1, part])

    def z_wait(direction, step, part):
        ref = r.at[z_block(direction, step), chunk(direction, part)]
        arrived(ref, z_send.at[direction, step - 1, part], z_recv.at[direction, step - 1, part])

    def y_copy(direction, step, part):
        ref = r.at[z_block(direction, step), chunk(direction, part)]
        target = y_plus if part < PARTS // 2 else y_minus
        send(ref, target, y_send.at[direction, step - 1, part], y_recv.at[direction, step - 1, part])

    def y_wait(direction, step, part):
        shift = 3 * QUARTER if part < PARTS // 2 else QUARTER
        ref = r.at[z_block(direction, step), chunk(direction, part, shift)]
        arrived(ref, y_send.at[direction, step - 1, part], y_recv.at[direction, step - 1, part])

    for part in range(PARTS):
        for direction in range(2):
            z_copy(direction, 1, part)

    acc_p[...] = low
    acc_m[...] = high

    @pl.when(y == 0)
    def _():
        acc_m[...] = mm(g[1], acc_m[...])

    @pl.when(y == 1)
    def _():
        acc_p[...] = g[0]

    @pl.when(y == 2)
    def _():
        acc_m[...] = g[3]

    @pl.when(y == 3)
    def _():
        acc_p[...] = mm(acc_p[...], g[2])

    @pl.when(y == 0)
    def _():
        acc_p[...] = (row == column).astype(F32)

    @pl.when(y == 3)
    def _():
        acc_m[...] = (row == column).astype(F32)

    def lefts_from(left0):
        left1 = mm(left0, t[0])
        left1_ref[...] = left1
        lout[0] = jnp.where(column < kept_ref[0, 0], left0, 0.0)
        lout[1] = jnp.where(column < kept_ref[0, 1], left1, 0.0)

    def take_blocks(step):
        for direction in range(2):
            for part in range(PARTS):
                y_wait(direction, step, part)
        plus = z_block(0, step)
        minus = z_block(1, step)

        @pl.when(step <= z)
        def _():
            acc_p[...] = mm(r[plus], acc_p[...])

        @pl.when(step == z + 1)
        def _():
            post[...] = r[plus]

        @pl.when(step > z + 1)
        def _():
            post[...] = mm(r[plus], post[...])

        @pl.when(step <= Z - 1 - z)
        def _():
            acc_m[...] = mm(acc_m[...], r[minus])

        @pl.when(step == Z - z)
        def _():
            post[...] = r[minus]

        @pl.when(step > Z - z)
        def _():
            post[...] = mm(post[...], r[minus])

    for step in range(1, 4):
        for part in range(PARTS):
            for direction in range(2):
                z_wait(direction, step, part)
                z_copy(direction, step + 1, part)
                y_copy(direction, step, part)
        if step > 1:
            take_blocks(step - 1)
    take_blocks(3)

    @pl.when(z < 4)
    def _():
        lefts_from(acc_p[...])
        whole = mm(left1_ref[...], t[1])
        inner[0] = mm(acc_p[...], whole, TN)
        inner[1] = mm(left1_ref[...], whole, TN)
        inner[2] = mm(whole, whole, TN)

    @pl.when(z >= 4)
    def _():
        right1 = acc_m[...]
        right0 = mm(t[1], right1)
        whole = mm(t[0], right0)
        inner[0] = mm(whole, right0, NT)
        inner[1] = mm(whole, right1, NT)
        inner[2] = mm(whole, whole, NT)

    for part in range(PARTS):
        for direction in range(2):
            z_wait(direction, 4, part)
    middle = lax.rem(z + 4, Z)

    @pl.when(z < 4)
    def _():
        acc_m[...] = mm(acc_m[...], r[middle])

    @pl.when(z < 3)
    def _():
        acc_m[...] = mm(acc_m[...], post[...])

    @pl.when(z >= 4)
    def _():
        acc_p[...] = mm(r[middle], acc_p[...])

    @pl.when(z > 4)
    def _():
        acc_p[...] = mm(post[...], acc_p[...])

    def lanes(x):
        x = jnp.sum(x, axis=0, keepdims=True)
        return x[:, :128] + x[:, 128:]

    def reduce(inner0, inner1, gram):
        rows = [lanes(inner0 * h[0, k]) for k in range(TERMS)]
        rows += [lanes(inner1 * h[1, k]) for k in range(TERMS)]
        rows += [lanes(inner[2] * gram), jnp.zeros((1, 128), F32)]
        red[sec] = jnp.concatenate(rows, axis=0)

    @pl.when(z < 4)
    def _():
        gram = mm(acc_m[...], acc_m[...], NT)
        reduce(mm(inner[0], gram), mm(inner[1], gram), gram)

    @pl.when(z >= 4)
    def _():
        gram = mm(acc_p[...], acc_p[...], TN)
        reduce(mm(gram, inner[0]), mm(gram, inner[1]), gram)

    for d in (4, 3, 5, 2, 6, 1, 7):
        send(red.at[sec], (col, lax.rem(sec + d, S)), s_send.at[d], s_recv.at[d])

    @pl.when(z >= 4)
    def _():
        lefts_from(acc_p[...])

    for d in range(1, S):
        arrived(red.at[lax.rem(sec - d + S, S)], s_send.at[d], s_recv.at[d])
    total = red[0]
    for k in range(1, S):
        total = total + red[k]
    sums_ref[...] = total

    for copy in sends:
        copy.wait_send()


def finish(lefts, sums_ref, left_hbm, energy_ref, sems):
    stores = []
    for c in range(2):
        for k in range(4):
            rows = pl.ds(k * QUARTER, QUARTER)
            copy = pltpu.make_async_copy(lefts.at[c, rows], left_hbm.at[c, 0, rows], sems.at[c, k])
            copy.start()
            stores.append(copy)
    total = sums_ref[...]
    total = jnp.sum(total, axis=1, keepdims=True)
    values = (float(N * S) * total[0:6]) / total[6:7]
    place = 3 * lax.broadcasted_iota(jnp.int32, (2, 3), 0) + lax.broadcasted_iota(jnp.int32, (2, 3), 1)
    energy = jnp.zeros((2, 3), F32)
    for k in range(6):
        energy = jnp.where(place == k, values[k:k + 1], energy)
    energy_ref[...] = energy
    for copy in stores:
        copy.wait()


def per_device(transfer, hamiltonian, kept):
    dma = pltpu.SemaphoreType.DMA
    vmem = pl.BlockSpec(memory_space=pltpu.VMEM)
    lefts, sums = pl.pallas_call(
        kernel,
        name="chain",
        out_shape=(pltpu.VMEM((2, N, N), F32), pltpu.VMEM((8, 128), F32)),
        in_specs=[
            pl.BlockSpec(memory_space=pl.ANY),
            pl.BlockSpec(memory_space=pl.ANY),
            pl.BlockSpec(memory_space=pltpu.SMEM),
        ],
        out_specs=(vmem, vmem),
        scratch_shapes=[
            pltpu.VMEM((2, N, N), F32),
            pltpu.VMEM((2, TERMS, N, N), F32),
            pltpu.VMEM((Y, N, N), F32),
            pltpu.VMEM((Z, N, N), F32),
            *[pltpu.VMEM((N, N), F32)] * 4,
            pltpu.VMEM((3, N, N), F32),
            pltpu.VMEM((S, 8, 128), F32),
            dma((3,)),
            dma((2, 6)),
            dma((2, 6)),
            dma((2, 4, PARTS)),
            dma((2, 4, PARTS)),
            dma((2, 3, PARTS)),
            dma((2, 3, PARTS)),
            dma((S,)),
            dma((S,)),
        ],
        compiler_params=pltpu.CompilerParams(collective_id=0, has_side_effects=True),
    )(transfer, hamiltonian, kept.T)
    return pl.pallas_call(
        finish,
        name="finish",
        out_shape=(
            jax.ShapeDtypeStruct((2, 1, N, N), F32),
            jax.ShapeDtypeStruct((2, TERMS), F32),
        ),
        in_specs=[vmem, vmem],
        out_specs=(pl.BlockSpec(memory_space=pl.ANY), vmem),
        scratch_shapes=[dma((2, 4))],
    )(*(pltpu.with_memory_space_constraint(x, pltpu.VMEM) for x in (lefts, sums)))


def solution(mesh):
    in_specs = (P("col", "sec", None, None), P("col", None, "sec", None, None), P("col", "sec"))
    out_specs = (P("col", "sec", None, None), P("col", None))
    return jax.shard_map(
        per_device, mesh=mesh, in_specs=in_specs, out_specs=out_specs, check_vma=False
    )
```

```python
import jax
import jax.numpy as jnp
from jax import lax
from jax.experimental import pallas as pl
from jax.experimental.pallas import tpu as pltpu
from jax.sharding import PartitionSpec as P

MESH = pl.DeviceIdType.MESH
F32 = jnp.float32
BF16 = jnp.bfloat16
Y = 4
Z = 8
S = 8
N = 256
HALF = N // 2
QUARTER = N // 4
PARTS = 4
ROWS = HALF // PARTS
TERMS = 3
NN = (((1,), (0,)), ((), ()))
NT = (((1,), (1,)), ((), ()))
TN = (((0,), (0,)), ((), ()))


def split(x):
    high = x.astype(BF16)
    return high, (x - high.astype(F32)).astype(BF16)


def mm(a, b, dims=NN):
    ah, al = split(a)
    bh, bl = split(b)

    def dot(p, q):
        return lax.dot_general(p, q, dims, preferred_element_type=F32)

    return dot(ah, bh) + (dot(ah, bl) + dot(al, bh))


def kernel(
    t_hbm, h_hbm, kept_ref,
    lout, sums_ref,
    t, h, g, r, acc_p, acc_m, post, left1_ref, inner, red,
    load_sem, g_send, g_recv, z_send, z_recv, y_send, y_recv, s_send, s_recv,
):
    col = lax.axis_index("col")
    sec = lax.axis_index("sec")
    y = lax.rem(col, Y)
    z = col // Y

    def at_y(d):
        return z * Y + lax.rem(y + d + Y, Y)

    def at_z(d):
        return lax.rem(z + d + Z, Z) * Y + y

    loads = []
    for c in range(2):
        loads.append(pltpu.make_async_copy(t_hbm.at[c, 0], t.at[c], load_sem.at[c]))
    loads.append(pltpu.make_async_copy(h_hbm.at[:, :, 0], h, load_sem.at[2]))
    loads[0].start()
    loads[1].start()

    barrier = pltpu.get_barrier_semaphore()
    partners = [(at_y(1), sec), (at_y(-1), sec), (at_z(1), sec), (at_z(-1), sec)]
    partners += [(col, lax.rem(sec + d, S)) for d in range(1, S)]
    for partner in partners:
        pl.semaphore_signal(barrier, inc=1, device_id=partner, device_id_type=MESH)

    sends = []

    def send(ref, target, send_sem, recv_sem):
        copy = pltpu.make_async_remote_copy(
            src_ref=ref, dst_ref=ref, send_sem=send_sem, recv_sem=recv_sem,
            device_id=target, device_id_type=MESH,
        )
        copy.start()
        sends.append(copy)

    def arrived(ref, send_sem, recv_sem):
        pltpu.make_async_remote_copy(
            src_ref=ref, dst_ref=ref, send_sem=send_sem, recv_sem=recv_sem,
            device_id=(col, sec), device_id_type=MESH,
        ).wait_recv()

    top = pl.ds(0, HALF)
    bottom = pl.ds(HALF, HALF)
    loads[0].wait()
    loads[1].wait()
    loads[2].start()
    g[y, top] = mm(t[0, top], t[1])
    pl.semaphore_wait(barrier, len(partners))

    y_plus, y_minus = (at_y(1), sec), (at_y(-1), sec)
    z_plus, z_minus = (at_z(1), sec), (at_z(-1), sec)
    before, after, opposite = lax.rem(y + 3, Y), lax.rem(y + 1, Y), lax.rem(y + 2, Y)

    def g_rows(direction, index):
        part = (index + 2 * direction) % 4
        return pl.ds(part * QUARTER, QUARTER)

    def g_copy(direction, index, block):
        target = y_plus if direction == 0 else y_minus
        rows = g_rows(direction, index % 4)
        send(g.at[block, rows], target, g_send.at[direction, index], g_recv.at[direction, index])

    def g_wait(direction, index, block):
        rows = g_rows(direction, index % 4)
        arrived(g.at[block, rows], g_send.at[direction, index], g_recv.at[direction, index])

    g_copy(0, 0, y)
    g_copy(0, 1, y)
    g[y, bottom] = mm(t[0, bottom], t[1])
    for direction, index in ((1, 0), (1, 1), (0, 2), (1, 2), (0, 3), (1, 3)):
        g_copy(direction, index, y)

    loads[2].wait()
    row = lax.broadcasted_iota(jnp.int32, (N, N), 0)
    column = lax.broadcasted_iota(jnp.int32, (N, N), 1)
    for c in range(2):
        kept = row < kept_ref[0, c]
        for k in range(TERMS):
            h[c, k] = jnp.where(kept, h[c, k], 0.0)
    for k in range(TERMS):

        @pl.when(z < 4)
        def _():
            h[0, k] = mm(h[0, k], t[1])

        @pl.when(z >= 4)
        def _():
            h[1, k] = mm(t[0], h[1, k])

    neighbours = (before, after)
    for index in range(2):
        for direction in range(2):
            g_wait(direction, index, neighbours[direction])
            g_copy(direction, index + 4, neighbours[direction])
    for index in range(2, 4):
        for direction in range(2):
            g_wait(direction, index, neighbours[direction])
    for index in range(4, 6):
        for direction in range(2):
            g_wait(direction, index, opposite)

    low = mm(g[0], g[1])
    high = mm(g[2], g[3])
    r[z] = mm(low, high)

    def chunk(direction, part, shift=0):
        start = lax.rem(y * QUARTER + direction * HALF + part * ROWS + shift, N)
        return pl.ds(pl.multiple_of(start, ROWS), ROWS)

    def z_block(direction, step):
        return lax.rem(z - step + Z, Z) if direction == 0 else lax.rem(z + step, Z)

    def z_copy(direction, step, part):
        ref = r.at[z_block(direction, step - 1), chunk(direction, part)]
        target = z_plus if direction == 0 else z_minus
        send(ref, target, z_send.at[direction, step - 1, part], z_recv.at[direction, step - 1, part])

    def z_wait(direction, step, part):
        ref = r.at[z_block(direction, step), chunk(direction, part)]
        arrived(ref, z_send.at[direction, step - 1, part], z_recv.at[direction, step - 1, part])

    def y_copy(direction, step, part):
        ref = r.at[z_block(direction, step), chunk(direction, part)]
        target = y_plus if part < PARTS // 2 else y_minus
        send(ref, target, y_send.at[direction, step - 1, part], y_recv.at[direction, step - 1, part])

    def y_wait(direction, step, part):
        shift = 3 * QUARTER if part < PARTS // 2 else QUARTER
        ref = r.at[z_block(direction, step), chunk(direction, part, shift)]
        arrived(ref, y_send.at[direction, step - 1, part], y_recv.at[direction, step - 1, part])

    for part in range(PARTS):
        for direction in range(2):
            z_copy(direction, 1, part)

    acc_p[...] = low
    acc_m[...] = high

    @pl.when(y == 0)
    def _():
        acc_m[...] = mm(g[1], acc_m[...])

    @pl.when(y == 1)
    def _():
        acc_p[...] = g[0]

    @pl.when(y == 2)
    def _():
        acc_m[...] = g[3]

    @pl.when(y == 3)
    def _():
        acc_p[...] = mm(acc_p[...], g[2])

    @pl.when(y == 0)
    def _():
        acc_p[...] = (row == column).astype(F32)

    @pl.when(y == 3)
    def _():
        acc_m[...] = (row == column).astype(F32)

    def lefts_from(left0):
        left1 = mm(left0, t[0])
        left1_ref[...] = left1
        lout[0] = jnp.where(column < kept_ref[0, 0], left0, 0.0)
        lout[1] = jnp.where(column < kept_ref[0, 1], left1, 0.0)

    def take_blocks(step):
        for direction in range(2):
            for part in range(PARTS):
                y_wait(direction, step, part)
        plus = z_block(0, step)
        minus = z_block(1, step)

        @pl.when(step <= z)
        def _():
            acc_p[...] = mm(r[plus], acc_p[...])

        @pl.when(step == z + 1)
        def _():
            post[...] = r[plus]

        @pl.when(step > z + 1)
        def _():
            post[...] = mm(r[plus], post[...])

        @pl.when(step <= Z - 1 - z)
        def _():
            acc_m[...] = mm(acc_m[...], r[minus])

        @pl.when(step == Z - z)
        def _():
            post[...] = r[minus]

        @pl.when(step > Z - z)
        def _():
            post[...] = mm(post[...], r[minus])

    for step in range(1, 4):
        for part in range(PARTS):
            for direction in range(2):
                z_wait(direction, step, part)
                z_copy(direction, step + 1, part)
                y_copy(direction, step, part)
        if step > 1:
            take_blocks(step - 1)

    def from_lefts():
        lefts_from(acc_p[...])
        whole = mm(left1_ref[...], t[1])
        inner[0] = mm(acc_p[...], whole, TN)
        inner[1] = mm(left1_ref[...], whole, TN)
        inner[2] = mm(whole, whole, TN)

    def from_rights():
        right1 = acc_m[...]
        right0 = mm(t[1], right1)
        whole = mm(t[0], right0)
        inner[0] = mm(whole, right0, NT)
        inner[1] = mm(whole, right1, NT)
        inner[2] = mm(whole, whole, NT)

    pl.when(z < 3)(from_lefts)
    pl.when(z > 4)(from_rights)
    take_blocks(3)
    pl.when(z == 3)(from_lefts)
    pl.when(z == 4)(from_rights)

    for part in range(PARTS):
        for direction in range(2):
            z_wait(direction, 4, part)
    middle = lax.rem(z + 4, Z)

    @pl.when(z < 4)
    def _():
        acc_m[...] = mm(acc_m[...], r[middle])

    @pl.when(z < 3)
    def _():
        acc_m[...] = mm(acc_m[...], post[...])

    @pl.when(z >= 4)
    def _():
        acc_p[...] = mm(r[middle], acc_p[...])

    @pl.when(z > 4)
    def _():
        acc_p[...] = mm(post[...], acc_p[...])

    def lanes(x):
        x = jnp.sum(x, axis=0, keepdims=True)
        return x[:, :128] + x[:, 128:]

    def reduce(inner0, inner1, gram):
        rows = [lanes(inner0 * h[0, k]) for k in range(TERMS)]
        rows += [lanes(inner1 * h[1, k]) for k in range(TERMS)]
        rows += [lanes(inner[2] * gram), jnp.zeros((1, 128), F32)]
        red[sec] = jnp.concatenate(rows, axis=0)

    @pl.when(z < 4)
    def _():
        gram = mm(acc_m[...], acc_m[...], NT)
        reduce(mm(inner[0], gram), mm(inner[1], gram), gram)

    @pl.when(z >= 4)
    def _():
        gram = mm(acc_p[...], acc_p[...], TN)
        reduce(mm(gram, inner[0]), mm(gram, inner[1]), gram)

    for d in (4, 3, 5, 2, 6, 1, 7):
        send(red.at[sec], (col, lax.rem(sec + d, S)), s_send.at[d], s_recv.at[d])

    @pl.when(z >= 4)
    def _():
        lefts_from(acc_p[...])

    for d in range(1, S):
        arrived(red.at[lax.rem(sec - d + S, S)], s_send.at[d], s_recv.at[d])
    total = red[0]
    for k in range(1, S):
        total = total + red[k]
    sums_ref[...] = total

    for copy in sends:
        copy.wait_send()


def finish(lefts, sums_ref, left_hbm, energy_ref, sems):
    stores = []
    for c in range(2):
        copy = pltpu.make_async_copy(lefts.at[c], left_hbm.at[c, 0], sems.at[c])
        copy.start()
        stores.append(copy)
    total = sums_ref[...]
    total = jnp.sum(total, axis=1, keepdims=True)
    values = (float(N * S) * total[0:6]) / total[6:7]
    place = 3 * lax.broadcasted_iota(jnp.int32, (2, 3), 0) + lax.broadcasted_iota(jnp.int32, (2, 3), 1)
    energy = jnp.zeros((2, 3), F32)
    for k in range(6):
        energy = jnp.where(place == k, values[k:k + 1], energy)
    energy_ref[...] = energy
    for copy in stores:
        copy.wait()


def per_device(transfer, hamiltonian, kept):
    dma = pltpu.SemaphoreType.DMA
    vmem = pl.BlockSpec(memory_space=pltpu.VMEM)
    lefts, sums = pl.pallas_call(
        kernel,
        name="chain",
        out_shape=(pltpu.VMEM((2, N, N), F32), pltpu.VMEM((8, 128), F32)),
        in_specs=[
            pl.BlockSpec(memory_space=pl.ANY),
            pl.BlockSpec(memory_space=pl.ANY),
            pl.BlockSpec(memory_space=pltpu.SMEM),
        ],
        out_specs=(vmem, vmem),
        scratch_shapes=[
            pltpu.VMEM((2, N, N), F32),
            pltpu.VMEM((2, TERMS, N, N), F32),
            pltpu.VMEM((Y, N, N), F32),
            pltpu.VMEM((Z, N, N), F32),
            *[pltpu.VMEM((N, N), F32)] * 4,
            pltpu.VMEM((3, N, N), F32),
            pltpu.VMEM((S, 8, 128), F32),
            dma((3,)),
            dma((2, 6)),
            dma((2, 6)),
            dma((2, 4, PARTS)),
            dma((2, 4, PARTS)),
            dma((2, 3, PARTS)),
            dma((2, 3, PARTS)),
            dma((S,)),
            dma((S,)),
        ],
        compiler_params=pltpu.CompilerParams(collective_id=0, has_side_effects=True),
    )(transfer, hamiltonian, kept.T)
    return pl.pallas_call(
        finish,
        name="finish",
        out_shape=(
            jax.ShapeDtypeStruct((2, 1, N, N), F32),
            jax.ShapeDtypeStruct((2, TERMS), F32),
        ),
        in_specs=[vmem, vmem],
        out_specs=(pl.BlockSpec(memory_space=pl.ANY), vmem),
        scratch_shapes=[dma((2,))],
    )(*(pltpu.with_memory_space_constraint(x, pltpu.VMEM) for x in (lefts, sums)))


def solution(mesh):
    in_specs = (P("col", "sec", None, None), P("col", None, "sec", None, None), P("col", "sec"))
    out_specs = (P("col", "sec", None, None), P("col", None))
    return jax.shard_map(
        per_device, mesh=mesh, in_specs=in_specs, out_specs=out_specs, check_vma=False
    )
```

```python
import jax
import jax.numpy as jnp
from jax import lax
from jax.experimental import pallas as pl
from jax.experimental.pallas import tpu as pltpu
from jax.sharding import PartitionSpec as P

MESH = pl.DeviceIdType.MESH
F32 = jnp.float32
BF16 = jnp.bfloat16
Y = 4
Z = 8
S = 8
N = 256
HALF = N // 2
QUARTER = N // 4
PARTS = 4
ROWS = HALF // PARTS
TERMS = 3
NN = (((1,), (0,)), ((), ()))
NT = (((1,), (1,)), ((), ()))
TN = (((0,), (0,)), ((), ()))


def split(x):
    high = x.astype(BF16)
    return high, (x - high.astype(F32)).astype(BF16)


def mm(a, b, dims=NN):
    ah, al = split(a)
    bh, bl = split(b)

    def dot(p, q):
        return lax.dot_general(p, q, dims, preferred_element_type=F32)

    return dot(ah, bh) + (dot(ah, bl) + dot(al, bh))


def kernel(
    t_hbm, h_hbm, kept_ref,
    lout, sums_ref,
    t, h, g, r, away, acc_p, acc_m, post, left1_ref, inner, red,
    load_sem, g_send, g_recv, z_send, z_recv, y_send, y_recv, c_send, c_recv, s_send, s_recv,
):
    col = lax.axis_index("col")
    sec = lax.axis_index("sec")
    y = lax.rem(col, Y)
    z = col // Y

    def at_y(d):
        return z * Y + lax.rem(y + d + Y, Y)

    def at_z(d):
        return lax.rem(z + d + Z, Z) * Y + y

    loads = []
    for c in range(2):
        loads.append(pltpu.make_async_copy(t_hbm.at[c, 0], t.at[c], load_sem.at[c]))
    loads.append(pltpu.make_async_copy(h_hbm.at[:, :, 0], h, load_sem.at[2]))
    loads[0].start()
    loads[1].start()

    barrier = pltpu.get_barrier_semaphore()
    other = sec + 1 - 2 * lax.rem(sec, 2)
    partners = [(at_y(1), sec), (at_y(-1), sec), (at_y(1), other), (at_y(-1), other)]
    partners += [(at_z(1), other), (at_z(-1), other)]
    partners += [(col, lax.rem(sec + d, S)) for d in range(1, S)]
    for partner in partners:
        pl.semaphore_signal(barrier, inc=1, device_id=partner, device_id_type=MESH)

    sends = []

    def send(ref, target, send_sem, recv_sem, to=None):
        copy = pltpu.make_async_remote_copy(
            src_ref=ref, dst_ref=ref if to is None else to, send_sem=send_sem, recv_sem=recv_sem,
            device_id=target, device_id_type=MESH,
        )
        copy.start()
        sends.append(copy)

    def arrived(ref, send_sem, recv_sem):
        pltpu.make_async_remote_copy(
            src_ref=ref, dst_ref=ref, send_sem=send_sem, recv_sem=recv_sem,
            device_id=(col, sec), device_id_type=MESH,
        ).wait_recv()

    top = pl.ds(0, HALF)
    bottom = pl.ds(HALF, HALF)
    loads[0].wait()
    loads[1].wait()
    loads[2].start()
    g[y, top] = mm(t[0, top], t[1])
    pl.semaphore_wait(barrier, len(partners))

    y_plus, y_minus = (at_y(1), sec), (at_y(-1), sec)
    z_plus, z_minus = (at_z(1), other), (at_z(-1), other)
    before, after, opposite = lax.rem(y + 3, Y), lax.rem(y + 1, Y), lax.rem(y + 2, Y)

    def g_rows(direction, index):
        part = (index + 2 * direction) % 4
        return pl.ds(part * QUARTER, QUARTER)

    def g_copy(direction, index, block):
        target = y_plus if direction == 0 else y_minus
        rows = g_rows(direction, index % 4)
        send(g.at[block, rows], target, g_send.at[direction, index], g_recv.at[direction, index])

    def g_wait(direction, index, block):
        rows = g_rows(direction, index % 4)
        arrived(g.at[block, rows], g_send.at[direction, index], g_recv.at[direction, index])

    g_copy(0, 0, y)
    g_copy(0, 1, y)
    g[y, bottom] = mm(t[0, bottom], t[1])
    for direction, index in ((1, 0), (1, 1), (0, 2), (1, 2), (0, 3), (1, 3)):
        g_copy(direction, index, y)

    loads[2].wait()
    row = lax.broadcasted_iota(jnp.int32, (N, N), 0)
    column = lax.broadcasted_iota(jnp.int32, (N, N), 1)
    for c in range(2):
        kept = row < kept_ref[0, c]
        for k in range(TERMS):
            h[c, k] = jnp.where(kept, h[c, k], 0.0)
    for k in range(TERMS):

        @pl.when(z < 4)
        def _():
            h[0, k] = mm(h[0, k], t[1])

        @pl.when(z >= 4)
        def _():
            h[1, k] = mm(t[0], h[1, k])

    neighbours = (before, after)
    for index in range(2):
        for direction in range(2):
            g_wait(direction, index, neighbours[direction])
            g_copy(direction, index + 4, neighbours[direction])
    for index in range(2, 4):
        for direction in range(2):
            g_wait(direction, index, neighbours[direction])
    for index in range(4, 6):
        for direction in range(2):
            g_wait(direction, index, opposite)

    low = mm(g[0], g[1])
    high = mm(g[2], g[3])
    r[z] = mm(low, high)

    def chunk(direction, part, shift=0):
        start = lax.rem(y * QUARTER + direction * HALF + part * ROWS + shift, N)
        return pl.ds(pl.multiple_of(start, ROWS), ROWS)

    def z_block(direction, step):
        return lax.rem(z - step + Z, Z) if direction == 0 else lax.rem(z + step, Z)

    def z_copy(direction, step, part):
        place = (z_block(direction, step - 1), chunk(direction, part))
        target = z_plus if direction == 0 else z_minus
        here, there = (r, away) if step % 2 else (away, r)
        index = (direction, step - 1, part)
        send(here.at[place], target, z_send.at[index], z_recv.at[index], there.at[place])

    def z_wait(direction, step, part):
        ref = (away if step % 2 else r).at[z_block(direction, step), chunk(direction, part)]
        index = (direction, step - 1, part)
        arrived(ref, z_send.at[index], z_recv.at[index])

    def y_copy(direction, step, part):
        place = (z_block(direction, step), chunk(direction, part))
        owner = other if step % 2 else sec
        target = (at_y(1 if part < PARTS // 2 else -1), owner)
        index = (direction, step - 1, part)
        here = away if step % 2 else r
        send(here.at[place], target, y_send.at[index], y_recv.at[index], r.at[place])

    def c_copy(direction, step, part):
        place = (z_block(direction, step), chunk(direction, part))
        index = (direction, step // 2, part)
        send(away.at[place], (col, other), c_send.at[index], c_recv.at[index], r.at[place])

    def c_wait(direction, step, part):
        index = (direction, step // 2, part)
        arrived(r.at[z_block(direction, step), chunk(direction, part)], c_send.at[index], c_recv.at[index])

    def y_wait(direction, step, part):
        shift = 3 * QUARTER if part < PARTS // 2 else QUARTER
        ref = r.at[z_block(direction, step), chunk(direction, part, shift)]
        arrived(ref, y_send.at[direction, step - 1, part], y_recv.at[direction, step - 1, part])

    for part in range(PARTS):
        for direction in range(2):
            z_copy(direction, 1, part)

    acc_p[...] = low
    acc_m[...] = high

    @pl.when(y == 0)
    def _():
        acc_m[...] = mm(g[1], acc_m[...])

    @pl.when(y == 1)
    def _():
        acc_p[...] = g[0]

    @pl.when(y == 2)
    def _():
        acc_m[...] = g[3]

    @pl.when(y == 3)
    def _():
        acc_p[...] = mm(acc_p[...], g[2])

    @pl.when(y == 0)
    def _():
        acc_p[...] = (row == column).astype(F32)

    @pl.when(y == 3)
    def _():
        acc_m[...] = (row == column).astype(F32)

    def lefts_from(left0):
        left1 = mm(left0, t[0])
        left1_ref[...] = left1
        lout[0] = jnp.where(column < kept_ref[0, 0], left0, 0.0)
        lout[1] = jnp.where(column < kept_ref[0, 1], left1, 0.0)

    def take_blocks(step):
        for direction in range(2):
            for part in range(PARTS):
                if step % 2:
                    c_wait(direction, step, part)
                y_wait(direction, step, part)
        plus = z_block(0, step)
        minus = z_block(1, step)

        @pl.when(step <= z)
        def _():
            acc_p[...] = mm(r[plus], acc_p[...])

        @pl.when(step == z + 1)
        def _():
            post[...] = r[plus]

        @pl.when(step > z + 1)
        def _():
            post[...] = mm(r[plus], post[...])

        @pl.when(step <= Z - 1 - z)
        def _():
            acc_m[...] = mm(acc_m[...], r[minus])

        @pl.when(step == Z - z)
        def _():
            post[...] = r[minus]

        @pl.when(step > Z - z)
        def _():
            post[...] = mm(post[...], r[minus])

    for step in range(1, 4):
        for part in range(PARTS):
            for direction in range(2):
                z_wait(direction, step, part)
                z_copy(direction, step + 1, part)
                y_copy(direction, step, part)
                if step % 2:
                    c_copy(direction, step, part)
        if step > 1:
            take_blocks(step - 1)

    def from_lefts():
        lefts_from(acc_p[...])
        whole = mm(left1_ref[...], t[1])
        inner[0] = mm(acc_p[...], whole, TN)
        inner[1] = mm(left1_ref[...], whole, TN)
        inner[2] = mm(whole, whole, TN)

    def from_rights():
        right1 = acc_m[...]
        right0 = mm(t[1], right1)
        whole = mm(t[0], right0)
        inner[0] = mm(whole, right0, NT)
        inner[1] = mm(whole, right1, NT)
        inner[2] = mm(whole, whole, NT)

    pl.when(z < 3)(from_lefts)
    pl.when(z > 4)(from_rights)
    take_blocks(3)
    pl.when(z == 3)(from_lefts)
    pl.when(z == 4)(from_rights)

    for part in range(PARTS):
        for direction in range(2):
            z_wait(direction, 4, part)
    middle = lax.rem(z + 4, Z)

    @pl.when(z < 4)
    def _():
        acc_m[...] = mm(acc_m[...], r[middle])

    @pl.when(z < 3)
    def _():
        acc_m[...] = mm(acc_m[...], post[...])

    @pl.when(z >= 4)
    def _():
        acc_p[...] = mm(r[middle], acc_p[...])

    @pl.when(z > 4)
    def _():
        acc_p[...] = mm(post[...], acc_p[...])

    def lanes(x):
        x = jnp.sum(x, axis=0, keepdims=True)
        return x[:, :128] + x[:, 128:]

    def reduce(inner0, inner1, gram):
        rows = [lanes(inner0 * h[0, k]) for k in range(TERMS)]
        rows += [lanes(inner1 * h[1, k]) for k in range(TERMS)]
        rows += [lanes(inner[2] * gram), jnp.zeros((1, 128), F32)]
        red[sec] = jnp.concatenate(rows, axis=0)

    @pl.when(z < 4)
    def _():
        gram = mm(acc_m[...], acc_m[...], NT)
        reduce(mm(inner[0], gram), mm(inner[1], gram), gram)

    @pl.when(z >= 4)
    def _():
        gram = mm(acc_p[...], acc_p[...], TN)
        reduce(mm(gram, inner[0]), mm(gram, inner[1]), gram)

    for d in (4, 3, 5, 2, 6, 1, 7):
        send(red.at[sec], (col, lax.rem(sec + d, S)), s_send.at[d], s_recv.at[d])

    @pl.when(z >= 4)
    def _():
        lefts_from(acc_p[...])

    for d in range(1, S):
        arrived(red.at[lax.rem(sec - d + S, S)], s_send.at[d], s_recv.at[d])
    total = red[0]
    for k in range(1, S):
        total = total + red[k]
    sums_ref[...] = total

    for copy in sends:
        copy.wait_send()


def finish(lefts, sums_ref, left_hbm, energy_ref, sems):
    stores = []
    for c in range(2):
        copy = pltpu.make_async_copy(lefts.at[c], left_hbm.at[c, 0], sems.at[c])
        copy.start()
        stores.append(copy)
    total = sums_ref[...]
    total = jnp.sum(total, axis=1, keepdims=True)
    values = (float(N * S) * total[0:6]) / total[6:7]
    place = 3 * lax.broadcasted_iota(jnp.int32, (2, 3), 0) + lax.broadcasted_iota(jnp.int32, (2, 3), 1)
    energy = jnp.zeros((2, 3), F32)
    for k in range(6):
        energy = jnp.where(place == k, values[k:k + 1], energy)
    energy_ref[...] = energy
    for copy in stores:
        copy.wait()


def per_device(transfer, hamiltonian, kept):
    dma = pltpu.SemaphoreType.DMA
    vmem = pl.BlockSpec(memory_space=pltpu.VMEM)
    lefts, sums = pl.pallas_call(
        kernel,
        name="chain",
        out_shape=(pltpu.VMEM((2, N, N), F32), pltpu.VMEM((8, 128), F32)),
        in_specs=[
            pl.BlockSpec(memory_space=pl.ANY),
            pl.BlockSpec(memory_space=pl.ANY),
            pl.BlockSpec(memory_space=pltpu.SMEM),
        ],
        out_specs=(vmem, vmem),
        scratch_shapes=[
            pltpu.VMEM((2, N, N), F32),
            pltpu.VMEM((2, TERMS, N, N), F32),
            pltpu.VMEM((Y, N, N), F32),
            pltpu.VMEM((Z, N, N), F32),
            pltpu.VMEM((Z, N, N), F32),
            *[pltpu.VMEM((N, N), F32)] * 4,
            pltpu.VMEM((3, N, N), F32),
            pltpu.VMEM((S, 8, 128), F32),
            dma((3,)),
            dma((2, 6)),
            dma((2, 6)),
            dma((2, 4, PARTS)),
            dma((2, 4, PARTS)),
            dma((2, 3, PARTS)),
            dma((2, 3, PARTS)),
            dma((2, 2, PARTS)),
            dma((2, 2, PARTS)),
            dma((S,)),
            dma((S,)),
        ],
        compiler_params=pltpu.CompilerParams(collective_id=0, has_side_effects=True),
    )(transfer, hamiltonian, kept.T)
    return pl.pallas_call(
        finish,
        name="finish",
        out_shape=(
            jax.ShapeDtypeStruct((2, 1, N, N), F32),
            jax.ShapeDtypeStruct((2, TERMS), F32),
        ),
        in_specs=[vmem, vmem],
        out_specs=(pl.BlockSpec(memory_space=pl.ANY), vmem),
        scratch_shapes=[dma((2,))],
    )(*(pltpu.with_memory_space_constraint(x, pltpu.VMEM) for x in (lefts, sums)))


def solution(mesh):
    in_specs = (P("col", "sec", None, None), P("col", None, "sec", None, None), P("col", "sec"))
    out_specs = (P("col", "sec", None, None), P("col", None))
    return jax.shard_map(
        per_device, mesh=mesh, in_specs=in_specs, out_specs=out_specs, check_vma=False
    )
```

```python
import jax
import jax.numpy as jnp
from jax import lax
from jax.experimental import pallas as pl
from jax.experimental.pallas import tpu as pltpu
from jax.sharding import PartitionSpec as P

MESH = pl.DeviceIdType.MESH
F32 = jnp.float32
BF16 = jnp.bfloat16
Y = 4
Z = 8
S = 8
N = 256
HALF = N // 2
QUARTER = N // 4
PARTS = 4
ROWS = HALF // PARTS
TERMS = 3
NN = (((1,), (0,)), ((), ()))
NT = (((1,), (1,)), ((), ()))
TN = (((0,), (0,)), ((), ()))


def split(x):
    high = x.astype(BF16)
    return high, (x - high.astype(F32)).astype(BF16)


def mm(a, b, dims=NN):
    ah, al = split(a)
    bh, bl = split(b)

    def dot(p, q):
        return lax.dot_general(p, q, dims, preferred_element_type=F32)

    return dot(ah, bh) + (dot(ah, bl) + dot(al, bh))


def kernel(
    t_hbm, h_hbm, kept_ref,
    lout, sums_ref,
    t, h, g, r, away, acc_p, acc_m, post, factor, q, red,
    load_sem, g_send, g_recv, z_send, z_recv, y_send, y_recv, c_send, c_recv, s_send, s_recv,
):
    col = lax.axis_index("col")
    sec = lax.axis_index("sec")
    y = lax.rem(col, Y)
    z = col // Y

    def at_y(d):
        return z * Y + lax.rem(y + d + Y, Y)

    def at_z(d):
        return lax.rem(z + d + Z, Z) * Y + y

    loads = []
    for c in range(2):
        loads.append(pltpu.make_async_copy(t_hbm.at[c, 0], t.at[c], load_sem.at[c]))
    loads.append(pltpu.make_async_copy(h_hbm.at[:, :, 0], h, load_sem.at[2]))
    loads[0].start()
    loads[1].start()

    barrier = pltpu.get_barrier_semaphore()
    other = sec + 1 - 2 * lax.rem(sec, 2)
    partners = [(at_y(1), sec), (at_y(-1), sec), (at_y(1), other), (at_y(-1), other)]
    partners += [(at_z(1), other), (at_z(-1), other)]
    partners += [(col, lax.rem(sec + d, S)) for d in range(1, S)]
    for partner in partners:
        pl.semaphore_signal(barrier, inc=1, device_id=partner, device_id_type=MESH)

    sends = []

    def send(ref, target, send_sem, recv_sem, to=None):
        copy = pltpu.make_async_remote_copy(
            src_ref=ref, dst_ref=ref if to is None else to, send_sem=send_sem, recv_sem=recv_sem,
            device_id=target, device_id_type=MESH,
        )
        copy.start()
        sends.append(copy)

    def arrived(ref, send_sem, recv_sem):
        pltpu.make_async_remote_copy(
            src_ref=ref, dst_ref=ref, send_sem=send_sem, recv_sem=recv_sem,
            device_id=(col, sec), device_id_type=MESH,
        ).wait_recv()

    top = pl.ds(0, HALF)
    bottom = pl.ds(HALF, HALF)
    loads[0].wait()
    loads[1].wait()
    loads[2].start()
    g[y, top] = mm(t[0, top], t[1])
    pl.semaphore_wait(barrier, len(partners))

    y_plus, y_minus = (at_y(1), sec), (at_y(-1), sec)
    z_plus, z_minus = (at_z(1), other), (at_z(-1), other)
    before, after, opposite = lax.rem(y + 3, Y), lax.rem(y + 1, Y), lax.rem(y + 2, Y)

    def g_rows(direction, index):
        part = (index + 2 * direction) % 4
        return pl.ds(part * QUARTER, QUARTER)

    def g_copy(direction, index, block):
        target = y_plus if direction == 0 else y_minus
        rows = g_rows(direction, index % 4)
        send(g.at[block, rows], target, g_send.at[direction, index], g_recv.at[direction, index])

    def g_wait(direction, index, block):
        rows = g_rows(direction, index % 4)
        arrived(g.at[block, rows], g_send.at[direction, index], g_recv.at[direction, index])

    g_copy(0, 0, y)
    g_copy(0, 1, y)
    g[y, bottom] = mm(t[0, bottom], t[1])
    for direction, index in ((1, 0), (1, 1), (0, 2), (1, 2), (0, 3), (1, 3)):
        g_copy(direction, index, y)

    loads[2].wait()
    row = lax.broadcasted_iota(jnp.int32, (N, N), 0)
    column = lax.broadcasted_iota(jnp.int32, (N, N), 1)
    for c in range(2):
        kept = row < kept_ref[0, c]
        for k in range(TERMS):
            h[c, k] = jnp.where(kept, h[c, k], 0.0)
    for k in range(TERMS):

        @pl.when(z < 4)
        def _():
            h[0, k] = mm(h[0, k], t[1])

        @pl.when(z >= 4)
        def _():
            h[1, k] = mm(t[0], h[1, k])

    neighbours = (before, after)
    for index in range(2):
        for direction in range(2):
            g_wait(direction, index, neighbours[direction])
            g_copy(direction, index + 4, neighbours[direction])
    for index in range(2, 4):
        for direction in range(2):
            g_wait(direction, index, neighbours[direction])
    for index in range(4, 6):
        for direction in range(2):
            g_wait(direction, index, opposite)

    low = mm(g[0], g[1])
    high = mm(g[2], g[3])
    r[z] = mm(low, high)

    def chunk(direction, part, shift=0):
        start = lax.rem(y * QUARTER + direction * HALF + part * ROWS + shift, N)
        return pl.ds(pl.multiple_of(start, ROWS), ROWS)

    def z_block(direction, step):
        return lax.rem(z - step + Z, Z) if direction == 0 else lax.rem(z + step, Z)

    def z_copy(direction, step, part):
        place = (z_block(direction, step - 1), chunk(direction, part))
        target = z_plus if direction == 0 else z_minus
        here, there = (r, away) if step % 2 else (away, r)
        index = (direction, step - 1, part)
        send(here.at[place], target, z_send.at[index], z_recv.at[index], there.at[place])

    def z_wait(direction, step, part):
        ref = (away if step % 2 else r).at[z_block(direction, step), chunk(direction, part)]
        index = (direction, step - 1, part)
        arrived(ref, z_send.at[index], z_recv.at[index])

    def y_copy(direction, step, part):
        place = (z_block(direction, step), chunk(direction, part))
        owner = other if step % 2 else sec
        target = (at_y(1 if part < PARTS // 2 else -1), owner)
        index = (direction, step - 1, part)
        here = away if step % 2 else r
        send(here.at[place], target, y_send.at[index], y_recv.at[index], r.at[place])

    def c_copy(direction, step, part):
        place = (z_block(direction, step), chunk(direction, part))
        index = (direction, step // 2, part)
        send(away.at[place], (col, other), c_send.at[index], c_recv.at[index], r.at[place])

    def c_wait(direction, step, part):
        index = (direction, step // 2, part)
        arrived(r.at[z_block(direction, step), chunk(direction, part)], c_send.at[index], c_recv.at[index])

    def y_wait(direction, step, part):
        shift = 3 * QUARTER if part < PARTS // 2 else QUARTER
        ref = r.at[z_block(direction, step), chunk(direction, part, shift)]
        arrived(ref, y_send.at[direction, step - 1, part], y_recv.at[direction, step - 1, part])

    for part in range(PARTS):
        for direction in range(2):
            z_copy(direction, 1, part)

    acc_p[...] = low
    acc_m[...] = high

    @pl.when(y == 0)
    def _():
        acc_m[...] = mm(g[1], acc_m[...])

    @pl.when(y == 1)
    def _():
        acc_p[...] = g[0]

    @pl.when(y == 2)
    def _():
        acc_m[...] = g[3]

    @pl.when(y == 3)
    def _():
        acc_p[...] = mm(acc_p[...], g[2])

    @pl.when(y == 0)
    def _():
        acc_p[...] = (row == column).astype(F32)

    @pl.when(y == 3)
    def _():
        acc_m[...] = (row == column).astype(F32)

    def write_lefts(left0, left1):
        lout[0] = jnp.where(column < kept_ref[0, 0], left0, 0.0)
        lout[1] = jnp.where(column < kept_ref[0, 1], left1, 0.0)

    def take_blocks(step):
        for direction in range(2):
            for part in range(PARTS):
                if step % 2:
                    c_wait(direction, step, part)
                y_wait(direction, step, part)
        plus = z_block(0, step)
        minus = z_block(1, step)

        @pl.when(step <= z - step // 3)
        def _():
            acc_p[...] = mm(r[plus], acc_p[...])

        @pl.when(step == z + 1)
        def _():
            post[...] = r[plus]

        @pl.when(step > z + 1)
        def _():
            post[...] = mm(r[plus], post[...])

        @pl.when(step <= Z - 1 - z - step // 3)
        def _():
            acc_m[...] = mm(acc_m[...], r[minus])

        @pl.when(step == Z - z)
        def _():
            post[...] = r[minus]

        @pl.when(step > Z - z)
        def _():
            post[...] = mm(post[...], r[minus])

    for step in range(1, 4):
        for part in range(PARTS):
            for direction in range(2):
                z_wait(direction, step, part)
                z_copy(direction, step + 1, part)
                y_copy(direction, step, part)
                if step % 2:
                    c_copy(direction, step, part)
        if step > 1:
            take_blocks(step - 1)

    @pl.when(z < 4)
    def _():
        x0 = acc_p[...]
        x1 = mm(x0, t[0])
        x2 = mm(x1, t[1])
        q[6] = x2
        factor[...] = x2
        for k in range(TERMS):
            q[k] = mm(x0, h[0, k])
            q[3 + k] = mm(x1, h[1, k])
        write_lefts(x0, x1)

    @pl.when(z >= 4)
    def _():
        x0 = acc_m[...]
        x1 = mm(t[1], x0)
        x2 = mm(t[0], x1)
        q[6] = x2
        factor[...] = x2
        for k in range(TERMS):
            q[k] = mm(h[0, k], x1)
            q[3 + k] = mm(h[1, k], x0)

    take_blocks(3)

    @pl.when(z == 3)
    def _():
        block = r[0]
        factor[...] = mm(block, mm(block, factor[...]), TN)

    @pl.when(z == 4)
    def _():
        block = r[Z - 1]
        factor[...] = mm(mm(factor[...], block), block, NT)

    for part in range(PARTS):
        for direction in range(2):
            z_wait(direction, 4, part)
    middle = lax.rem(z + 4, Z)

    @pl.when(z < 4)
    def _():
        acc_m[...] = mm(acc_m[...], r[middle])

    @pl.when(z < 3)
    def _():
        acc_m[...] = mm(acc_m[...], post[...])

    @pl.when(z >= 4)
    def _():
        acc_p[...] = mm(r[middle], acc_p[...])

    @pl.when(z > 4)
    def _():
        acc_p[...] = mm(post[...], acc_p[...])

    def lanes(x):
        x = jnp.sum(x, axis=0, keepdims=True)
        return x[:, :128] + x[:, 128:]

    def reduce(v):
        rows = [lanes(v * q[k]) for k in range(7)] + [jnp.zeros((1, 128), F32)]
        red[sec] = jnp.concatenate(rows, axis=0)

    @pl.when(z < 4)
    def _():
        gram = mm(acc_m[...], acc_m[...], NT)
        reduce(mm(factor[...], gram))

    @pl.when(z >= 4)
    def _():
        gram = mm(acc_p[...], acc_p[...], TN)
        reduce(mm(gram, factor[...]))

    for d in (4, 3, 5, 2, 6, 1, 7):
        send(red.at[sec], (col, lax.rem(sec + d, S)), s_send.at[d], s_recv.at[d])

    @pl.when(z == 3)
    def _():
        left0 = mm(r[0], acc_p[...])
        write_lefts(left0, mm(left0, t[0]))

    @pl.when(z >= 4)
    def _():
        write_lefts(acc_p[...], mm(acc_p[...], t[0]))

    for d in range(1, S):
        arrived(red.at[lax.rem(sec - d + S, S)], s_send.at[d], s_recv.at[d])
    total = red[0]
    for k in range(1, S):
        total = total + red[k]
    sums_ref[...] = total

    for copy in sends:
        copy.wait_send()


def finish(lefts, sums_ref, left_hbm, energy_ref, sems):
    stores = []
    for c in range(2):
        copy = pltpu.make_async_copy(lefts.at[c], left_hbm.at[c, 0], sems.at[c])
        copy.start()
        stores.append(copy)
    total = sums_ref[...]
    total = jnp.sum(total, axis=1, keepdims=True)
    values = (float(N * S) * total[0:6]) / total[6:7]
    place = 3 * lax.broadcasted_iota(jnp.int32, (2, 3), 0) + lax.broadcasted_iota(jnp.int32, (2, 3), 1)
    energy = jnp.zeros((2, 3), F32)
    for k in range(6):
        energy = jnp.where(place == k, values[k:k + 1], energy)
    energy_ref[...] = energy
    for copy in stores:
        copy.wait()


def per_device(transfer, hamiltonian, kept):
    dma = pltpu.SemaphoreType.DMA
    vmem = pl.BlockSpec(memory_space=pltpu.VMEM)
    lefts, sums = pl.pallas_call(
        kernel,
        name="chain",
        out_shape=(pltpu.VMEM((2, N, N), F32), pltpu.VMEM((8, 128), F32)),
        in_specs=[
            pl.BlockSpec(memory_space=pl.ANY),
            pl.BlockSpec(memory_space=pl.ANY),
            pl.BlockSpec(memory_space=pltpu.SMEM),
        ],
        out_specs=(vmem, vmem),
        scratch_shapes=[
            pltpu.VMEM((2, N, N), F32),
            pltpu.VMEM((2, TERMS, N, N), F32),
            pltpu.VMEM((Y, N, N), F32),
            pltpu.VMEM((Z, N, N), F32),
            pltpu.VMEM((Z, N, N), F32),
            *[pltpu.VMEM((N, N), F32)] * 4,
            pltpu.VMEM((7, N, N), F32),
            pltpu.VMEM((S, 8, 128), F32),
            dma((3,)),
            dma((2, 6)),
            dma((2, 6)),
            dma((2, 4, PARTS)),
            dma((2, 4, PARTS)),
            dma((2, 3, PARTS)),
            dma((2, 3, PARTS)),
            dma((2, 2, PARTS)),
            dma((2, 2, PARTS)),
            dma((S,)),
            dma((S,)),
        ],
        compiler_params=pltpu.CompilerParams(collective_id=0, has_side_effects=True),
    )(transfer, hamiltonian, kept.T)
    return pl.pallas_call(
        finish,
        name="finish",
        out_shape=(
            jax.ShapeDtypeStruct((2, 1, N, N), F32),
            jax.ShapeDtypeStruct((2, TERMS), F32),
        ),
        in_specs=[vmem, vmem],
        out_specs=(pl.BlockSpec(memory_space=pl.ANY), vmem),
        scratch_shapes=[dma((2,))],
    )(*(pltpu.with_memory_space_constraint(x, pltpu.VMEM) for x in (lefts, sums)))


def solution(mesh):
    in_specs = (P("col", "sec", None, None), P("col", None, "sec", None, None), P("col", "sec"))
    out_specs = (P("col", "sec", None, None), P("col", None))
    return jax.shard_map(
        per_device, mesh=mesh, in_specs=in_specs, out_specs=out_specs, check_vma=False
    )
```

```python
import jax
import jax.numpy as jnp
from jax import lax
from jax.experimental import pallas as pl
from jax.experimental.pallas import tpu as pltpu
from jax.sharding import PartitionSpec as P

MESH = pl.DeviceIdType.MESH
F32 = jnp.float32
BF16 = jnp.bfloat16
Y = 4
Z = 8
S = 8
N = 256
HALF = N // 2
QUARTER = N // 4
PARTS = 4
ROWS = HALF // PARTS
TERMS = 3
NN = (((1,), (0,)), ((), ()))
NT = (((1,), (1,)), ((), ()))
TN = (((0,), (0,)), ((), ()))


def split(x):
    high = x.astype(BF16)
    return high, (x - high.astype(F32)).astype(BF16)


def mm(a, b, dims=NN):
    ah, al = split(a)
    bh, bl = split(b)

    def dot(p, q):
        return lax.dot_general(p, q, dims, preferred_element_type=F32)

    return dot(ah, bh) + (dot(ah, bl) + dot(al, bh))


def kernel(
    t_hbm, h_hbm, kept_ref,
    lout, sums_ref,
    t, h, g, r, away, acc_p, acc_m, post, factor, q, red,
    load_sem, g_send, g_recv, z_send, z_recv, y_send, y_recv, c_send, c_recv, s_send, s_recv,
):
    col = lax.axis_index("col")
    sec = lax.axis_index("sec")
    y = lax.rem(col, Y)
    z = col // Y

    def at_y(d):
        return z * Y + lax.rem(y + d + Y, Y)

    def at_z(d):
        return lax.rem(z + d + Z, Z) * Y + y

    loads = []
    for c in range(2):
        loads.append(pltpu.make_async_copy(t_hbm.at[c, 0], t.at[c], load_sem.at[c]))
    loads.append(pltpu.make_async_copy(h_hbm.at[:, :, 0], h, load_sem.at[2]))
    loads[0].start()
    loads[1].start()

    barrier = pltpu.get_barrier_semaphore()
    other = sec + 1 - 2 * lax.rem(sec, 2)
    partners = [(at_y(1), sec), (at_y(-1), sec), (at_y(1), other), (at_y(-1), other)]
    partners += [(at_z(1), other), (at_z(-1), other)]
    partners += [(col, lax.rem(sec + d, S)) for d in range(1, S)]
    for partner in partners:
        pl.semaphore_signal(barrier, inc=1, device_id=partner, device_id_type=MESH)

    sends = []

    def send(ref, target, send_sem, recv_sem, to=None):
        copy = pltpu.make_async_remote_copy(
            src_ref=ref, dst_ref=ref if to is None else to, send_sem=send_sem, recv_sem=recv_sem,
            device_id=target, device_id_type=MESH,
        )
        copy.start()
        sends.append(copy)

    def arrived(ref, send_sem, recv_sem):
        pltpu.make_async_remote_copy(
            src_ref=ref, dst_ref=ref, send_sem=send_sem, recv_sem=recv_sem,
            device_id=(col, sec), device_id_type=MESH,
        ).wait_recv()

    top = pl.ds(0, HALF)
    bottom = pl.ds(HALF, HALF)
    loads[0].wait()
    loads[1].wait()
    loads[2].start()
    g[y, top] = mm(t[0, top], t[1])
    pl.semaphore_wait(barrier, len(partners))

    y_plus, y_minus = (at_y(1), sec), (at_y(-1), sec)
    z_plus, z_minus = (at_z(1), other), (at_z(-1), other)
    before, after, opposite = lax.rem(y + 3, Y), lax.rem(y + 1, Y), lax.rem(y + 2, Y)

    def g_rows(direction, index):
        part = (index + 2 * direction) % 4
        return pl.ds(part * QUARTER, QUARTER)

    def g_copy(direction, index, block):
        target = y_plus if direction == 0 else y_minus
        rows = g_rows(direction, index % 4)
        send(g.at[block, rows], target, g_send.at[direction, index], g_recv.at[direction, index])

    def g_wait(direction, index, block):
        rows = g_rows(direction, index % 4)
        arrived(g.at[block, rows], g_send.at[direction, index], g_recv.at[direction, index])

    g_copy(0, 0, y)
    g_copy(0, 1, y)
    g[y, bottom] = mm(t[0, bottom], t[1])
    for direction, index in ((1, 0), (1, 1), (0, 2), (1, 2), (0, 3), (1, 3)):
        g_copy(direction, index, y)

    loads[2].wait()
    row = lax.broadcasted_iota(jnp.int32, (N, N), 0)
    column = lax.broadcasted_iota(jnp.int32, (N, N), 1)
    for c in range(2):
        kept = row < kept_ref[0, c]
        for k in range(TERMS):
            h[c, k] = jnp.where(kept, h[c, k], 0.0)
    for k in range(TERMS):

        @pl.when(z < 4)
        def _():
            h[0, k] = mm(h[0, k], t[1])

        @pl.when(z >= 4)
        def _():
            h[1, k] = mm(t[0], h[1, k])

    neighbours = (before, after)
    for index in range(2):
        for direction in range(2):
            g_wait(direction, index, neighbours[direction])
            g_copy(direction, index + 4, neighbours[direction])
    for index in range(2, 4):
        for direction in range(2):
            g_wait(direction, index, neighbours[direction])
    for index in range(4, 6):
        for direction in range(2):
            g_wait(direction, index, opposite)

    low = mm(g[0], g[1])
    high = mm(g[2], g[3])
    r[z] = mm(low, high)

    def chunk(direction, part, shift=0):
        start = lax.rem(y * QUARTER + direction * HALF + part * ROWS + shift, N)
        return pl.ds(pl.multiple_of(start, ROWS), ROWS)

    def z_block(direction, step):
        return lax.rem(z - step + Z, Z) if direction == 0 else lax.rem(z + step, Z)

    def z_copy(direction, step, part):
        place = (z_block(direction, step - 1), chunk(direction, part))
        target = z_plus if direction == 0 else z_minus
        here, there = (r, away) if step % 2 else (away, r)
        index = (direction, step - 1, part)
        send(here.at[place], target, z_send.at[index], z_recv.at[index], there.at[place])

    def z_wait(direction, step, part):
        ref = (away if step % 2 else r).at[z_block(direction, step), chunk(direction, part)]
        index = (direction, step - 1, part)
        arrived(ref, z_send.at[index], z_recv.at[index])

    def y_copy(direction, step, part):
        place = (z_block(direction, step), chunk(direction, part))
        owner = other if step % 2 else sec
        target = (at_y(1 - 2 * (part // (PARTS // 2))), owner)
        index = (direction, step - 1, part)
        here = away if step % 2 else r
        send(here.at[place], target, y_send.at[index], y_recv.at[index], r.at[place])

    def c_copy(direction, step, part):
        place = (z_block(direction, step), chunk(direction, part))
        index = (direction, step // 2, part)
        send(away.at[place], (col, other), c_send.at[index], c_recv.at[index], r.at[place])

    def c_wait(direction, step, part):
        index = (direction, step // 2, part)
        arrived(r.at[z_block(direction, step), chunk(direction, part)], c_send.at[index], c_recv.at[index])

    def y_wait(direction, step, part):
        shift = 3 * QUARTER if part < PARTS // 2 else QUARTER
        ref = r.at[z_block(direction, step), chunk(direction, part, shift)]
        arrived(ref, y_send.at[direction, step - 1, part], y_recv.at[direction, step - 1, part])

    order = [lax.rem(part + (PARTS // 2) * ((Y - 1 - y) // (Y - 1)), PARTS) for part in range(PARTS)]
    for part in order:
        for direction in range(2):
            z_copy(direction, 1, part)

    acc_p[...] = low
    acc_m[...] = high

    @pl.when(y == 0)
    def _():
        acc_m[...] = mm(g[1], acc_m[...])

    @pl.when(y == 1)
    def _():
        acc_p[...] = g[0]

    @pl.when(y == 2)
    def _():
        acc_m[...] = g[3]

    @pl.when(y == 3)
    def _():
        acc_p[...] = mm(acc_p[...], g[2])

    @pl.when(y == 0)
    def _():
        acc_p[...] = (row == column).astype(F32)

    @pl.when(y == 3)
    def _():
        acc_m[...] = (row == column).astype(F32)

    def write_lefts(left0, left1):
        lout[0] = jnp.where(column < kept_ref[0, 0], left0, 0.0)
        lout[1] = jnp.where(column < kept_ref[0, 1], left1, 0.0)

    def take_blocks(step):
        for direction in range(2):
            for part in range(PARTS):
                if step % 2:
                    c_wait(direction, step, part)
                y_wait(direction, step, part)
        plus = z_block(0, step)
        minus = z_block(1, step)

        @pl.when(step <= z - step // 3)
        def _():
            acc_p[...] = mm(r[plus], acc_p[...])

        @pl.when(step == z + 1)
        def _():
            post[...] = r[plus]

        @pl.when(step > z + 1)
        def _():
            post[...] = mm(r[plus], post[...])

        @pl.when(step <= Z - 1 - z - step // 3)
        def _():
            acc_m[...] = mm(acc_m[...], r[minus])

        @pl.when(step == Z - z)
        def _():
            post[...] = r[minus]

        @pl.when(step > Z - z)
        def _():
            post[...] = mm(post[...], r[minus])

    for step in range(1, 4):
        for part in order:
            for direction in range(2):
                z_wait(direction, step, part)
                z_copy(direction, step + 1, part)
                y_copy(direction, step, part)
                if step % 2:
                    c_copy(direction, step, part)
        if step > 1:
            take_blocks(step - 1)

    @pl.when(z < 4)
    def _():
        x0 = acc_p[...]
        x1 = mm(x0, t[0])
        x2 = mm(x1, t[1])
        q[6] = x2
        factor[...] = x2
        for k in range(TERMS):
            q[k] = mm(x0, h[0, k])
            q[3 + k] = mm(x1, h[1, k])
        write_lefts(x0, x1)

    @pl.when(z >= 4)
    def _():
        x0 = acc_m[...]
        x1 = mm(t[1], x0)
        x2 = mm(t[0], x1)
        q[6] = x2
        factor[...] = x2
        for k in range(TERMS):
            q[k] = mm(h[0, k], x1)
            q[3 + k] = mm(h[1, k], x0)

    take_blocks(3)

    @pl.when(z == 3)
    def _():
        block = r[0]
        factor[...] = mm(block, mm(block, factor[...]), TN)

    @pl.when(z == 4)
    def _():
        block = r[Z - 1]
        factor[...] = mm(mm(factor[...], block), block, NT)

    for part in range(PARTS):
        for direction in range(2):
            z_wait(direction, 4, part)
    middle = lax.rem(z + 4, Z)

    @pl.when(z < 4)
    def _():
        acc_m[...] = mm(acc_m[...], r[middle])

    @pl.when(z < 3)
    def _():
        acc_m[...] = mm(acc_m[...], post[...])

    @pl.when(z >= 4)
    def _():
        acc_p[...] = mm(r[middle], acc_p[...])

    @pl.when(z > 4)
    def _():
        acc_p[...] = mm(post[...], acc_p[...])

    def lanes(x):
        x = jnp.sum(x, axis=0, keepdims=True)
        return x[:, :128] + x[:, 128:]

    def reduce(v):
        rows = [lanes(v * q[k]) for k in range(7)] + [jnp.zeros((1, 128), F32)]
        red[sec] = jnp.concatenate(rows, axis=0)

    @pl.when(z < 4)
    def _():
        gram = mm(acc_m[...], acc_m[...], NT)
        reduce(mm(factor[...], gram))

    @pl.when(z >= 4)
    def _():
        gram = mm(acc_p[...], acc_p[...], TN)
        reduce(mm(gram, factor[...]))

    for d in (4, 3, 5, 2, 6, 1, 7):
        send(red.at[sec], (col, lax.rem(sec + d, S)), s_send.at[d], s_recv.at[d])

    @pl.when(z == 3)
    def _():
        left0 = mm(r[0], acc_p[...])
        write_lefts(left0, mm(left0, t[0]))

    @pl.when(z >= 4)
    def _():
        write_lefts(acc_p[...], mm(acc_p[...], t[0]))

    for d in range(1, S):
        arrived(red.at[lax.rem(sec - d + S, S)], s_send.at[d], s_recv.at[d])
    total = red[0]
    for k in range(1, S):
        total = total + red[k]
    sums_ref[...] = total

    for copy in sends:
        copy.wait_send()


def finish(lefts, sums_ref, left_hbm, energy_ref, sems):
    stores = []
    for c in range(2):
        copy = pltpu.make_async_copy(lefts.at[c], left_hbm.at[c, 0], sems.at[c])
        copy.start()
        stores.append(copy)
    total = sums_ref[...]
    total = jnp.sum(total, axis=1, keepdims=True)
    values = (float(N * S) * total[0:6]) / total[6:7]
    place = 3 * lax.broadcasted_iota(jnp.int32, (2, 3), 0) + lax.broadcasted_iota(jnp.int32, (2, 3), 1)
    energy = jnp.zeros((2, 3), F32)
    for k in range(6):
        energy = jnp.where(place == k, values[k:k + 1], energy)
    energy_ref[...] = energy
    for copy in stores:
        copy.wait()


def per_device(transfer, hamiltonian, kept):
    dma = pltpu.SemaphoreType.DMA
    vmem = pl.BlockSpec(memory_space=pltpu.VMEM)
    lefts, sums = pl.pallas_call(
        kernel,
        name="chain",
        out_shape=(pltpu.VMEM((2, N, N), F32), pltpu.VMEM((8, 128), F32)),
        in_specs=[
            pl.BlockSpec(memory_space=pl.ANY),
            pl.BlockSpec(memory_space=pl.ANY),
            pl.BlockSpec(memory_space=pltpu.SMEM),
        ],
        out_specs=(vmem, vmem),
        scratch_shapes=[
            pltpu.VMEM((2, N, N), F32),
            pltpu.VMEM((2, TERMS, N, N), F32),
            pltpu.VMEM((Y, N, N), F32),
            pltpu.VMEM((Z, N, N), F32),
            pltpu.VMEM((Z, N, N), F32),
            *[pltpu.VMEM((N, N), F32)] * 4,
            pltpu.VMEM((7, N, N), F32),
            pltpu.VMEM((S, 8, 128), F32),
            dma((3,)),
            dma((2, 6)),
            dma((2, 6)),
            dma((2, 4, PARTS)),
            dma((2, 4, PARTS)),
            dma((2, 3, PARTS)),
            dma((2, 3, PARTS)),
            dma((2, 2, PARTS)),
            dma((2, 2, PARTS)),
            dma((S,)),
            dma((S,)),
        ],
        compiler_params=pltpu.CompilerParams(collective_id=0, has_side_effects=True),
    )(transfer, hamiltonian, kept.T)
    return pl.pallas_call(
        finish,
        name="finish",
        out_shape=(
            jax.ShapeDtypeStruct((2, 1, N, N), F32),
            jax.ShapeDtypeStruct((2, TERMS), F32),
        ),
        in_specs=[vmem, vmem],
        out_specs=(pl.BlockSpec(memory_space=pl.ANY), vmem),
        scratch_shapes=[dma((2,))],
    )(*(pltpu.with_memory_space_constraint(x, pltpu.VMEM) for x in (lefts, sums)))


def solution(mesh):
    in_specs = (P("col", "sec", None, None), P("col", None, "sec", None, None), P("col", "sec"))
    out_specs = (P("col", "sec", None, None), P("col", None))
    return jax.shard_map(
        per_device, mesh=mesh, in_specs=in_specs, out_specs=out_specs, check_vma=False
    )
```

```python
import jax
import jax.numpy as jnp
from jax import lax
from jax.experimental import pallas as pl
from jax.experimental.pallas import tpu as pltpu
from jax.sharding import PartitionSpec as P

MESH = pl.DeviceIdType.MESH
F32 = jnp.float32
BF16 = jnp.bfloat16
Y = 4
Z = 8
S = 8
N = 256
HALF = N // 2
QUARTER = N // 4
SIZES = ((64,), (40, 24))
PARTS = [(half, sum(sizes[:k]), sizes[k]) for half, sizes in enumerate(SIZES) for k in range(len(sizes))]
TERMS = 3
NN = (((1,), (0,)), ((), ()))
NT = (((1,), (1,)), ((), ()))
TN = (((0,), (0,)), ((), ()))


def split(x):
    high = x.astype(BF16)
    return high, (x - high.astype(F32)).astype(BF16)


def mm(a, b, dims=NN):
    ah, al = split(a)
    bh, bl = split(b)

    def dot(p, q):
        return lax.dot_general(p, q, dims, preferred_element_type=F32)

    return dot(ah, bh) + (dot(ah, bl) + dot(al, bh))


def kernel(
    t_hbm, h_hbm, kept_ref,
    lout, sums_ref,
    t, h, g, r, away, acc_p, acc_m, post, factor, q, red,
    load_sem, g_send, g_recv, z_send, z_recv, y_send, y_recv, c_send, c_recv, s_send, s_recv,
):
    col = lax.axis_index("col")
    sec = lax.axis_index("sec")
    y = lax.rem(col, Y)
    z = col // Y

    def at_y(d):
        return z * Y + lax.rem(y + d + Y, Y)

    def at_z(d):
        return lax.rem(z + d + Z, Z) * Y + y

    loads = []
    for c in range(2):
        loads.append(pltpu.make_async_copy(t_hbm.at[c, 0], t.at[c], load_sem.at[c]))
    loads.append(pltpu.make_async_copy(h_hbm.at[:, :, 0], h, load_sem.at[2]))
    loads[0].start()
    loads[1].start()

    barrier = pltpu.get_barrier_semaphore()
    other = sec + 1 - 2 * lax.rem(sec, 2)
    partners = [(at_y(1), sec), (at_y(-1), sec), (at_y(1), other), (at_y(-1), other)]
    partners += [(at_z(1), other), (at_z(-1), other)]
    partners += [(col, lax.rem(sec + d, S)) for d in range(1, S)]
    for partner in partners:
        pl.semaphore_signal(barrier, inc=1, device_id=partner, device_id_type=MESH)

    sends = []

    def send(ref, target, send_sem, recv_sem, to=None):
        copy = pltpu.make_async_remote_copy(
            src_ref=ref, dst_ref=ref if to is None else to, send_sem=send_sem, recv_sem=recv_sem,
            device_id=target, device_id_type=MESH,
        )
        copy.start()
        sends.append(copy)

    def arrived(ref, send_sem, recv_sem):
        pltpu.make_async_remote_copy(
            src_ref=ref, dst_ref=ref, send_sem=send_sem, recv_sem=recv_sem,
            device_id=(col, sec), device_id_type=MESH,
        ).wait_recv()

    top = pl.ds(0, HALF)
    bottom = pl.ds(HALF, HALF)
    loads[0].wait()
    loads[1].wait()
    loads[2].start()
    g[y, top] = mm(t[0, top], t[1])
    pl.semaphore_wait(barrier, len(partners))

    y_plus, y_minus = (at_y(1), sec), (at_y(-1), sec)
    z_plus, z_minus = (at_z(1), other), (at_z(-1), other)
    before, after, opposite = lax.rem(y + 3, Y), lax.rem(y + 1, Y), lax.rem(y + 2, Y)

    def g_rows(direction, index):
        part = (index + 2 * direction) % 4
        return pl.ds(part * QUARTER, QUARTER)

    def g_copy(direction, index, block):
        target = y_plus if direction == 0 else y_minus
        rows = g_rows(direction, index % 4)
        send(g.at[block, rows], target, g_send.at[direction, index], g_recv.at[direction, index])

    def g_wait(direction, index, block):
        rows = g_rows(direction, index % 4)
        arrived(g.at[block, rows], g_send.at[direction, index], g_recv.at[direction, index])

    g_copy(0, 0, y)
    g_copy(0, 1, y)
    g[y, bottom] = mm(t[0, bottom], t[1])
    for direction, index in ((1, 0), (1, 1), (0, 2), (1, 2), (0, 3), (1, 3)):
        g_copy(direction, index, y)

    loads[2].wait()
    row = lax.broadcasted_iota(jnp.int32, (N, N), 0)
    column = lax.broadcasted_iota(jnp.int32, (N, N), 1)
    for c in range(2):
        kept = row < kept_ref[0, c]
        for k in range(TERMS):
            h[c, k] = jnp.where(kept, h[c, k], 0.0)
    for k in range(TERMS):

        @pl.when(z < 4)
        def _():
            h[0, k] = mm(h[0, k], t[1])

        @pl.when(z >= 4)
        def _():
            h[1, k] = mm(t[0], h[1, k])

    neighbours = (before, after)
    for index in range(2):
        for direction in range(2):
            g_wait(direction, index, neighbours[direction])
            g_copy(direction, index + 4, neighbours[direction])
    for index in range(2, 4):
        for direction in range(2):
            g_wait(direction, index, neighbours[direction])

    @pl.when(y < 2)
    def _():
        acc_p[...] = mm(g[0], g[1])

    @pl.when(y >= 2)
    def _():
        acc_m[...] = mm(g[2], g[3])

    for index in range(4, 6):
        for direction in range(2):
            g_wait(direction, index, opposite)

    @pl.when(y < 2)
    def _():
        acc_m[...] = mm(g[2], g[3])

    @pl.when(y >= 2)
    def _():
        acc_p[...] = mm(g[0], g[1])

    r[z] = mm(acc_p[...], acc_m[...])

    flip = (Y - 1 - y) // (Y - 1)

    def rows_at(start, size):
        return pl.ds(pl.multiple_of(lax.rem(y * QUARTER + start, N), 8), size)

    def chunk(direction, part):
        half, offset, size = PARTS[part]
        return rows_at(direction * HALF + lax.rem(half + flip, 2) * QUARTER + offset, size)

    def z_block(direction, step):
        return lax.rem(z - step + Z, Z) if direction == 0 else lax.rem(z + step, Z)

    def z_copy(direction, step, part):
        place = (z_block(direction, step - 1), chunk(direction, part))
        target = z_plus if direction == 0 else z_minus
        here, there = (r, away) if step % 2 else (away, r)
        index = (direction, step - 1, part)
        send(here.at[place], target, z_send.at[index], z_recv.at[index], there.at[place])

    def z_wait(direction, step, part):
        ref = (away if step % 2 else r).at[z_block(direction, step), chunk(direction, part)]
        index = (direction, step - 1, part)
        arrived(ref, z_send.at[index], z_recv.at[index])

    def y_copy(direction, step, part):
        place = (z_block(direction, step), chunk(direction, part))
        owner = other if step % 2 else sec
        quarter = lax.rem(PARTS[part][0] + flip, 2)
        target = (at_y(1 - 2 * quarter), owner)
        here = away if step % 2 else r
        send(here.at[place], target, y_send.at[direction, step - 1, part], y_recv.at[direction, step - 1, quarter], r.at[place])

    def quarter_rows(direction, half):
        return rows_at(direction * HALF + lax.rem(half + flip, 2) * QUARTER, QUARTER)

    def c_copy(direction, step, half):
        place = (z_block(direction, step), quarter_rows(direction, half))
        index = (direction, step // 2, half)
        send(away.at[place], (col, other), c_send.at[index], c_recv.at[index], r.at[place])

    def c_wait(direction, step, half):
        index = (direction, step // 2, half)
        arrived(r.at[z_block(direction, step), quarter_rows(direction, half)], c_send.at[index], c_recv.at[index])

    def y_wait(direction, step, quarter):
        rows = rows_at(direction * HALF + (3 - quarter) * QUARTER, QUARTER)
        index = (direction, step - 1, quarter)
        arrived(r.at[z_block(direction, step), rows], y_send.at[direction, step - 1, 0], y_recv.at[index])

    for part in range(len(PARTS)):
        for direction in range(2):
            z_copy(direction, 1, part)

    @pl.when(y == 0)
    def _():
        acc_m[...] = mm(g[1], acc_m[...])

    @pl.when(y == 1)
    def _():
        acc_p[...] = g[0]

    @pl.when(y == 2)
    def _():
        acc_m[...] = g[3]

    @pl.when(y == 3)
    def _():
        acc_p[...] = mm(acc_p[...], g[2])

    @pl.when(y == 0)
    def _():
        acc_p[...] = (row == column).astype(F32)

    @pl.when(y == 3)
    def _():
        acc_m[...] = (row == column).astype(F32)

    def write_lefts(left0, left1):
        lout[0] = jnp.where(column < kept_ref[0, 0], left0, 0.0)
        lout[1] = jnp.where(column < kept_ref[0, 1], left1, 0.0)

    def take_blocks(step):
        for direction in range(2):
            if step % 2:
                for half in range(2):
                    c_wait(direction, step, half)
            for quarter in range(2):
                y_wait(direction, step, quarter)
        plus = z_block(0, step)
        minus = z_block(1, step)

        @pl.when(step <= z - step // 3)
        def _():
            acc_p[...] = mm(r[plus], acc_p[...])

        @pl.when(step == z + 1)
        def _():
            post[...] = r[plus]

        @pl.when(step > z + 1)
        def _():
            post[...] = mm(r[plus], post[...])

        @pl.when(step <= Z - 1 - z - step // 3)
        def _():
            acc_m[...] = mm(acc_m[...], r[minus])

        @pl.when(step == Z - z)
        def _():
            post[...] = r[minus]

        @pl.when(step > Z - z)
        def _():
            post[...] = mm(post[...], r[minus])

    for step in range(1, 4):
        for part in range(len(PARTS)):
            for direction in range(2):
                z_wait(direction, step, part)
                z_copy(direction, step + 1, part)
                y_copy(direction, step, part)
                if step % 2 and sum(PARTS[part][1:]) == QUARTER:
                    c_copy(direction, step, PARTS[part][0])
        if step > 1:
            take_blocks(step - 1)

    @pl.when(z < 4)
    def _():
        x0 = acc_p[...]
        x1 = mm(x0, t[0])
        x2 = mm(x1, t[1])
        q[6] = x2
        factor[...] = x2
        for k in range(TERMS):
            q[k] = mm(x0, h[0, k])
            q[3 + k] = mm(x1, h[1, k])
        write_lefts(x0, x1)

    @pl.when(z >= 4)
    def _():
        x0 = acc_m[...]
        x1 = mm(t[1], x0)
        x2 = mm(t[0], x1)
        q[6] = x2
        factor[...] = x2
        for k in range(TERMS):
            q[k] = mm(h[0, k], x1)
            q[3 + k] = mm(h[1, k], x0)

    take_blocks(3)

    @pl.when(z == 3)
    def _():
        block = r[0]
        factor[...] = mm(block, mm(block, factor[...]), TN)

    @pl.when(z == 4)
    def _():
        block = r[Z - 1]
        factor[...] = mm(mm(factor[...], block), block, NT)

    for part in range(len(PARTS)):
        for direction in range(2):
            z_wait(direction, 4, part)
    middle = lax.rem(z + 4, Z)

    @pl.when(z < 4)
    def _():
        acc_m[...] = mm(acc_m[...], r[middle])

    @pl.when(z < 3)
    def _():
        acc_m[...] = mm(acc_m[...], post[...])

    @pl.when(z >= 4)
    def _():
        acc_p[...] = mm(r[middle], acc_p[...])

    @pl.when(z > 4)
    def _():
        acc_p[...] = mm(post[...], acc_p[...])

    def lanes(x):
        x = jnp.sum(x, axis=0, keepdims=True)
        return x[:, :128] + x[:, 128:]

    def reduce(v):
        rows = [lanes(v * q[k]) for k in range(7)] + [jnp.zeros((1, 128), F32)]
        red[sec] = jnp.concatenate(rows, axis=0)

    @pl.when(z < 4)
    def _():
        gram = mm(acc_m[...], acc_m[...], NT)
        reduce(mm(factor[...], gram))

    @pl.when(z >= 4)
    def _():
        gram = mm(acc_p[...], acc_p[...], TN)
        reduce(mm(gram, factor[...]))

    for d in (4, 3, 5, 2, 6, 1, 7):
        send(red.at[sec], (col, lax.rem(sec + d, S)), s_send.at[d], s_recv.at[d])

    @pl.when(z == 3)
    def _():
        left0 = mm(r[0], acc_p[...])
        write_lefts(left0, mm(left0, t[0]))

    @pl.when(z >= 4)
    def _():
        write_lefts(acc_p[...], mm(acc_p[...], t[0]))

    for d in range(1, S):
        arrived(red.at[lax.rem(sec - d + S, S)], s_send.at[d], s_recv.at[d])
    total = red[0]
    for k in range(1, S):
        total = total + red[k]
    sums_ref[...] = total

    for copy in sends:
        copy.wait_send()


def finish(lefts, sums_ref, left_hbm, energy_ref, sems):
    stores = []
    for c in range(2):
        copy = pltpu.make_async_copy(lefts.at[c], left_hbm.at[c, 0], sems.at[c])
        copy.start()
        stores.append(copy)
    total = sums_ref[...]
    total = jnp.sum(total, axis=1, keepdims=True)
    values = (float(N * S) * total[0:6]) / total[6:7]
    place = 3 * lax.broadcasted_iota(jnp.int32, (2, 3), 0) + lax.broadcasted_iota(jnp.int32, (2, 3), 1)
    energy = jnp.zeros((2, 3), F32)
    for k in range(6):
        energy = jnp.where(place == k, values[k:k + 1], energy)
    energy_ref[...] = energy
    for copy in stores:
        copy.wait()


def per_device(transfer, hamiltonian, kept):
    dma = pltpu.SemaphoreType.DMA
    vmem = pl.BlockSpec(memory_space=pltpu.VMEM)
    lefts, sums = pl.pallas_call(
        kernel,
        name="chain",
        out_shape=(pltpu.VMEM((2, N, N), F32), pltpu.VMEM((8, 128), F32)),
        in_specs=[
            pl.BlockSpec(memory_space=pl.ANY),
            pl.BlockSpec(memory_space=pl.ANY),
            pl.BlockSpec(memory_space=pltpu.SMEM),
        ],
        out_specs=(vmem, vmem),
        scratch_shapes=[
            pltpu.VMEM((2, N, N), F32),
            pltpu.VMEM((2, TERMS, N, N), F32),
            pltpu.VMEM((Y, N, N), F32),
            pltpu.VMEM((Z, N, N), F32),
            pltpu.VMEM((Z, N, N), F32),
            *[pltpu.VMEM((N, N), F32)] * 4,
            pltpu.VMEM((7, N, N), F32),
            pltpu.VMEM((S, 8, 128), F32),
            dma((3,)),
            dma((2, 6)),
            dma((2, 6)),
            dma((2, 4, len(PARTS))),
            dma((2, 4, len(PARTS))),
            dma((2, 3, len(PARTS))),
            dma((2, 3, 2)),
            dma((2, 2, len(PARTS))),
            dma((2, 2, len(PARTS))),
            dma((S,)),
            dma((S,)),
        ],
        compiler_params=pltpu.CompilerParams(collective_id=0, has_side_effects=True),
    )(transfer, hamiltonian, kept.T)
    return pl.pallas_call(
        finish,
        name="finish",
        out_shape=(
            jax.ShapeDtypeStruct((2, 1, N, N), F32),
            jax.ShapeDtypeStruct((2, TERMS), F32),
        ),
        in_specs=[vmem, vmem],
        out_specs=(pl.BlockSpec(memory_space=pl.ANY), vmem),
        scratch_shapes=[dma((2,))],
    )(*(pltpu.with_memory_space_constraint(x, pltpu.VMEM) for x in (lefts, sums)))


def solution(mesh):
    in_specs = (P("col", "sec", None, None), P("col", None, "sec", None, None), P("col", "sec"))
    out_specs = (P("col", "sec", None, None), P("col", None))
    return jax.shard_map(
        per_device, mesh=mesh, in_specs=in_specs, out_specs=out_specs, check_vma=False
    )
```

```python
import jax
import jax.numpy as jnp
from jax import lax
from jax.experimental import pallas as pl
from jax.experimental.pallas import tpu as pltpu
from jax.sharding import PartitionSpec as P

MESH = pl.DeviceIdType.MESH
F32 = jnp.float32
BF16 = jnp.bfloat16
Y = 4
Z = 8
S = 8
N = 256
HALF = N // 2
QUARTER = N // 4
BASE = 104
CUTS = ((0, BASE), (BASE, N - 2 * BASE), (N - BASE, BASE))
SIZES = ((64,), (40, 24))
PARTS = [(half, sum(sizes[:k]), sizes[k]) for half, sizes in enumerate(SIZES) for k in range(len(sizes))]
TERMS = 3
NN = (((1,), (0,)), ((), ()))
NT = (((1,), (1,)), ((), ()))
TN = (((0,), (0,)), ((), ()))


def split(x):
    high = x.astype(BF16)
    return high, (x - high.astype(F32)).astype(BF16)


def mm(a, b, dims=NN):
    ah, al = split(a)
    bh, bl = split(b)

    def dot(p, q):
        return lax.dot_general(p, q, dims, preferred_element_type=F32)

    return dot(ah, bh) + (dot(ah, bl) + dot(al, bh))


def kernel(
    t_hbm, h_hbm, kept_ref,
    lout, sums_ref,
    t, h, g, r, away, acc_p, acc_m, post, factor, q, red,
    load_sem, g_send, g_recv, z_send, z_recv, y_send, y_recv, c_send, c_recv, s_send, s_recv,
):
    col = lax.axis_index("col")
    sec = lax.axis_index("sec")
    y = lax.rem(col, Y)
    z = col // Y

    def at_y(d):
        return z * Y + lax.rem(y + d + Y, Y)

    def at_z(d):
        return lax.rem(z + d + Z, Z) * Y + y

    loads = []
    for c in range(2):
        loads.append(pltpu.make_async_copy(t_hbm.at[c, 0], t.at[c], load_sem.at[c]))
    loads.append(pltpu.make_async_copy(h_hbm.at[:, :, 0], h, load_sem.at[2]))
    loads[0].start()
    loads[1].start()

    barrier = pltpu.get_barrier_semaphore()
    other = sec + 1 - 2 * lax.rem(sec, 2)
    partners = [(at_y(1), sec), (at_y(-1), sec), (at_y(1), other), (at_y(-1), other)]
    partners += [(at_z(1), other), (at_z(-1), other)]
    partners += [(col, lax.rem(sec + d, S)) for d in range(1, S)]
    for partner in partners:
        pl.semaphore_signal(barrier, inc=1, device_id=partner, device_id_type=MESH)

    sends = []

    def send(ref, target, send_sem, recv_sem, to=None):
        copy = pltpu.make_async_remote_copy(
            src_ref=ref, dst_ref=ref if to is None else to, send_sem=send_sem, recv_sem=recv_sem,
            device_id=target, device_id_type=MESH,
        )
        copy.start()
        sends.append(copy)

    def arrived(ref, send_sem, recv_sem):
        pltpu.make_async_remote_copy(
            src_ref=ref, dst_ref=ref, send_sem=send_sem, recv_sem=recv_sem,
            device_id=(col, sec), device_id_type=MESH,
        ).wait_recv()

    top = pl.ds(0, HALF)
    bottom = pl.ds(HALF, HALF)
    loads[0].wait()
    loads[1].wait()
    loads[2].start()
    g[y, top] = mm(t[0, top], t[1])
    pl.semaphore_wait(barrier, len(partners))

    y_plus, y_minus = (at_y(1), sec), (at_y(-1), sec)
    z_plus, z_minus = (at_z(1), other), (at_z(-1), other)
    before, after, opposite = lax.rem(y + 3, Y), lax.rem(y + 1, Y), lax.rem(y + 2, Y)

    def g_rows(direction, index):
        start, size = CUTS[index if direction == 0 else 2 - index]
        return pl.ds(start, size)

    def g_copy(direction, index, block):
        target = y_plus if direction == 0 else y_minus
        rows = g_rows(direction, index % 3)
        send(g.at[block, rows], target, g_send.at[direction, index], g_recv.at[direction, index])

    def g_wait(direction, index, block):
        rows = g_rows(direction, index % 3)
        arrived(g.at[block, rows], g_send.at[direction, index], g_recv.at[direction, index])

    g_copy(0, 0, y)
    g[y, bottom] = mm(t[0, bottom], t[1])
    for direction, index in ((1, 0), (0, 1), (1, 1), (0, 2), (1, 2)):
        g_copy(direction, index, y)

    loads[2].wait()
    row = lax.broadcasted_iota(jnp.int32, (N, N), 0)
    column = lax.broadcasted_iota(jnp.int32, (N, N), 1)
    for c in range(2):
        kept = row < kept_ref[0, c]
        for k in range(TERMS):
            h[c, k] = jnp.where(kept, h[c, k], 0.0)
    for k in range(TERMS):

        @pl.when(z < 4)
        def _():
            h[0, k] = mm(h[0, k], t[1])

        @pl.when(z >= 4)
        def _():
            h[1, k] = mm(t[0], h[1, k])

    neighbours = (before, after)
    inside = lax.rem(y, Y - 1) != 0
    for direction in range(2):
        g_wait(direction, 0, neighbours[direction])
        g_copy(direction, 3, neighbours[direction])
    for direction in range(2):
        g_wait(direction, 1, neighbours[direction])

    @pl.when(inside)
    def _():
        for direction in range(2):
            g_copy(direction, 4, neighbours[direction])
            sends.pop()

    for direction in range(2):
        g_wait(direction, 2, neighbours[direction])

    @pl.when(y < 2)
    def _():
        acc_p[...] = mm(g[0], g[1])

    @pl.when(y >= 2)
    def _():
        acc_m[...] = mm(g[2], g[3])

    for direction in range(2):
        g_wait(direction, 3, opposite)

    @pl.when(y < 2)
    def _():
        g_wait(1, 4, opposite)

    @pl.when(y >= 2)
    def _():
        g_wait(0, 4, opposite)

    @pl.when(y < 2)
    def _():
        acc_m[...] = mm(g[2], g[3])

    @pl.when(y >= 2)
    def _():
        acc_p[...] = mm(g[0], g[1])

    r[z] = mm(acc_p[...], acc_m[...])

    flip = (Y - 1 - y) // (Y - 1)

    def rows_at(start, size):
        return pl.ds(pl.multiple_of(lax.rem(y * QUARTER + start, N), 8), size)

    def chunk(direction, part):
        half, offset, size = PARTS[part]
        return rows_at(direction * HALF + lax.rem(half + flip, 2) * QUARTER + offset, size)

    def z_block(direction, step):
        return lax.rem(z - step + Z, Z) if direction == 0 else lax.rem(z + step, Z)

    def z_copy(direction, step, part):
        place = (z_block(direction, step - 1), chunk(direction, part))
        target = z_plus if direction == 0 else z_minus
        here, there = (r, away) if step % 2 else (away, r)
        index = (direction, step - 1, part)
        send(here.at[place], target, z_send.at[index], z_recv.at[index], there.at[place])

    def z_wait(direction, step, part):
        ref = (away if step % 2 else r).at[z_block(direction, step), chunk(direction, part)]
        index = (direction, step - 1, part)
        arrived(ref, z_send.at[index], z_recv.at[index])

    def y_copy(direction, step, part):
        place = (z_block(direction, step), chunk(direction, part))
        owner = other if step % 2 else sec
        quarter = lax.rem(PARTS[part][0] + flip, 2)
        target = (at_y(1 - 2 * quarter), owner)
        here = away if step % 2 else r
        send(here.at[place], target, y_send.at[direction, step - 1, part], y_recv.at[direction, step - 1, quarter], r.at[place])

    def quarter_rows(direction, half):
        return rows_at(direction * HALF + lax.rem(half + flip, 2) * QUARTER, QUARTER)

    def c_copy(direction, step, half):
        place = (z_block(direction, step), quarter_rows(direction, half))
        index = (direction, step // 2, half)
        send(away.at[place], (col, other), c_send.at[index], c_recv.at[index], r.at[place])

    def c_wait(direction, step, half):
        index = (direction, step // 2, half)
        arrived(r.at[z_block(direction, step), quarter_rows(direction, half)], c_send.at[index], c_recv.at[index])

    def y_wait(direction, step, quarter):
        rows = rows_at(direction * HALF + (3 - quarter) * QUARTER, QUARTER)
        index = (direction, step - 1, quarter)
        arrived(r.at[z_block(direction, step), rows], y_send.at[direction, step - 1, 0], y_recv.at[index])

    for part in range(len(PARTS)):
        for direction in range(2):
            z_copy(direction, 1, part)

    @pl.when(y == 0)
    def _():
        acc_m[...] = mm(g[1], acc_m[...])

    @pl.when(y == 1)
    def _():
        acc_p[...] = g[0]

    @pl.when(y == 2)
    def _():
        acc_m[...] = g[3]

    @pl.when(y == 3)
    def _():
        acc_p[...] = mm(acc_p[...], g[2])

    @pl.when(y == 0)
    def _():
        acc_p[...] = (row == column).astype(F32)

    @pl.when(y == 3)
    def _():
        acc_m[...] = (row == column).astype(F32)

    def write_lefts(left0, left1):
        lout[0] = jnp.where(column < kept_ref[0, 0], left0, 0.0)
        lout[1] = jnp.where(column < kept_ref[0, 1], left1, 0.0)

    def take_blocks(step):
        for direction in range(2):
            if step % 2:
                for half in range(2):
                    c_wait(direction, step, half)
            for quarter in range(2):
                y_wait(direction, step, quarter)
        plus = z_block(0, step)
        minus = z_block(1, step)

        @pl.when(step <= z - step // 3)
        def _():
            acc_p[...] = mm(r[plus], acc_p[...])

        @pl.when(step == z + 1)
        def _():
            post[...] = r[plus]

        @pl.when(step > z + 1)
        def _():
            post[...] = mm(r[plus], post[...])

        @pl.when(step <= Z - 1 - z - step // 3)
        def _():
            acc_m[...] = mm(acc_m[...], r[minus])

        @pl.when(step == Z - z)
        def _():
            post[...] = r[minus]

        @pl.when(step > Z - z)
        def _():
            post[...] = mm(post[...], r[minus])

    for step in range(1, 4):
        for part in range(len(PARTS)):
            for direction in range(2):
                z_wait(direction, step, part)
                z_copy(direction, step + 1, part)
                y_copy(direction, step, part)
                if step % 2 and sum(PARTS[part][1:]) == QUARTER:
                    c_copy(direction, step, PARTS[part][0])
        if step > 1:
            take_blocks(step - 1)

    @pl.when(z < 4)
    def _():
        x0 = acc_p[...]
        x1 = mm(x0, t[0])
        x2 = mm(x1, t[1])
        q[6] = x2
        factor[...] = x2
        for k in range(TERMS):
            q[k] = mm(x0, h[0, k])
            q[3 + k] = mm(x1, h[1, k])
        write_lefts(x0, x1)

    @pl.when(z >= 4)
    def _():
        x0 = acc_m[...]
        x1 = mm(t[1], x0)
        x2 = mm(t[0], x1)
        q[6] = x2
        factor[...] = x2
        for k in range(TERMS):
            q[k] = mm(h[0, k], x1)
            q[3 + k] = mm(h[1, k], x0)

    take_blocks(3)

    @pl.when(z == 3)
    def _():
        block = r[0]
        factor[...] = mm(block, mm(block, factor[...]), TN)

    @pl.when(z == 4)
    def _():
        block = r[Z - 1]
        factor[...] = mm(mm(factor[...], block), block, NT)

    for part in range(len(PARTS)):
        for direction in range(2):
            z_wait(direction, 4, part)
    middle = lax.rem(z + 4, Z)

    @pl.when(z < 4)
    def _():
        acc_m[...] = mm(acc_m[...], r[middle])

    @pl.when(z < 3)
    def _():
        acc_m[...] = mm(acc_m[...], post[...])

    @pl.when(z >= 4)
    def _():
        acc_p[...] = mm(r[middle], acc_p[...])

    @pl.when(z > 4)
    def _():
        acc_p[...] = mm(post[...], acc_p[...])

    def lanes(x):
        x = jnp.sum(x, axis=0, keepdims=True)
        return x[:, :128] + x[:, 128:]

    def reduce(v):
        rows = [lanes(v * q[k]) for k in range(7)] + [jnp.zeros((1, 128), F32)]
        red[sec] = jnp.concatenate(rows, axis=0)

    @pl.when(z < 4)
    def _():
        gram = mm(acc_m[...], acc_m[...], NT)
        reduce(mm(factor[...], gram))

    @pl.when(z >= 4)
    def _():
        gram = mm(acc_p[...], acc_p[...], TN)
        reduce(mm(gram, factor[...]))

    for d in (4, 3, 5, 2, 6, 1, 7):
        send(red.at[sec], (col, lax.rem(sec + d, S)), s_send.at[d], s_recv.at[d])

    @pl.when(z == 3)
    def _():
        left0 = mm(r[0], acc_p[...])
        write_lefts(left0, mm(left0, t[0]))

    @pl.when(z >= 4)
    def _():
        write_lefts(acc_p[...], mm(acc_p[...], t[0]))

    for d in range(1, S):
        arrived(red.at[lax.rem(sec - d + S, S)], s_send.at[d], s_recv.at[d])
    total = red[0]
    for k in range(1, S):
        total = total + red[k]
    sums_ref[...] = total

    for copy in sends:
        copy.wait_send()

    @pl.when(inside)
    def _():
        for direction in range(2):
            ref = g.at[neighbours[direction], g_rows(direction, 1)]
            pltpu.make_async_remote_copy(
                src_ref=ref, dst_ref=ref, send_sem=g_send.at[direction, 4], recv_sem=g_recv.at[direction, 4],
                device_id=y_plus, device_id_type=MESH,
            ).wait_send()


def finish(lefts, sums_ref, left_hbm, energy_ref, sems):
    stores = []
    for c in range(2):
        copy = pltpu.make_async_copy(lefts.at[c], left_hbm.at[c, 0], sems.at[c])
        copy.start()
        stores.append(copy)
    total = sums_ref[...]
    total = jnp.sum(total, axis=1, keepdims=True)
    values = (float(N * S) * total[0:6]) / total[6:7]
    place = 3 * lax.broadcasted_iota(jnp.int32, (2, 3), 0) + lax.broadcasted_iota(jnp.int32, (2, 3), 1)
    energy = jnp.zeros((2, 3), F32)
    for k in range(6):
        energy = jnp.where(place == k, values[k:k + 1], energy)
    energy_ref[...] = energy
    for copy in stores:
        copy.wait()


def per_device(transfer, hamiltonian, kept):
    dma = pltpu.SemaphoreType.DMA
    vmem = pl.BlockSpec(memory_space=pltpu.VMEM)
    lefts, sums = pl.pallas_call(
        kernel,
        name="chain",
        out_shape=(pltpu.VMEM((2, N, N), F32), pltpu.VMEM((8, 128), F32)),
        in_specs=[
            pl.BlockSpec(memory_space=pl.ANY),
            pl.BlockSpec(memory_space=pl.ANY),
            pl.BlockSpec(memory_space=pltpu.SMEM),
        ],
        out_specs=(vmem, vmem),
        scratch_shapes=[
            pltpu.VMEM((2, N, N), F32),
            pltpu.VMEM((2, TERMS, N, N), F32),
            pltpu.VMEM((Y, N, N), F32),
            pltpu.VMEM((Z, N, N), F32),
            pltpu.VMEM((Z, N, N), F32),
            *[pltpu.VMEM((N, N), F32)] * 4,
            pltpu.VMEM((7, N, N), F32),
            pltpu.VMEM((S, 8, 128), F32),
            dma((3,)),
            dma((2, 5)),
            dma((2, 5)),
            dma((2, 4, len(PARTS))),
            dma((2, 4, len(PARTS))),
            dma((2, 3, len(PARTS))),
            dma((2, 3, 2)),
            dma((2, 2, len(PARTS))),
            dma((2, 2, len(PARTS))),
            dma((S,)),
            dma((S,)),
        ],
        compiler_params=pltpu.CompilerParams(collective_id=0, has_side_effects=True),
    )(transfer, hamiltonian, kept.T)
    return pl.pallas_call(
        finish,
        name="finish",
        out_shape=(
            jax.ShapeDtypeStruct((2, 1, N, N), F32),
            jax.ShapeDtypeStruct((2, TERMS), F32),
        ),
        in_specs=[vmem, vmem],
        out_specs=(pl.BlockSpec(memory_space=pl.ANY), vmem),
        scratch_shapes=[dma((2,))],
    )(*(pltpu.with_memory_space_constraint(x, pltpu.VMEM) for x in (lefts, sums)))


def solution(mesh):
    in_specs = (P("col", "sec", None, None), P("col", None, "sec", None, None), P("col", "sec"))
    out_specs = (P("col", "sec", None, None), P("col", None))
    return jax.shard_map(
        per_device, mesh=mesh, in_specs=in_specs, out_specs=out_specs, check_vma=False
    )
```

```python
import jax
import jax.numpy as jnp
from jax import lax
from jax.experimental import pallas as pl
from jax.experimental.pallas import tpu as pltpu
from jax.sharding import PartitionSpec as P

MESH = pl.DeviceIdType.MESH
F32 = jnp.float32
BF16 = jnp.bfloat16
Y = 4
Z = 8
S = 8
N = 256
HALF = N // 2
QUARTER = N // 4
BASE = 104
CUTS = ((0, BASE), (BASE, N - 2 * BASE), (N - BASE, BASE))
SIZES = ((64,), (40, 24))
PARTS = [(half, sum(sizes[:k]), sizes[k]) for half, sizes in enumerate(SIZES) for k in range(len(sizes))]
TERMS = 3
NN = (((1,), (0,)), ((), ()))
NT = (((1,), (1,)), ((), ()))
TN = (((0,), (0,)), ((), ()))


def split(x):
    high = x.astype(BF16)
    return high, (x - high.astype(F32)).astype(BF16)


def mm(a, b, dims=NN):
    ah, al = split(a)
    bh, bl = split(b)

    def dot(p, q):
        return lax.dot_general(p, q, dims, preferred_element_type=F32)

    return dot(ah, bh) + (dot(ah, bl) + dot(al, bh))


def kernel(
    t_hbm, h_hbm, kept_ref,
    lout, sums_ref,
    t, h, g, r, away, acc_p, acc_m, post, factor, q, red,
    load_sem, g_send, g_recv, z_send, z_recv, y_send, y_recv, c_send, c_recv, s_send, s_recv,
):
    col = lax.axis_index("col")
    sec = lax.axis_index("sec")
    y = lax.rem(col, Y)
    z = col // Y

    def at_y(d):
        return z * Y + lax.rem(y + d + Y, Y)

    def at_z(d):
        return lax.rem(z + d + Z, Z) * Y + y

    loads = []
    for c in range(2):
        loads.append(pltpu.make_async_copy(t_hbm.at[c, 0], t.at[c], load_sem.at[c]))
    loads.append(pltpu.make_async_copy(h_hbm.at[:, :, 0], h, load_sem.at[2]))
    loads[0].start()
    loads[1].start()

    barrier = pltpu.get_barrier_semaphore()
    other = sec + 1 - 2 * lax.rem(sec, 2)
    partners = [(at_y(1), sec), (at_y(-1), sec), (at_y(1), other), (at_y(-1), other)]
    partners += [(at_z(1), other), (at_z(-1), other)]
    partners += [(col, lax.rem(sec + d, S)) for d in range(1, S)]
    for partner in partners:
        pl.semaphore_signal(barrier, inc=1, device_id=partner, device_id_type=MESH)

    sends = []

    def send(ref, target, send_sem, recv_sem, to=None):
        copy = pltpu.make_async_remote_copy(
            src_ref=ref, dst_ref=ref if to is None else to, send_sem=send_sem, recv_sem=recv_sem,
            device_id=target, device_id_type=MESH,
        )
        copy.start()
        sends.append(copy)

    def arrived(ref, send_sem, recv_sem):
        pltpu.make_async_remote_copy(
            src_ref=ref, dst_ref=ref, send_sem=send_sem, recv_sem=recv_sem,
            device_id=(col, sec), device_id_type=MESH,
        ).wait_recv()

    top = pl.ds(0, HALF)
    bottom = pl.ds(HALF, HALF)
    loads[0].wait()
    loads[1].wait()
    loads[2].start()
    g[y, top] = mm(t[0, top], t[1])
    pl.semaphore_wait(barrier, len(partners))

    y_plus, y_minus = (at_y(1), sec), (at_y(-1), sec)
    z_plus, z_minus = (at_z(1), other), (at_z(-1), other)
    before, after, opposite = lax.rem(y + 3, Y), lax.rem(y + 1, Y), lax.rem(y + 2, Y)

    def g_rows(direction, index):
        start, size = CUTS[index if direction == 0 else 2 - index]
        return pl.ds(start, size)

    def g_copy(direction, index, block):
        target = y_plus if direction == 0 else y_minus
        rows = g_rows(direction, index % 3)
        send(g.at[block, rows], target, g_send.at[direction, index], g_recv.at[direction, index])

    def g_wait(direction, index, block):
        rows = g_rows(direction, index % 3)
        arrived(g.at[block, rows], g_send.at[direction, index], g_recv.at[direction, index])

    g_copy(0, 0, y)
    g[y, bottom] = mm(t[0, bottom], t[1])
    for direction, index in ((1, 0), (0, 1), (1, 1), (0, 2), (1, 2)):
        g_copy(direction, index, y)

    loads[2].wait()
    row = lax.broadcasted_iota(jnp.int32, (N, N), 0)
    column = lax.broadcasted_iota(jnp.int32, (N, N), 1)
    for c in range(2):
        kept = row < kept_ref[0, c]
        for k in range(TERMS):
            h[c, k] = jnp.where(kept, h[c, k], 0.0)
    for k in range(TERMS):

        @pl.when(z < 4)
        def _():
            h[0, k] = mm(h[0, k], t[1])

        @pl.when(z >= 4)
        def _():
            h[1, k] = mm(t[0], h[1, k])

    neighbours = (before, after)
    inside = lax.rem(y, Y - 1) != 0
    for direction in range(2):
        g_wait(direction, 0, neighbours[direction])
        g_copy(direction, 3, neighbours[direction])
    for direction in range(2):
        g_wait(direction, 1, neighbours[direction])

    @pl.when(inside)
    def _():
        for direction in range(2):
            g_copy(direction, 4, neighbours[direction])
            sends.pop()

    for direction in range(2):
        g_wait(direction, 2, neighbours[direction])

    @pl.when(y < 2)
    def _():
        acc_p[...] = mm(g[0], g[1])

    @pl.when(y >= 2)
    def _():
        acc_m[...] = mm(g[2], g[3])

    for direction in range(2):
        g_wait(direction, 3, opposite)

    @pl.when(y < 2)
    def _():
        g_wait(1, 4, opposite)

    @pl.when(y >= 2)
    def _():
        g_wait(0, 4, opposite)

    @pl.when(y < 2)
    def _():
        acc_m[...] = mm(g[2], g[3])

    @pl.when(y >= 2)
    def _():
        acc_p[...] = mm(g[0], g[1])

    r[z] = mm(acc_p[...], acc_m[...])

    flip = (Y - 1 - y) // (Y - 1)

    def rows_at(start, size):
        return pl.ds(pl.multiple_of(lax.rem(y * QUARTER + start, N), 8), size)

    def chunk(direction, part):
        half, offset, size = PARTS[part]
        return rows_at(direction * HALF + lax.rem(half + flip, 2) * QUARTER + offset, size)

    def z_block(direction, step):
        return lax.rem(z - step + Z, Z) if direction == 0 else lax.rem(z + step, Z)

    def z_copy(direction, step, part):
        place = (z_block(direction, step - 1), chunk(direction, part))
        target = z_plus if direction == 0 else z_minus
        here, there = (r, away) if step % 2 else (away, r)
        index = (direction, step - 1, part)
        send(here.at[place], target, z_send.at[index], z_recv.at[index], there.at[place])

    def z_wait(direction, step, part):
        ref = (away if step % 2 else r).at[z_block(direction, step), chunk(direction, part)]
        index = (direction, step - 1, part)
        arrived(ref, z_send.at[index], z_recv.at[index])

    def y_copy(direction, step, part):
        place = (z_block(direction, step), chunk(direction, part))
        owner = other if step % 2 else sec
        quarter = lax.rem(PARTS[part][0] + flip, 2)
        target = (at_y(1 - 2 * quarter), owner)
        here = away if step % 2 else r
        send(here.at[place], target, y_send.at[direction, step - 1, part], y_recv.at[direction, step - 1, quarter], r.at[place])

    def quarter_rows(direction, half):
        return rows_at(direction * HALF + lax.rem(half + flip, 2) * QUARTER, QUARTER)

    def c_copy(direction, step, half):
        place = (z_block(direction, step), quarter_rows(direction, half))
        index = (direction, step // 2, half)
        send(away.at[place], (col, other), c_send.at[index], c_recv.at[index], r.at[place])

    def c_wait(direction, step, half):
        index = (direction, step // 2, half)
        arrived(r.at[z_block(direction, step), quarter_rows(direction, half)], c_send.at[index], c_recv.at[index])

    def y_wait(direction, step, quarter):
        rows = rows_at(direction * HALF + (3 - quarter) * QUARTER, QUARTER)
        index = (direction, step - 1, quarter)
        arrived(r.at[z_block(direction, step), rows], y_send.at[direction, step - 1, 0], y_recv.at[index])

    for part in range(len(PARTS)):
        for direction in range(2):
            z_copy(direction, 1, part)

    @pl.when(y == 0)
    def _():
        acc_m[...] = mm(g[1], acc_m[...])

    @pl.when(y == 1)
    def _():
        acc_p[...] = g[0]

    @pl.when(y == 2)
    def _():
        acc_m[...] = g[3]

    @pl.when(y == 3)
    def _():
        acc_p[...] = mm(acc_p[...], g[2])

    @pl.when(y == 0)
    def _():
        acc_p[...] = (row == column).astype(F32)

    @pl.when(y == 3)
    def _():
        acc_m[...] = (row == column).astype(F32)

    def write_lefts(left0, left1):
        lout[0] = jnp.where(column < kept_ref[0, 0], left0, 0.0)
        lout[1] = jnp.where(column < kept_ref[0, 1], left1, 0.0)

    def take_blocks(step):
        for direction in range(2):
            if step % 2:
                for half in range(2):
                    c_wait(direction, step, half)
            for quarter in range(2):
                y_wait(direction, step, quarter)
        plus = z_block(0, step)
        minus = z_block(1, step)

        @pl.when(step <= z - step // 3)
        def _():
            acc_p[...] = mm(r[plus], acc_p[...])

        @pl.when(step == z + 1)
        def _():
            post[...] = r[plus]

        @pl.when(step > z + 1)
        def _():
            post[...] = mm(r[plus], post[...])

        @pl.when(step <= Z - 1 - z - step // 3)
        def _():
            acc_m[...] = mm(acc_m[...], r[minus])

        @pl.when(step == Z - z)
        def _():
            post[...] = r[minus]

        @pl.when(step > Z - z)
        def _():
            post[...] = mm(post[...], r[minus])

    for step in range(1, 4):
        for part in range(len(PARTS)):
            for direction in range(2):
                z_wait(direction, step, part)
                z_copy(direction, step + 1, part)
                y_copy(direction, step, part)
                if step % 2 and sum(PARTS[part][1:]) == QUARTER:
                    c_copy(direction, step, PARTS[part][0])
        if step == 3:
            take_blocks(1)
            take_blocks(2)

    @pl.when(z < 4)
    def _():
        x0 = acc_p[...]
        x1 = mm(x0, t[0])
        x2 = mm(x1, t[1])
        q[6] = x2
        factor[...] = x2
        for k in range(TERMS):
            q[k] = mm(x0, h[0, k])
            q[3 + k] = mm(x1, h[1, k])
        write_lefts(x0, x1)

    @pl.when(z >= 4)
    def _():
        x0 = acc_m[...]
        x1 = mm(t[1], x0)
        x2 = mm(t[0], x1)
        q[6] = x2
        factor[...] = x2
        for k in range(TERMS):
            q[k] = mm(h[0, k], x1)
            q[3 + k] = mm(h[1, k], x0)

    take_blocks(3)

    @pl.when(z == 3)
    def _():
        block = r[0]
        factor[...] = mm(block, mm(block, factor[...]), TN)

    @pl.when(z == 4)
    def _():
        block = r[Z - 1]
        factor[...] = mm(mm(factor[...], block), block, NT)

    for part in range(len(PARTS)):
        for direction in range(2):
            z_wait(direction, 4, part)
    middle = lax.rem(z + 4, Z)

    @pl.when(z < 4)
    def _():
        acc_m[...] = mm(acc_m[...], r[middle])

    @pl.when(z < 3)
    def _():
        acc_m[...] = mm(acc_m[...], post[...])

    @pl.when(z >= 4)
    def _():
        acc_p[...] = mm(r[middle], acc_p[...])

    @pl.when(z > 4)
    def _():
        acc_p[...] = mm(post[...], acc_p[...])

    def lanes(x):
        x = jnp.sum(x, axis=0, keepdims=True)
        return x[:, :128] + x[:, 128:]

    def reduce(v):
        rows = [lanes(v * q[k]) for k in range(7)] + [jnp.zeros((1, 128), F32)]
        red[sec] = jnp.concatenate(rows, axis=0)

    @pl.when(z < 4)
    def _():
        gram = mm(acc_m[...], acc_m[...], NT)
        reduce(mm(factor[...], gram))

    @pl.when(z >= 4)
    def _():
        gram = mm(acc_p[...], acc_p[...], TN)
        reduce(mm(gram, factor[...]))

    for d in (4, 3, 5, 2, 6, 1, 7):
        send(red.at[sec], (col, lax.rem(sec + d, S)), s_send.at[d], s_recv.at[d])

    @pl.when(z == 3)
    def _():
        left0 = mm(r[0], acc_p[...])
        write_lefts(left0, mm(left0, t[0]))

    @pl.when(z >= 4)
    def _():
        write_lefts(acc_p[...], mm(acc_p[...], t[0]))

    for d in range(1, S):
        arrived(red.at[lax.rem(sec - d + S, S)], s_send.at[d], s_recv.at[d])
    total = red[0]
    for k in range(1, S):
        total = total + red[k]
    sums_ref[...] = total

    for copy in sends:
        copy.wait_send()

    @pl.when(inside)
    def _():
        for direction in range(2):
            ref = g.at[neighbours[direction], g_rows(direction, 1)]
            pltpu.make_async_remote_copy(
                src_ref=ref, dst_ref=ref, send_sem=g_send.at[direction, 4], recv_sem=g_recv.at[direction, 4],
                device_id=y_plus, device_id_type=MESH,
            ).wait_send()


def finish(lefts, sums_ref, left_hbm, energy_ref, sems):
    stores = []
    for c in range(2):
        copy = pltpu.make_async_copy(lefts.at[c], left_hbm.at[c, 0], sems.at[c])
        copy.start()
        stores.append(copy)
    total = sums_ref[...]
    total = jnp.sum(total, axis=1, keepdims=True)
    values = (float(N * S) * total[0:6]) / total[6:7]
    place = 3 * lax.broadcasted_iota(jnp.int32, (2, 3), 0) + lax.broadcasted_iota(jnp.int32, (2, 3), 1)
    energy = jnp.zeros((2, 3), F32)
    for k in range(6):
        energy = jnp.where(place == k, values[k:k + 1], energy)
    energy_ref[...] = energy
    for copy in stores:
        copy.wait()


def per_device(transfer, hamiltonian, kept):
    dma = pltpu.SemaphoreType.DMA
    vmem = pl.BlockSpec(memory_space=pltpu.VMEM)
    lefts, sums = pl.pallas_call(
        kernel,
        name="chain",
        out_shape=(pltpu.VMEM((2, N, N), F32), pltpu.VMEM((8, 128), F32)),
        in_specs=[
            pl.BlockSpec(memory_space=pl.ANY),
            pl.BlockSpec(memory_space=pl.ANY),
            pl.BlockSpec(memory_space=pltpu.SMEM),
        ],
        out_specs=(vmem, vmem),
        scratch_shapes=[
            pltpu.VMEM((2, N, N), F32),
            pltpu.VMEM((2, TERMS, N, N), F32),
            pltpu.VMEM((Y, N, N), F32),
            pltpu.VMEM((Z, N, N), F32),
            pltpu.VMEM((Z, N, N), F32),
            *[pltpu.VMEM((N, N), F32)] * 4,
            pltpu.VMEM((7, N, N), F32),
            pltpu.VMEM((S, 8, 128), F32),
            dma((3,)),
            dma((2, 5)),
            dma((2, 5)),
            dma((2, 4, len(PARTS))),
            dma((2, 4, len(PARTS))),
            dma((2, 3, len(PARTS))),
            dma((2, 3, 2)),
            dma((2, 2, len(PARTS))),
            dma((2, 2, len(PARTS))),
            dma((S,)),
            dma((S,)),
        ],
        compiler_params=pltpu.CompilerParams(collective_id=0, has_side_effects=True),
    )(transfer, hamiltonian, kept.T)
    return pl.pallas_call(
        finish,
        name="finish",
        out_shape=(
            jax.ShapeDtypeStruct((2, 1, N, N), F32),
            jax.ShapeDtypeStruct((2, TERMS), F32),
        ),
        in_specs=[vmem, vmem],
        out_specs=(pl.BlockSpec(memory_space=pl.ANY), vmem),
        scratch_shapes=[dma((2,))],
    )(*(pltpu.with_memory_space_constraint(x, pltpu.VMEM) for x in (lefts, sums)))


def solution(mesh):
    in_specs = (P("col", "sec", None, None), P("col", None, "sec", None, None), P("col", "sec"))
    out_specs = (P("col", "sec", None, None), P("col", None))
    return jax.shard_map(
        per_device, mesh=mesh, in_specs=in_specs, out_specs=out_specs, check_vma=False
    )
```

```python
import jax
import jax.numpy as jnp
from jax import lax
from jax.experimental import pallas as pl
from jax.experimental.pallas import tpu as pltpu
from jax.sharding import PartitionSpec as P

MESH = pl.DeviceIdType.MESH
F32 = jnp.float32
BF16 = jnp.bfloat16
Y = 4
Z = 8
S = 8
N = 256
HALF = N // 2
QUARTER = N // 4
BASE = 104
CUTS = ((0, BASE), (BASE, N - 2 * BASE), (N - BASE, BASE))
SIZES = ((64,), (40, 24))
PARTS = [(half, sum(sizes[:k]), sizes[k]) for half, sizes in enumerate(SIZES) for k in range(len(sizes))]
TERMS = 3
NN = (((1,), (0,)), ((), ()))
NT = (((1,), (1,)), ((), ()))
TN = (((0,), (0,)), ((), ()))


def split(x):
    high = x.astype(BF16)
    return high, (x - high.astype(F32)).astype(BF16)


def mm(a, b, dims=NN):
    ah, al = split(a)
    bh, bl = split(b)

    def dot(p, q):
        return lax.dot_general(p, q, dims, preferred_element_type=F32)

    return dot(ah, bh) + (dot(ah, bl) + dot(al, bh))


def kernel(
    t_hbm, h_hbm, kept_ref,
    lout, sums_ref,
    t, h, g, r, away, acc_p, acc_m, post, factor, q, red,
    load_sem, g_send, g_recv, z_send, z_recv, y_send, y_recv, c_send, c_recv, s_send, s_recv,
):
    col = lax.axis_index("col")
    sec = lax.axis_index("sec")
    y = lax.rem(col, Y)
    z = col // Y

    def at_y(d):
        return z * Y + lax.rem(y + d + Y, Y)

    def at_z(d):
        return lax.rem(z + d + Z, Z) * Y + y

    loads = []
    for c in range(2):
        loads.append(pltpu.make_async_copy(t_hbm.at[c, 0], t.at[c], load_sem.at[c]))
    loads.append(pltpu.make_async_copy(h_hbm.at[:, :, 0], h, load_sem.at[2]))
    loads[0].start()
    loads[1].start()

    barrier = pltpu.get_barrier_semaphore()
    other = sec + 1 - 2 * lax.rem(sec, 2)
    partners = [(at_y(1), sec), (at_y(-1), sec), (at_y(1), other), (at_y(-1), other)]
    partners += [(at_z(1), other), (at_z(-1), other)]
    partners += [(col, lax.rem(sec + d, S)) for d in range(1, S)]
    for partner in partners:
        pl.semaphore_signal(barrier, inc=1, device_id=partner, device_id_type=MESH)

    sends = []

    def send(ref, target, send_sem, recv_sem, to=None):
        copy = pltpu.make_async_remote_copy(
            src_ref=ref, dst_ref=ref if to is None else to, send_sem=send_sem, recv_sem=recv_sem,
            device_id=target, device_id_type=MESH,
        )
        copy.start()
        sends.append(copy)

    def arrived(ref, send_sem, recv_sem):
        pltpu.make_async_remote_copy(
            src_ref=ref, dst_ref=ref, send_sem=send_sem, recv_sem=recv_sem,
            device_id=(col, sec), device_id_type=MESH,
        ).wait_recv()

    top = pl.ds(0, HALF)
    bottom = pl.ds(HALF, HALF)
    loads[0].wait()
    loads[1].wait()
    loads[2].start()
    g[y, top] = mm(t[0, top], t[1])
    pl.semaphore_wait(barrier, len(partners))

    y_plus, y_minus = (at_y(1), sec), (at_y(-1), sec)
    z_plus, z_minus = (at_z(1), other), (at_z(-1), other)
    before, after, opposite = lax.rem(y + 3, Y), lax.rem(y + 1, Y), lax.rem(y + 2, Y)

    def g_rows(direction, index):
        start, size = CUTS[index if direction == 0 else 2 - index]
        return pl.ds(start, size)

    def g_copy(direction, index, block):
        target = y_plus if direction == 0 else y_minus
        rows = g_rows(direction, index % 3)
        send(g.at[block, rows], target, g_send.at[direction, index], g_recv.at[direction, index])

    def g_wait(direction, index, block):
        rows = g_rows(direction, index % 3)
        arrived(g.at[block, rows], g_send.at[direction, index], g_recv.at[direction, index])

    g_copy(0, 0, y)
    g[y, bottom] = mm(t[0, bottom], t[1])
    for direction, index in ((1, 0), (0, 1), (1, 1), (0, 2), (1, 2)):
        g_copy(direction, index, y)

    loads[2].wait()
    row = lax.broadcasted_iota(jnp.int32, (N, N), 0)
    column = lax.broadcasted_iota(jnp.int32, (N, N), 1)
    for c in range(2):
        kept = row < kept_ref[0, c]
        for k in range(TERMS):
            h[c, k] = jnp.where(kept, h[c, k], 0.0)
    for k in range(TERMS):

        @pl.when(z < 4)
        def _():
            h[0, k] = mm(h[0, k], t[1])

        @pl.when(z >= 4)
        def _():
            h[1, k] = mm(t[0], h[1, k])

    neighbours = (before, after)
    inside = lax.rem(y, Y - 1) != 0
    for direction in range(2):
        g_wait(direction, 0, neighbours[direction])
        g_copy(direction, 3, neighbours[direction])
    for direction in range(2):
        g_wait(direction, 1, neighbours[direction])

    @pl.when(inside)
    def _():
        for direction in range(2):
            g_copy(direction, 4, neighbours[direction])
            sends.pop()

    for direction in range(2):
        g_wait(direction, 2, neighbours[direction])

    @pl.when(y < 2)
    def _():
        acc_p[...] = mm(g[0], g[1])

    @pl.when(y >= 2)
    def _():
        acc_m[...] = mm(g[2], g[3])

    for direction in range(2):
        g_wait(direction, 3, opposite)

    @pl.when(y < 2)
    def _():
        g_wait(1, 4, opposite)

    @pl.when(y >= 2)
    def _():
        g_wait(0, 4, opposite)

    @pl.when(y < 2)
    def _():
        acc_m[...] = mm(g[2], g[3])

    @pl.when(y >= 2)
    def _():
        acc_p[...] = mm(g[0], g[1])

    r[z] = mm(acc_p[...], acc_m[...])

    flip = (Y - 1 - y) // (Y - 1)

    def rows_at(start, size):
        return pl.ds(pl.multiple_of(lax.rem(y * QUARTER + start, N), 8), size)

    def chunk(direction, part):
        half, offset, size = PARTS[part]
        return rows_at(direction * HALF + lax.rem(half + flip, 2) * QUARTER + offset, size)

    def z_block(direction, step):
        return lax.rem(z - step + Z, Z) if direction == 0 else lax.rem(z + step, Z)

    def z_copy(direction, step, part):
        place = (z_block(direction, step - 1), chunk(direction, part))
        target = z_plus if direction == 0 else z_minus
        here, there = (r, away) if step % 2 else (away, r)
        index = (direction, step - 1, part)
        send(here.at[place], target, z_send.at[index], z_recv.at[index], there.at[place])

    def z_wait(direction, step, part):
        ref = (away if step % 2 else r).at[z_block(direction, step), chunk(direction, part)]
        index = (direction, step - 1, part)
        arrived(ref, z_send.at[index], z_recv.at[index])

    def y_copy(direction, step, part):
        place = (z_block(direction, step), chunk(direction, part))
        owner = other if step % 2 else sec
        quarter = lax.rem(PARTS[part][0] + flip, 2)
        target = (at_y(1 - 2 * quarter), owner)
        here = away if step % 2 else r
        send(here.at[place], target, y_send.at[direction, step - 1, part], y_recv.at[direction, step - 1, quarter], r.at[place])

    def quarter_rows(direction, half):
        return rows_at(direction * HALF + lax.rem(half + flip, 2) * QUARTER, QUARTER)

    def c_copy(direction, step, half):
        place = (z_block(direction, step), quarter_rows(direction, half))
        index = (direction, step // 2, half)
        send(away.at[place], (col, other), c_send.at[index], c_recv.at[index], r.at[place])

    def c_wait(direction, step, half):
        index = (direction, step // 2, half)
        arrived(r.at[z_block(direction, step), quarter_rows(direction, half)], c_send.at[index], c_recv.at[index])

    def y_wait(direction, step, quarter):
        rows = rows_at(direction * HALF + (3 - quarter) * QUARTER, QUARTER)
        index = (direction, step - 1, quarter)
        arrived(r.at[z_block(direction, step), rows], y_send.at[direction, step - 1, 0], y_recv.at[index])

    for part in range(len(PARTS)):
        for direction in range(2):
            z_copy(direction, 1, part)

    @pl.when(y == 0)
    def _():
        acc_m[...] = mm(g[1], acc_m[...])

    @pl.when(y == 1)
    def _():
        acc_p[...] = g[0]

    @pl.when(y == 2)
    def _():
        acc_m[...] = g[3]

    @pl.when(y == 3)
    def _():
        acc_p[...] = mm(acc_p[...], g[2])

    @pl.when(y == 0)
    def _():
        acc_p[...] = (row == column).astype(F32)

    @pl.when(y == 3)
    def _():
        acc_m[...] = (row == column).astype(F32)

    def write_lefts(left0, left1):
        lout[0] = jnp.where(column < kept_ref[0, 0], left0, 0.0)
        lout[1] = jnp.where(column < kept_ref[0, 1], left1, 0.0)

    def take_blocks(step):
        for direction in range(2):
            if step % 2:
                for half in range(2):
                    c_wait(direction, step, half)
            for quarter in range(2):
                y_wait(direction, step, quarter)
        plus = z_block(0, step)
        minus = z_block(1, step)

        @pl.when(step <= z - step // 3)
        def _():
            acc_p[...] = mm(r[plus], acc_p[...])

        @pl.when(step == z + 1)
        def _():
            post[...] = r[plus]

        @pl.when(step > z + 1)
        def _():
            post[...] = mm(r[plus], post[...])

        @pl.when(step <= Z - 1 - z - step // 3)
        def _():
            acc_m[...] = mm(acc_m[...], r[minus])

        @pl.when(step == Z - z)
        def _():
            post[...] = r[minus]

        @pl.when(step > Z - z)
        def _():
            post[...] = mm(post[...], r[minus])

    for step in range(1, 4):
        for part in range(len(PARTS)):
            for direction in range(2):
                z_wait(direction, step, part)
                z_copy(direction, step + 1, part)
                y_copy(direction, step, part)
                if step % 2 and sum(PARTS[part][1:]) == QUARTER:
                    c_copy(direction, step, PARTS[part][0])
        if step > 1:
            take_blocks(step - 1)

    @pl.when(z < 4)
    def _():
        x0 = acc_p[...]
        x1 = mm(x0, t[0])
        x2 = mm(x1, t[1])
        q[6] = x2
        factor[...] = x2
        for k in range(TERMS):
            q[k] = mm(x0, h[0, k])
            q[3 + k] = mm(x1, h[1, k])
        write_lefts(x0, x1)

    @pl.when(z >= 4)
    def _():
        x0 = acc_m[...]
        x1 = mm(t[1], x0)
        x2 = mm(t[0], x1)
        q[6] = x2
        factor[...] = x2
        for k in range(TERMS):
            q[k] = mm(h[0, k], x1)
            q[3 + k] = mm(h[1, k], x0)

    take_blocks(3)

    @pl.when(z == 3)
    def _():
        block = r[0]
        factor[...] = mm(block, mm(block, factor[...]), TN)

    @pl.when(z == 4)
    def _():
        block = r[Z - 1]
        factor[...] = mm(mm(factor[...], block), block, NT)

    for part in range(len(PARTS)):
        for direction in range(2):
            z_wait(direction, 4, part)
    middle = lax.rem(z + 4, Z)

    @pl.when(z < 4)
    def _():
        acc_m[...] = mm(acc_m[...], r[middle])

    @pl.when(z < 3)
    def _():
        acc_m[...] = mm(acc_m[...], post[...])

    @pl.when(z >= 4)
    def _():
        acc_p[...] = mm(r[middle], acc_p[...])

    @pl.when(z > 4)
    def _():
        acc_p[...] = mm(post[...], acc_p[...])

    def lanes(x):
        x = jnp.sum(x, axis=0, keepdims=True)
        return x[:, :128] + x[:, 128:]

    def reduce(v):
        rows = [lanes(v * q[k]) for k in range(7)] + [jnp.zeros((1, 128), F32)]
        red[sec] = jnp.concatenate(rows, axis=0)

    @pl.when(z < 4)
    def _():
        gram = mm(acc_m[...], acc_m[...], NT)
        reduce(mm(factor[...], gram))

    @pl.when(z >= 4)
    def _():
        gram = mm(acc_p[...], acc_p[...], TN)
        reduce(mm(gram, factor[...]))

    for d in (4, 3, 5, 2, 6, 1, 7):
        send(red.at[sec], (col, lax.rem(sec + d, S)), s_send.at[d], s_recv.at[d])

    @pl.when(z == 3)
    def _():
        left0 = mm(r[0], acc_p[...])
        write_lefts(left0, mm(left0, t[0]))

    @pl.when(z >= 4)
    def _():
        write_lefts(acc_p[...], mm(acc_p[...], t[0]))

    for copy in sends:
        copy.wait_send()

    @pl.when(inside)
    def _():
        for direction in range(2):
            ref = g.at[neighbours[direction], g_rows(direction, 1)]
            pltpu.make_async_remote_copy(
                src_ref=ref, dst_ref=ref, send_sem=g_send.at[direction, 4], recv_sem=g_recv.at[direction, 4],
                device_id=y_plus, device_id_type=MESH,
            ).wait_send()

    for d in range(1, S):
        arrived(red.at[lax.rem(sec - d + S, S)], s_send.at[d], s_recv.at[d])
    total = red[0]
    for k in range(1, S):
        total = total + red[k]
    sums_ref[...] = total


def finish(lefts, sums_ref, left_hbm, energy_ref, sems):
    stores = []
    for c in range(2):
        copy = pltpu.make_async_copy(lefts.at[c], left_hbm.at[c, 0], sems.at[c])
        copy.start()
        stores.append(copy)
    total = sums_ref[...]
    total = jnp.sum(total, axis=1, keepdims=True)
    values = (float(N * S) * total[0:6]) / total[6:7]
    place = 3 * lax.broadcasted_iota(jnp.int32, (2, 3), 0) + lax.broadcasted_iota(jnp.int32, (2, 3), 1)
    energy = jnp.zeros((2, 3), F32)
    for k in range(6):
        energy = jnp.where(place == k, values[k:k + 1], energy)
    energy_ref[...] = energy
    for copy in stores:
        copy.wait()


def per_device(transfer, hamiltonian, kept):
    dma = pltpu.SemaphoreType.DMA
    vmem = pl.BlockSpec(memory_space=pltpu.VMEM)
    lefts, sums = pl.pallas_call(
        kernel,
        name="chain",
        out_shape=(pltpu.VMEM((2, N, N), F32), pltpu.VMEM((8, 128), F32)),
        in_specs=[
            pl.BlockSpec(memory_space=pl.ANY),
            pl.BlockSpec(memory_space=pl.ANY),
            pl.BlockSpec(memory_space=pltpu.SMEM),
        ],
        out_specs=(vmem, vmem),
        scratch_shapes=[
            pltpu.VMEM((2, N, N), F32),
            pltpu.VMEM((2, TERMS, N, N), F32),
            pltpu.VMEM((Y, N, N), F32),
            pltpu.VMEM((Z, N, N), F32),
            pltpu.VMEM((Z, N, N), F32),
            *[pltpu.VMEM((N, N), F32)] * 4,
            pltpu.VMEM((7, N, N), F32),
            pltpu.VMEM((S, 8, 128), F32),
            dma((3,)),
            dma((2, 5)),
            dma((2, 5)),
            dma((2, 4, len(PARTS))),
            dma((2, 4, len(PARTS))),
            dma((2, 3, len(PARTS))),
            dma((2, 3, 2)),
            dma((2, 2, len(PARTS))),
            dma((2, 2, len(PARTS))),
            dma((S,)),
            dma((S,)),
        ],
        compiler_params=pltpu.CompilerParams(collective_id=0, has_side_effects=True),
    )(transfer, hamiltonian, kept.T)
    return pl.pallas_call(
        finish,
        name="finish",
        out_shape=(
            jax.ShapeDtypeStruct((2, 1, N, N), F32),
            jax.ShapeDtypeStruct((2, TERMS), F32),
        ),
        in_specs=[vmem, vmem],
        out_specs=(pl.BlockSpec(memory_space=pl.ANY), vmem),
        scratch_shapes=[dma((2,))],
    )(*(pltpu.with_memory_space_constraint(x, pltpu.VMEM) for x in (lefts, sums)))


def solution(mesh):
    in_specs = (P("col", "sec", None, None), P("col", None, "sec", None, None), P("col", "sec"))
    out_specs = (P("col", "sec", None, None), P("col", None))
    return jax.shard_map(
        per_device, mesh=mesh, in_specs=in_specs, out_specs=out_specs, check_vma=False
    )
```

```python
import jax
import jax.numpy as jnp
from jax import lax
from jax.experimental import pallas as pl
from jax.experimental.pallas import tpu as pltpu
from jax.sharding import PartitionSpec as P

MESH = pl.DeviceIdType.MESH
F32 = jnp.float32
BF16 = jnp.bfloat16
Y = 4
Z = 8
S = 8
N = 256
HALF = N // 2
QUARTER = N // 4
BASE = 104
CUTS = ((0, BASE), (BASE, N - 2 * BASE), (N - BASE, BASE))
SIZES = ((64,), (64,))
PARTS = [(half, sum(sizes[:k]), sizes[k]) for half, sizes in enumerate(SIZES) for k in range(len(sizes))]
TERMS = 3
NN = (((1,), (0,)), ((), ()))
NT = (((1,), (1,)), ((), ()))
TN = (((0,), (0,)), ((), ()))


def split(x):
    high = x.astype(BF16)
    return high, (x - high.astype(F32)).astype(BF16)


def mm(a, b, dims=NN):
    ah, al = split(a)
    bh, bl = split(b)

    def dot(p, q):
        return lax.dot_general(p, q, dims, preferred_element_type=F32)

    return dot(ah, bh) + (dot(ah, bl) + dot(al, bh))


def kernel(
    t_hbm, h_hbm, kept_ref,
    lout, sums_ref,
    t, h, g, r, away, acc_p, acc_m, post, factor, q, red,
    load_sem, g_send, g_recv, z_send, z_recv, y_send, y_recv, c_send, c_recv, s_send, s_recv,
):
    col = lax.axis_index("col")
    sec = lax.axis_index("sec")
    y = lax.rem(col, Y)
    z = col // Y

    def at_y(d):
        return z * Y + lax.rem(y + d + Y, Y)

    def at_z(d):
        return lax.rem(z + d + Z, Z) * Y + y

    loads = []
    for c in range(2):
        loads.append(pltpu.make_async_copy(t_hbm.at[c, 0], t.at[c], load_sem.at[c]))
    loads.append(pltpu.make_async_copy(h_hbm.at[:, :, 0], h, load_sem.at[2]))
    loads[0].start()
    loads[1].start()

    barrier = pltpu.get_barrier_semaphore()
    other = sec + 1 - 2 * lax.rem(sec, 2)
    partners = [(at_y(1), sec), (at_y(-1), sec), (at_y(1), other), (at_y(-1), other)]
    partners += [(at_z(1), other), (at_z(-1), other)]
    partners += [(col, lax.rem(sec + d, S)) for d in range(1, S)]
    for partner in partners:
        pl.semaphore_signal(barrier, inc=1, device_id=partner, device_id_type=MESH)

    sends = []

    def send(ref, target, send_sem, recv_sem, to=None):
        copy = pltpu.make_async_remote_copy(
            src_ref=ref, dst_ref=ref if to is None else to, send_sem=send_sem, recv_sem=recv_sem,
            device_id=target, device_id_type=MESH,
        )
        copy.start()
        sends.append(copy)

    def arrived(ref, send_sem, recv_sem):
        pltpu.make_async_remote_copy(
            src_ref=ref, dst_ref=ref, send_sem=send_sem, recv_sem=recv_sem,
            device_id=(col, sec), device_id_type=MESH,
        ).wait_recv()

    top = pl.ds(0, HALF)
    bottom = pl.ds(HALF, HALF)
    loads[0].wait()
    loads[1].wait()
    loads[2].start()
    g[y, top] = mm(t[0, top], t[1])
    pl.semaphore_wait(barrier, len(partners))

    y_plus, y_minus = (at_y(1), sec), (at_y(-1), sec)
    z_plus, z_minus = (at_z(1), other), (at_z(-1), other)
    before, after, opposite = lax.rem(y + 3, Y), lax.rem(y + 1, Y), lax.rem(y + 2, Y)

    def g_rows(direction, index):
        start, size = CUTS[index if direction == 0 else 2 - index]
        return pl.ds(start, size)

    def g_copy(direction, index, block):
        target = y_plus if direction == 0 else y_minus
        rows = g_rows(direction, index % 3)
        send(g.at[block, rows], target, g_send.at[direction, index], g_recv.at[direction, index])

    def g_wait(direction, index, block):
        rows = g_rows(direction, index % 3)
        arrived(g.at[block, rows], g_send.at[direction, index], g_recv.at[direction, index])

    g_copy(0, 0, y)
    g[y, bottom] = mm(t[0, bottom], t[1])
    for direction, index in ((1, 0), (0, 1), (1, 1), (0, 2), (1, 2)):
        g_copy(direction, index, y)

    loads[2].wait()
    row = lax.broadcasted_iota(jnp.int32, (N, N), 0)
    column = lax.broadcasted_iota(jnp.int32, (N, N), 1)
    for c in range(2):
        kept = row < kept_ref[0, c]
        for k in range(TERMS):
            h[c, k] = jnp.where(kept, h[c, k], 0.0)
    for k in range(TERMS):

        @pl.when(z < 4)
        def _():
            h[0, k] = mm(h[0, k], t[1])

        @pl.when(z >= 4)
        def _():
            h[1, k] = mm(t[0], h[1, k])

    neighbours = (before, after)
    inside = lax.rem(y, Y - 1) != 0
    for direction in range(2):
        g_wait(direction, 0, neighbours[direction])
        g_copy(direction, 3, neighbours[direction])
    for direction in range(2):
        g_wait(direction, 1, neighbours[direction])

    @pl.when(inside)
    def _():
        for direction in range(2):
            g_copy(direction, 4, neighbours[direction])
            sends.pop()

    for direction in range(2):
        g_wait(direction, 2, neighbours[direction])

    @pl.when(y < 2)
    def _():
        acc_p[...] = mm(g[0], g[1])

    @pl.when(y >= 2)
    def _():
        acc_m[...] = mm(g[2], g[3])

    for direction in range(2):
        g_wait(direction, 3, opposite)

    @pl.when(y < 2)
    def _():
        g_wait(1, 4, opposite)

    @pl.when(y >= 2)
    def _():
        g_wait(0, 4, opposite)

    @pl.when(y < 2)
    def _():
        acc_m[...] = mm(g[2], g[3])

    @pl.when(y >= 2)
    def _():
        acc_p[...] = mm(g[0], g[1])

    r[z] = mm(acc_p[...], acc_m[...])

    flip = (Y - 1 - y) // (Y - 1)

    def rows_at(start, size):
        return pl.ds(pl.multiple_of(lax.rem(y * QUARTER + start, N), 8), size)

    def chunk(direction, part):
        half, offset, size = PARTS[part]
        return rows_at(direction * HALF + lax.rem(half + flip, 2) * QUARTER + offset, size)

    def z_block(direction, step):
        return lax.rem(z - step + Z, Z) if direction == 0 else lax.rem(z + step, Z)

    def z_copy(direction, step, part):
        place = (z_block(direction, step - 1), chunk(direction, part))
        target = z_plus if direction == 0 else z_minus
        here, there = (r, away) if step % 2 else (away, r)
        index = (direction, step - 1, part)
        send(here.at[place], target, z_send.at[index], z_recv.at[index], there.at[place])

    def z_wait(direction, step, part):
        ref = (away if step % 2 else r).at[z_block(direction, step), chunk(direction, part)]
        index = (direction, step - 1, part)
        arrived(ref, z_send.at[index], z_recv.at[index])

    def y_copy(direction, step, part):
        place = (z_block(direction, step), chunk(direction, part))
        owner = other if step % 2 else sec
        quarter = lax.rem(PARTS[part][0] + flip, 2)
        target = (at_y(1 - 2 * quarter), owner)
        here = away if step % 2 else r
        send(here.at[place], target, y_send.at[direction, step - 1, part], y_recv.at[direction, step - 1, quarter], r.at[place])

    def quarter_rows(direction, half):
        return rows_at(direction * HALF + lax.rem(half + flip, 2) * QUARTER, QUARTER)

    def c_copy(direction, step, half):
        place = (z_block(direction, step), quarter_rows(direction, half))
        index = (direction, step // 2, half)
        send(away.at[place], (col, other), c_send.at[index], c_recv.at[index], r.at[place])

    def c_wait(direction, step, half):
        index = (direction, step // 2, half)
        arrived(r.at[z_block(direction, step), quarter_rows(direction, half)], c_send.at[index], c_recv.at[index])

    def y_wait(direction, step, quarter):
        rows = rows_at(direction * HALF + (3 - quarter) * QUARTER, QUARTER)
        index = (direction, step - 1, quarter)
        arrived(r.at[z_block(direction, step), rows], y_send.at[direction, step - 1, 0], y_recv.at[index])

    for part in range(len(PARTS)):
        for direction in range(2):
            z_copy(direction, 1, part)

    @pl.when(y == 0)
    def _():
        acc_m[...] = mm(g[1], acc_m[...])

    @pl.when(y == 1)
    def _():
        acc_p[...] = g[0]

    @pl.when(y == 2)
    def _():
        acc_m[...] = g[3]

    @pl.when(y == 3)
    def _():
        acc_p[...] = mm(acc_p[...], g[2])

    @pl.when(y == 0)
    def _():
        acc_p[...] = (row == column).astype(F32)

    @pl.when(y == 3)
    def _():
        acc_m[...] = (row == column).astype(F32)

    def write_lefts(left0, left1):
        lout[0] = jnp.where(column < kept_ref[0, 0], left0, 0.0)
        lout[1] = jnp.where(column < kept_ref[0, 1], left1, 0.0)

    def take_blocks(step):
        for direction in range(2):
            if step % 2:
                for half in range(2):
                    c_wait(direction, step, half)
            for quarter in range(2):
                y_wait(direction, step, quarter)
        plus = z_block(0, step)
        minus = z_block(1, step)

        @pl.when(step <= z - step // 3)
        def _():
            acc_p[...] = mm(r[plus], acc_p[...])

        @pl.when(step == z + 1)
        def _():
            post[...] = r[plus]

        @pl.when(step > z + 1)
        def _():
            post[...] = mm(r[plus], post[...])

        @pl.when(step <= Z - 1 - z - step // 3)
        def _():
            acc_m[...] = mm(acc_m[...], r[minus])

        @pl.when(step == Z - z)
        def _():
            post[...] = r[minus]

        @pl.when(step > Z - z)
        def _():
            post[...] = mm(post[...], r[minus])

    for step in range(1, 4):
        for part in range(len(PARTS)):
            for direction in range(2):
                z_wait(direction, step, part)
                z_copy(direction, step + 1, part)
                y_copy(direction, step, part)
                if step % 2 and sum(PARTS[part][1:]) == QUARTER:
                    c_copy(direction, step, PARTS[part][0])
        if step > 1:
            take_blocks(step - 1)

    @pl.when(z < 4)
    def _():
        x0 = acc_p[...]
        x1 = mm(x0, t[0])
        x2 = mm(x1, t[1])
        q[6] = x2
        factor[...] = x2
        for k in range(TERMS):
            q[k] = mm(x0, h[0, k])
            q[3 + k] = mm(x1, h[1, k])
        write_lefts(x0, x1)

    @pl.when(z >= 4)
    def _():
        x0 = acc_m[...]
        x1 = mm(t[1], x0)
        x2 = mm(t[0], x1)
        q[6] = x2
        factor[...] = x2
        for k in range(TERMS):
            q[k] = mm(h[0, k], x1)
            q[3 + k] = mm(h[1, k], x0)

    take_blocks(3)

    @pl.when(z == 3)
    def _():
        block = r[0]
        factor[...] = mm(block, mm(block, factor[...]), TN)

    @pl.when(z == 4)
    def _():
        block = r[Z - 1]
        factor[...] = mm(mm(factor[...], block), block, NT)

    for part in range(len(PARTS)):
        for direction in range(2):
            z_wait(direction, 4, part)
    middle = lax.rem(z + 4, Z)

    @pl.when(z < 4)
    def _():
        acc_m[...] = mm(acc_m[...], r[middle])

    @pl.when(z < 3)
    def _():
        acc_m[...] = mm(acc_m[...], post[...])

    @pl.when(z >= 4)
    def _():
        acc_p[...] = mm(r[middle], acc_p[...])

    @pl.when(z > 4)
    def _():
        acc_p[...] = mm(post[...], acc_p[...])

    def lanes(x):
        x = jnp.sum(x, axis=0, keepdims=True)
        return x[:, :128] + x[:, 128:]

    def reduce(v):
        rows = [lanes(v * q[k]) for k in range(7)] + [jnp.zeros((1, 128), F32)]
        red[sec] = jnp.concatenate(rows, axis=0)

    @pl.when(z < 4)
    def _():
        gram = mm(acc_m[...], acc_m[...], NT)
        reduce(mm(factor[...], gram))

    @pl.when(z >= 4)
    def _():
        gram = mm(acc_p[...], acc_p[...], TN)
        reduce(mm(gram, factor[...]))

    for d in (4, 3, 5, 2, 6, 1, 7):
        send(red.at[sec], (col, lax.rem(sec + d, S)), s_send.at[d], s_recv.at[d])

    @pl.when(z == 3)
    def _():
        left0 = mm(r[0], acc_p[...])
        write_lefts(left0, mm(left0, t[0]))

    @pl.when(z >= 4)
    def _():
        write_lefts(acc_p[...], mm(acc_p[...], t[0]))

    for copy in sends:
        copy.wait_send()

    @pl.when(inside)
    def _():
        for direction in range(2):
            ref = g.at[neighbours[direction], g_rows(direction, 1)]
            pltpu.make_async_remote_copy(
                src_ref=ref, dst_ref=ref, send_sem=g_send.at[direction, 4], recv_sem=g_recv.at[direction, 4],
                device_id=y_plus, device_id_type=MESH,
            ).wait_send()

    for d in range(1, S):
        arrived(red.at[lax.rem(sec - d + S, S)], s_send.at[d], s_recv.at[d])
    total = red[0]
    for k in range(1, S):
        total = total + red[k]
    sums_ref[...] = total


def finish(lefts, sums_ref, left_hbm, energy_ref, sems):
    stores = []
    for c in range(2):
        copy = pltpu.make_async_copy(lefts.at[c], left_hbm.at[c, 0], sems.at[c])
        copy.start()
        stores.append(copy)
    total = sums_ref[...]
    total = jnp.sum(total, axis=1, keepdims=True)
    values = (float(N * S) * total[0:6]) / total[6:7]
    place = 3 * lax.broadcasted_iota(jnp.int32, (2, 3), 0) + lax.broadcasted_iota(jnp.int32, (2, 3), 1)
    energy = jnp.zeros((2, 3), F32)
    for k in range(6):
        energy = jnp.where(place == k, values[k:k + 1], energy)
    energy_ref[...] = energy
    for copy in stores:
        copy.wait()


def per_device(transfer, hamiltonian, kept):
    dma = pltpu.SemaphoreType.DMA
    vmem = pl.BlockSpec(memory_space=pltpu.VMEM)
    lefts, sums = pl.pallas_call(
        kernel,
        name="chain",
        out_shape=(pltpu.VMEM((2, N, N), F32), pltpu.VMEM((8, 128), F32)),
        in_specs=[
            pl.BlockSpec(memory_space=pl.ANY),
            pl.BlockSpec(memory_space=pl.ANY),
            pl.BlockSpec(memory_space=pltpu.SMEM),
        ],
        out_specs=(vmem, vmem),
        scratch_shapes=[
            pltpu.VMEM((2, N, N), F32),
            pltpu.VMEM((2, TERMS, N, N), F32),
            pltpu.VMEM((Y, N, N), F32),
            pltpu.VMEM((Z, N, N), F32),
            pltpu.VMEM((Z, N, N), F32),
            *[pltpu.VMEM((N, N), F32)] * 4,
            pltpu.VMEM((7, N, N), F32),
            pltpu.VMEM((S, 8, 128), F32),
            dma((3,)),
            dma((2, 5)),
            dma((2, 5)),
            dma((2, 4, len(PARTS))),
            dma((2, 4, len(PARTS))),
            dma((2, 3, len(PARTS))),
            dma((2, 3, 2)),
            dma((2, 2, len(PARTS))),
            dma((2, 2, len(PARTS))),
            dma((S,)),
            dma((S,)),
        ],
        compiler_params=pltpu.CompilerParams(collective_id=0, has_side_effects=True),
    )(transfer, hamiltonian, kept.T)
    return pl.pallas_call(
        finish,
        name="finish",
        out_shape=(
            jax.ShapeDtypeStruct((2, 1, N, N), F32),
            jax.ShapeDtypeStruct((2, TERMS), F32),
        ),
        in_specs=[vmem, vmem],
        out_specs=(pl.BlockSpec(memory_space=pl.ANY), vmem),
        scratch_shapes=[dma((2,))],
    )(*(pltpu.with_memory_space_constraint(x, pltpu.VMEM) for x in (lefts, sums)))


def solution(mesh):
    in_specs = (P("col", "sec", None, None), P("col", None, "sec", None, None), P("col", "sec"))
    out_specs = (P("col", "sec", None, None), P("col", None))
    return jax.shard_map(
        per_device, mesh=mesh, in_specs=in_specs, out_specs=out_specs, check_vma=False
    )
```

```python
import jax
import jax.numpy as jnp
from jax import lax
from jax.experimental import pallas as pl
from jax.experimental.pallas import tpu as pltpu
from jax.sharding import PartitionSpec as P

MESH = pl.DeviceIdType.MESH
F32 = jnp.float32
BF16 = jnp.bfloat16
Y = 4
Z = 8
S = 8
N = 256
HALF = N // 2
QUARTER = N // 4
BASE = 104
CUTS = ((0, BASE), (BASE, N - 2 * BASE), (N - BASE, BASE))
SIZES = ((40, 24), (40, 24))
PARTS = [(half, sum(sizes[:k]), sizes[k]) for half, sizes in enumerate(SIZES) for k in range(len(sizes))]
TERMS = 3
NN = (((1,), (0,)), ((), ()))
NT = (((1,), (1,)), ((), ()))
TN = (((0,), (0,)), ((), ()))


def split(x):
    high = x.astype(BF16)
    return high, (x - high.astype(F32)).astype(BF16)


def mm(a, b, dims=NN):
    ah, al = split(a)
    bh, bl = split(b)

    def dot(p, q):
        return lax.dot_general(p, q, dims, preferred_element_type=F32)

    return dot(ah, bh) + (dot(ah, bl) + dot(al, bh))


def kernel(
    t_hbm, h_hbm, kept_ref,
    lout, sums_ref,
    t, h, g, r, away, acc_p, acc_m, post, factor, q, red,
    load_sem, g_send, g_recv, z_send, z_recv, y_send, y_recv, c_send, c_recv, s_send, s_recv,
):
    col = lax.axis_index("col")
    sec = lax.axis_index("sec")
    y = lax.rem(col, Y)
    z = col // Y

    def at_y(d):
        return z * Y + lax.rem(y + d + Y, Y)

    def at_z(d):
        return lax.rem(z + d + Z, Z) * Y + y

    loads = []
    for c in range(2):
        loads.append(pltpu.make_async_copy(t_hbm.at[c, 0], t.at[c], load_sem.at[c]))
    loads.append(pltpu.make_async_copy(h_hbm.at[:, :, 0], h, load_sem.at[2]))
    loads[0].start()
    loads[1].start()

    barrier = pltpu.get_barrier_semaphore()
    other = sec + 1 - 2 * lax.rem(sec, 2)
    partners = [(at_y(1), sec), (at_y(-1), sec), (at_y(1), other), (at_y(-1), other)]
    partners += [(at_z(1), other), (at_z(-1), other)]
    partners += [(col, lax.rem(sec + d, S)) for d in range(1, S)]
    for partner in partners:
        pl.semaphore_signal(barrier, inc=1, device_id=partner, device_id_type=MESH)

    sends = []

    def send(ref, target, send_sem, recv_sem, to=None):
        copy = pltpu.make_async_remote_copy(
            src_ref=ref, dst_ref=ref if to is None else to, send_sem=send_sem, recv_sem=recv_sem,
            device_id=target, device_id_type=MESH,
        )
        copy.start()
        sends.append(copy)

    def arrived(ref, send_sem, recv_sem):
        pltpu.make_async_remote_copy(
            src_ref=ref, dst_ref=ref, send_sem=send_sem, recv_sem=recv_sem,
            device_id=(col, sec), device_id_type=MESH,
        ).wait_recv()

    top = pl.ds(0, HALF)
    bottom = pl.ds(HALF, HALF)
    loads[0].wait()
    loads[1].wait()
    loads[2].start()
    g[y, top] = mm(t[0, top], t[1])
    pl.semaphore_wait(barrier, len(partners))

    y_plus, y_minus = (at_y(1), sec), (at_y(-1), sec)
    z_plus, z_minus = (at_z(1), other), (at_z(-1), other)
    before, after, opposite = lax.rem(y + 3, Y), lax.rem(y + 1, Y), lax.rem(y + 2, Y)

    def g_rows(direction, index):
        start, size = CUTS[index if direction == 0 else 2 - index]
        return pl.ds(start, size)

    def g_copy(direction, index, block):
        target = y_plus if direction == 0 else y_minus
        rows = g_rows(direction, index % 3)
        send(g.at[block, rows], target, g_send.at[direction, index], g_recv.at[direction, index])

    def g_wait(direction, index, block):
        rows = g_rows(direction, index % 3)
        arrived(g.at[block, rows], g_send.at[direction, index], g_recv.at[direction, index])

    g_copy(0, 0, y)
    g[y, bottom] = mm(t[0, bottom], t[1])
    for direction, index in ((1, 0), (0, 1), (1, 1), (0, 2), (1, 2)):
        g_copy(direction, index, y)

    loads[2].wait()
    row = lax.broadcasted_iota(jnp.int32, (N, N), 0)
    column = lax.broadcasted_iota(jnp.int32, (N, N), 1)
    for c in range(2):
        kept = row < kept_ref[0, c]
        for k in range(TERMS):
            h[c, k] = jnp.where(kept, h[c, k], 0.0)
    for k in range(TERMS):

        @pl.when(z < 4)
        def _():
            h[0, k] = mm(h[0, k], t[1])

        @pl.when(z >= 4)
        def _():
            h[1, k] = mm(t[0], h[1, k])

    neighbours = (before, after)
    inside = lax.rem(y, Y - 1) != 0
    for direction in range(2):
        g_wait(direction, 0, neighbours[direction])
        g_copy(direction, 3, neighbours[direction])
    for direction in range(2):
        g_wait(direction, 1, neighbours[direction])

    @pl.when(inside)
    def _():
        for direction in range(2):
            g_copy(direction, 4, neighbours[direction])
            sends.pop()

    for direction in range(2):
        g_wait(direction, 2, neighbours[direction])

    @pl.when(y < 2)
    def _():
        acc_p[...] = mm(g[0], g[1])

    @pl.when(y >= 2)
    def _():
        acc_m[...] = mm(g[2], g[3])

    for direction in range(2):
        g_wait(direction, 3, opposite)

    @pl.when(y < 2)
    def _():
        g_wait(1, 4, opposite)

    @pl.when(y >= 2)
    def _():
        g_wait(0, 4, opposite)

    @pl.when(y < 2)
    def _():
        acc_m[...] = mm(g[2], g[3])

    @pl.when(y >= 2)
    def _():
        acc_p[...] = mm(g[0], g[1])

    r[z] = mm(acc_p[...], acc_m[...])

    flip = (Y - 1 - y) // (Y - 1)

    def rows_at(start, size):
        return pl.ds(pl.multiple_of(lax.rem(y * QUARTER + start, N), 8), size)

    def chunk(direction, part):
        half, offset, size = PARTS[part]
        return rows_at(direction * HALF + lax.rem(half + flip, 2) * QUARTER + offset, size)

    def z_block(direction, step):
        return lax.rem(z - step + Z, Z) if direction == 0 else lax.rem(z + step, Z)

    def z_copy(direction, step, part):
        place = (z_block(direction, step - 1), chunk(direction, part))
        target = z_plus if direction == 0 else z_minus
        here, there = (r, away) if step % 2 else (away, r)
        index = (direction, step - 1, part)
        send(here.at[place], target, z_send.at[index], z_recv.at[index], there.at[place])

    def z_wait(direction, step, part):
        ref = (away if step % 2 else r).at[z_block(direction, step), chunk(direction, part)]
        index = (direction, step - 1, part)
        arrived(ref, z_send.at[index], z_recv.at[index])

    def y_copy(direction, step, part):
        place = (z_block(direction, step), chunk(direction, part))
        owner = other if step % 2 else sec
        quarter = lax.rem(PARTS[part][0] + flip, 2)
        target = (at_y(1 - 2 * quarter), owner)
        here = away if step % 2 else r
        send(here.at[place], target, y_send.at[direction, step - 1, part], y_recv.at[direction, step - 1, quarter], r.at[place])

    def quarter_rows(direction, half):
        return rows_at(direction * HALF + lax.rem(half + flip, 2) * QUARTER, QUARTER)

    def c_copy(direction, step, half):
        place = (z_block(direction, step), quarter_rows(direction, half))
        index = (direction, step // 2, half)
        send(away.at[place], (col, other), c_send.at[index], c_recv.at[index], r.at[place])

    def c_wait(direction, step, half):
        index = (direction, step // 2, half)
        arrived(r.at[z_block(direction, step), quarter_rows(direction, half)], c_send.at[index], c_recv.at[index])

    def y_wait(direction, step, quarter):
        rows = rows_at(direction * HALF + (3 - quarter) * QUARTER, QUARTER)
        index = (direction, step - 1, quarter)
        arrived(r.at[z_block(direction, step), rows], y_send.at[direction, step - 1, 0], y_recv.at[index])

    for part in range(len(PARTS)):
        for direction in range(2):
            z_copy(direction, 1, part)

    @pl.when(y == 0)
    def _():
        acc_m[...] = mm(g[1], acc_m[...])

    @pl.when(y == 1)
    def _():
        acc_p[...] = g[0]

    @pl.when(y == 2)
    def _():
        acc_m[...] = g[3]

    @pl.when(y == 3)
    def _():
        acc_p[...] = mm(acc_p[...], g[2])

    @pl.when(y == 0)
    def _():
        acc_p[...] = (row == column).astype(F32)

    @pl.when(y == 3)
    def _():
        acc_m[...] = (row == column).astype(F32)

    def write_lefts(left0, left1):
        lout[0] = jnp.where(column < kept_ref[0, 0], left0, 0.0)
        lout[1] = jnp.where(column < kept_ref[0, 1], left1, 0.0)

    def take_blocks(step):
        for direction in range(2):
            if step % 2:
                for half in range(2):
                    c_wait(direction, step, half)
            for quarter in range(2):
                y_wait(direction, step, quarter)
        plus = z_block(0, step)
        minus = z_block(1, step)

        @pl.when(step <= z - step // 3)
        def _():
            acc_p[...] = mm(r[plus], acc_p[...])

        @pl.when(step == z + 1)
        def _():
            post[...] = r[plus]

        @pl.when(step > z + 1)
        def _():
            post[...] = mm(r[plus], post[...])

        @pl.when(step <= Z - 1 - z - step // 3)
        def _():
            acc_m[...] = mm(acc_m[...], r[minus])

        @pl.when(step == Z - z)
        def _():
            post[...] = r[minus]

        @pl.when(step > Z - z)
        def _():
            post[...] = mm(post[...], r[minus])

    for step in range(1, 4):
        for part in range(len(PARTS)):
            for direction in range(2):
                z_wait(direction, step, part)
                z_copy(direction, step + 1, part)
                y_copy(direction, step, part)
                if step % 2 and sum(PARTS[part][1:]) == QUARTER:
                    c_copy(direction, step, PARTS[part][0])
        if step > 1:
            take_blocks(step - 1)

    @pl.when(z < 4)
    def _():
        x0 = acc_p[...]
        x1 = mm(x0, t[0])
        x2 = mm(x1, t[1])
        q[6] = x2
        factor[...] = x2
        for k in range(TERMS):
            q[k] = mm(x0, h[0, k])
            q[3 + k] = mm(x1, h[1, k])
        write_lefts(x0, x1)

    @pl.when(z >= 4)
    def _():
        x0 = acc_m[...]
        x1 = mm(t[1], x0)
        x2 = mm(t[0], x1)
        q[6] = x2
        factor[...] = x2
        for k in range(TERMS):
            q[k] = mm(h[0, k], x1)
            q[3 + k] = mm(h[1, k], x0)

    take_blocks(3)

    @pl.when(z == 3)
    def _():
        block = r[0]
        factor[...] = mm(block, mm(block, factor[...]), TN)

    @pl.when(z == 4)
    def _():
        block = r[Z - 1]
        factor[...] = mm(mm(factor[...], block), block, NT)

    for part in range(len(PARTS)):
        for direction in range(2):
            z_wait(direction, 4, part)
    middle = lax.rem(z + 4, Z)

    @pl.when(z < 4)
    def _():
        acc_m[...] = mm(acc_m[...], r[middle])

    @pl.when(z < 3)
    def _():
        acc_m[...] = mm(acc_m[...], post[...])

    @pl.when(z >= 4)
    def _():
        acc_p[...] = mm(r[middle], acc_p[...])

    @pl.when(z > 4)
    def _():
        acc_p[...] = mm(post[...], acc_p[...])

    def lanes(x):
        x = jnp.sum(x, axis=0, keepdims=True)
        return x[:, :128] + x[:, 128:]

    def reduce(v):
        rows = [lanes(v * q[k]) for k in range(7)] + [jnp.zeros((1, 128), F32)]
        red[sec] = jnp.concatenate(rows, axis=0)

    @pl.when(z < 4)
    def _():
        gram = mm(acc_m[...], acc_m[...], NT)
        reduce(mm(factor[...], gram))

    @pl.when(z >= 4)
    def _():
        gram = mm(acc_p[...], acc_p[...], TN)
        reduce(mm(gram, factor[...]))

    for d in (4, 3, 5, 2, 6, 1, 7):
        send(red.at[sec], (col, lax.rem(sec + d, S)), s_send.at[d], s_recv.at[d])

    @pl.when(z == 3)
    def _():
        left0 = mm(r[0], acc_p[...])
        write_lefts(left0, mm(left0, t[0]))

    @pl.when(z >= 4)
    def _():
        write_lefts(acc_p[...], mm(acc_p[...], t[0]))

    for copy in sends:
        copy.wait_send()

    @pl.when(inside)
    def _():
        for direction in range(2):
            ref = g.at[neighbours[direction], g_rows(direction, 1)]
            pltpu.make_async_remote_copy(
                src_ref=ref, dst_ref=ref, send_sem=g_send.at[direction, 4], recv_sem=g_recv.at[direction, 4],
                device_id=y_plus, device_id_type=MESH,
            ).wait_send()

    for d in range(1, S):
        arrived(red.at[lax.rem(sec - d + S, S)], s_send.at[d], s_recv.at[d])
    total = red[0]
    for k in range(1, S):
        total = total + red[k]
    sums_ref[...] = total


def finish(lefts, sums_ref, left_hbm, energy_ref, sems):
    stores = []
    for c in range(2):
        copy = pltpu.make_async_copy(lefts.at[c], left_hbm.at[c, 0], sems.at[c])
        copy.start()
        stores.append(copy)
    total = sums_ref[...]
    total = jnp.sum(total, axis=1, keepdims=True)
    values = (float(N * S) * total[0:6]) / total[6:7]
    place = 3 * lax.broadcasted_iota(jnp.int32, (2, 3), 0) + lax.broadcasted_iota(jnp.int32, (2, 3), 1)
    energy = jnp.zeros((2, 3), F32)
    for k in range(6):
        energy = jnp.where(place == k, values[k:k + 1], energy)
    energy_ref[...] = energy
    for copy in stores:
        copy.wait()


def per_device(transfer, hamiltonian, kept):
    dma = pltpu.SemaphoreType.DMA
    vmem = pl.BlockSpec(memory_space=pltpu.VMEM)
    lefts, sums = pl.pallas_call(
        kernel,
        name="chain",
        out_shape=(pltpu.VMEM((2, N, N), F32), pltpu.VMEM((8, 128), F32)),
        in_specs=[
            pl.BlockSpec(memory_space=pl.ANY),
            pl.BlockSpec(memory_space=pl.ANY),
            pl.BlockSpec(memory_space=pltpu.SMEM),
        ],
        out_specs=(vmem, vmem),
        scratch_shapes=[
            pltpu.VMEM((2, N, N), F32),
            pltpu.VMEM((2, TERMS, N, N), F32),
            pltpu.VMEM((Y, N, N), F32),
            pltpu.VMEM((Z, N, N), F32),
            pltpu.VMEM((Z, N, N), F32),
            *[pltpu.VMEM((N, N), F32)] * 4,
            pltpu.VMEM((7, N, N), F32),
            pltpu.VMEM((S, 8, 128), F32),
            dma((3,)),
            dma((2, 5)),
            dma((2, 5)),
            dma((2, 4, len(PARTS))),
            dma((2, 4, len(PARTS))),
            dma((2, 3, len(PARTS))),
            dma((2, 3, 2)),
            dma((2, 2, len(PARTS))),
            dma((2, 2, len(PARTS))),
            dma((S,)),
            dma((S,)),
        ],
        compiler_params=pltpu.CompilerParams(collective_id=0, has_side_effects=True),
    )(transfer, hamiltonian, kept.T)
    return pl.pallas_call(
        finish,
        name="finish",
        out_shape=(
            jax.ShapeDtypeStruct((2, 1, N, N), F32),
            jax.ShapeDtypeStruct((2, TERMS), F32),
        ),
        in_specs=[vmem, vmem],
        out_specs=(pl.BlockSpec(memory_space=pl.ANY), vmem),
        scratch_shapes=[dma((2,))],
    )(*(pltpu.with_memory_space_constraint(x, pltpu.VMEM) for x in (lefts, sums)))


def solution(mesh):
    in_specs = (P("col", "sec", None, None), P("col", None, "sec", None, None), P("col", "sec"))
    out_specs = (P("col", "sec", None, None), P("col", None))
    return jax.shard_map(
        per_device, mesh=mesh, in_specs=in_specs, out_specs=out_specs, check_vma=False
    )
```
